128 devices in a mesh: ca: 8 (over y, core), fe: 16 (over z, x).
Axes of the slice: x: 4, y: 4, z: 4, core: 2. Of those that a mesh axis runs over, the one named last changes fastest.
Arguments:
- grain_ids: int32 [216, 262144], P(None, ('ca', 'fe')), may hold values from 0 to 4095
- euler_angles: float32 [3, 4096], replicated, may hold values from -3.140625 to 3.140625
- brick_active: int32 [262144], P(('ca', 'fe')), may hold values 0 or 1
- brick_owner: int32 [262144, 1], P(('ca', 'fe')), may hold values from 0 to 127, as said below
- brick_element: int32 [262144], P(('ca', 'fe')), may hold values from 0 to 224, as said below
- displacement: float32 [3, 128, 256], P(None, ('ca', 'fe')), may hold values from -0.3 to 0.3
- stress_old: float32 [6, 8, 28800], P(None, None, ('ca', 'fe')), may hold values from -3 to 3
- resistance: float32 [12, 8, 28800], P(None, None, ('ca', 'fe')), may hold values from 0.2 to 0.8
- quad_weights: int32 [8, 28800], P(None, ('ca', 'fe')), may hold values from 32768 to 98304
Outputs:
- stress_new: float32 [6, 8, 28800], P(None, None, ('ca', 'fe'))
- forces: float32 [3, 128, 256], P(None, ('ca', 'fe'))
The draws below stay inside these ranges and needn't reach their ends.
Inputs may be any that keep to these rules, and one draw needn't show every extreme that they name: `brick_owner`: the bricks of one device name each owner at least 2048 / 256 times and at most 40 times; one owner is named exactly 40 times by the bricks of every device. `brick_element`: every element of every owner is named by at least one brick.
All inputs are finite; a program needn't handle non-finite values. No bound on the sum of `brick_active` on one device may be relied on, other than what follows from the above.
Results may differ from the reference program's by a relative error of at most 0.0002.
Values sent between devices are 32-bit elements; how exact they have to be, the bound alone decides.
A program may use at most 448 MiB of HBM per device.

```python
import math
import jax
import jax.numpy as jnp
from jax import lax

CELLS = 216
QP = 8
SLIPS = 12
GX = 15
GZL = 1
BR = 2048
GRAINS = 4096
LAYER_NODES = 256
ELEM_DEV = 225
BRICKS = 262144
ELEMS = 28800
NODE_LAYERS = 128
N_CA = 8
N_FE = 16


def brick_plan(key):
    devices = BRICKS // BR
    half_count = BR // 2
    hot_count = devices // 8
    hot_most = 4 * half_count // devices
    key_hot = jax.random.fold_in(key, 101)
    key_rank = jax.random.fold_in(key, 102)
    key_order = jax.random.fold_in(key, 103)
    key_cover = jax.random.fold_in(key, 104)
    key_tail = jax.random.fold_in(key, 105)
    key_extra = jax.random.fold_in(key, 106)
    common_hot = jax.random.randint(key_hot, (), 0, devices, dtype=jnp.int32)
    ranked = jax.vmap(lambda sub_key: jax.random.permutation(sub_key, devices - 1))(jax.random.split(key_rank, devices)).astype(jnp.int32)
    others = (common_hot + 1 + ranked) % devices
    owner_list = jnp.concatenate([jnp.zeros((devices, 1), jnp.int32) + common_hot, others], axis=1)
    sender = jnp.arange(devices, dtype=jnp.int32)[:, None]
    local_index = jnp.arange(half_count, dtype=jnp.int32)[None, :]
    cover_owner = (sender + local_index) % devices
    skew_index = jnp.arange(half_count, dtype=jnp.int32)
    hot_part = skew_index // hot_most
    cold_part = hot_count + (skew_index - hot_count * hot_most) % (devices - hot_count)
    list_index = jnp.where(skew_index < hot_count * hot_most, hot_part, cold_part).astype(jnp.int32)
    skew_owner = jnp.take(owner_list, list_index, axis=1)
    cover_perm = jax.vmap(lambda sub_key: jax.random.permutation(sub_key, ELEM_DEV))(jax.random.split(key_cover, devices)).astype(jnp.int32)
    cover_tail = jax.random.randint(key_tail, (devices, half_count - ELEM_DEV), 0, ELEM_DEV, dtype=jnp.int32)
    cover_table = jnp.concatenate([cover_perm, cover_tail], axis=1)
    cover_element = jnp.take_along_axis(cover_table.T, cover_owner.T, axis=1).T
    skew_element = jax.random.randint(key_extra, (devices, half_count), 0, ELEM_DEV, dtype=jnp.int32)
    owner_all = jnp.concatenate([cover_owner, skew_owner], axis=1).astype(jnp.int32)
    element_all = jnp.concatenate([cover_element, skew_element], axis=1).astype(jnp.int32)
    local_order = jax.vmap(lambda sub_key: jax.random.permutation(sub_key, BR))(jax.random.split(key_order, devices)).astype(jnp.int32)
    owner_all = jnp.take_along_axis(owner_all, local_order, axis=1).reshape(BRICKS)
    element_all = jnp.take_along_axis(element_all, local_order, axis=1).reshape(BRICKS)
    return (owner_all, element_all)


def draw_brick_owner(key, part):
    owner_all, element_all = brick_plan(key)
    return owner_all.reshape(BRICKS, 1).astype(jnp.int32)


def draw_brick_element(key, part):
    owner_all, element_all = brick_plan(key)
    return element_all.astype(jnp.int32)


def draw_grain_ids(key, part):
    owner_all, element_all = brick_plan(key)
    devices = BRICKS // BR
    per_octant = CELLS // 8
    key_dominant = jax.random.fold_in(key, 111)
    key_second = jax.random.fold_in(key, 112)
    key_third = jax.random.fold_in(key, 113)
    key_speckle = jax.random.fold_in(key, 114)
    key_code = jax.random.fold_in(key, 115)
    key_reach_two = jax.random.fold_in(key, 116)
    key_reach_three = jax.random.fold_in(key, 117)
    dominant = jax.random.randint(key_dominant, (devices * ELEM_DEV,), 0, GRAINS, dtype=jnp.int32)
    first_grain = jnp.take(dominant, owner_all * ELEM_DEV + element_all)
    second_grain = jax.random.randint(key_second, (BRICKS,), 0, GRAINS, dtype=jnp.int32)
    third_grain = jax.random.randint(key_third, (BRICKS,), 0, GRAINS, dtype=jnp.int32)
    speckle_grain = jax.random.randint(key_speckle, (CELLS, BRICKS), 0, GRAINS, dtype=jnp.int32)
    mixed_code = jax.random.randint(key_code, (CELLS, BRICKS), 0, 16 * per_octant, dtype=jnp.int32)
    cell_code = mixed_code % per_octant
    second_reach = jnp.repeat(jax.random.randint(key_reach_two, (8, BRICKS), 0, per_octant // 4 + 1, dtype=jnp.int32), per_octant, axis=0)
    third_reach = jnp.repeat(jax.random.randint(key_reach_three, (8, BRICKS), 0, per_octant // 8 + 1, dtype=jnp.int32), per_octant, axis=0)
    grains = jnp.where(cell_code < second_reach, second_grain[None], jnp.where(cell_code >= per_octant - third_reach, third_grain[None], first_grain[None]))
    return jnp.where(mixed_code < per_octant, speckle_grain, grains).astype(jnp.int32)


def with_ends(drawn, own_key, least, top_value):
    spot = [jax.random.randint(jax.random.fold_in(own_key, axis), (), 0, length) for axis, length in enumerate(drawn.shape)]
    main_axis = drawn.shape.index(max(drawn.shape))
    neighbour = spot[:main_axis] + [(spot[main_axis] + 1) % drawn.shape[main_axis]] + spot[main_axis + 1:]
    return drawn.at[tuple(spot)].set(least).at[tuple(neighbour)].set(top_value)


def level_of(key, shape, cuts, low, largest):
    factor_of, own = 1.0, jax.random.fold_in(key, 6)
    for dim, parts in cuts:
        heights = jnp.exp(jax.random.uniform(jax.random.fold_in(own, dim), (parts,), jnp.float32, low / len(cuts), largest / len(cuts)))
        factor_of = factor_of * jnp.repeat(heights, shape[dim] // parts).reshape([-1 if axis == dim else 1 for axis in range(len(shape))])
    return factor_of


def centred(stream_key, extent, deviation, reach, shards=(), kind=jnp.bfloat16):
    level = level_of(stream_key, extent, shards, -0.22, 0.18) if shards else 1.0
    values = jax.random.normal(stream_key, extent, jnp.float32) * deviation * level
    return jnp.minimum(jnp.maximum(values, -reach), reach).astype(kind)


def setup_inputs(seed: int = 0) -> dict:
    streams_of = jax.random.split(jax.random.key(seed), 10)
    return {
        "grain_ids": draw_grain_ids(jax.random.fold_in(streams_of[9], 71), 0),
        "euler_angles": jnp.clip(jax.random.uniform(streams_of[1], (3, GRAINS), jnp.float32, -3.140625, 3.140625), -3.140625, 3.140625),
        "brick_active": with_ends((jax.random.randint(streams_of[2], (BRICKS,), 0, 8) < 7).astype(jnp.int32), jax.random.fold_in(streams_of[2], 1), 0, 1),
        "brick_owner": draw_brick_owner(jax.random.fold_in(streams_of[9], 71), 0),
        "brick_element": draw_brick_element(jax.random.fold_in(streams_of[9], 71), 0),
        "displacement": centred(streams_of[5], (3, NODE_LAYERS, LAYER_NODES), 0.05, 0.3, ((1, 128),), jnp.float32),
        "stress_old": centred(streams_of[6], (6, QP, ELEMS), 0.5, 3.0, ((2, 128),), jnp.float32),
        "resistance": jnp.clip(jnp.exp(math.log(0.8) - 1.3862944 * jax.random.uniform(streams_of[7], (SLIPS, QP, ELEMS), jnp.float32) ** level_of(streams_of[7], (SLIPS, QP, ELEMS), ((2, 128),), -0.2, 0.2)), 0.2, 0.8),
        "quad_weights": with_ends(jax.random.randint(streams_of[8], (QP, ELEMS), 32768, 98305), jax.random.fold_in(streams_of[8], 1), 32768, 98304).astype(jnp.int32),
    }


SLIP_PLANES = [[value / math.sqrt(3.0) for value in row] for row in [[1, 1, 1]] * 3 + [[-1, 1, 1]] * 3 + [[1, -1, 1]] * 3 + [[1, 1, -1]] * 3]
SLIP_DIRECTIONS = [[value / math.sqrt(2.0) for value in row] for row in [[0, 1, -1], [1, 0, -1], [1, -1, 0], [0, 1, -1], [1, 0, 1], [1, 1, 0], [0, 1, 1], [1, 0, -1], [1, 1, 0], [0, 1, 1], [1, 0, 1], [1, -1, 0]]]
LAMBDA_ELASTIC = 1.5
SHEAR_MODULUS = 1.0
RATE_STEP = 0.1
FIXED_POINT = 65536.0

def shape_gradients():
    grad_table = [[[0.0, 0.0, 0.0] for corner in range(8)] for quadrature in range(8)]
    point_offset = 1.0 / math.sqrt(3.0)
    for quadrature in range(8):
        natural = [(2 * (quadrature >> shift_bits & 1) - 1) * point_offset for shift_bits in (2, 1, 0)]
        for corner in range(8):
            sign_list = [2 * (corner >> shift_bits & 1) - 1 for shift_bits in (2, 1, 0)]
            factors = [1.0 + sign_list[axis_id] * natural[axis_id] for axis_id in range(3)]
            for direction in range(3):
                others = 1.0
                for axis_id in range(3):
                    if axis_id != direction:
                        others = others * factors[axis_id]
                grad_table[quadrature][corner][direction] = 2.0 * sign_list[direction] * others / 8.0
    return grad_table

def rotation_table(euler_angles):
    cos_one, sin_one = (jnp.cos(euler_angles[0]), jnp.sin(euler_angles[0]))
    cos_mid, sin_mid = (jnp.cos(euler_angles[1]), jnp.sin(euler_angles[1]))
    cos_two, sin_two = (jnp.cos(euler_angles[2]), jnp.sin(euler_angles[2]))
    entries_list = [cos_one * cos_two - sin_one * sin_two * cos_mid, -cos_one * sin_two - sin_one * cos_two * cos_mid, sin_one * sin_mid, sin_one * cos_two + cos_one * sin_two * cos_mid, -sin_one * sin_two + cos_one * cos_two * cos_mid, -cos_one * sin_mid, sin_two * sin_mid, cos_two * sin_mid, cos_mid]
    return jnp.stack(entries_list).astype(jnp.float32)

def octant_sums(rotation, grain_ids):
    per_octant = grain_ids.shape[0] // 8
    pieces = []
    for octant in range(8):
        picked = jnp.take(rotation, grain_ids[octant * per_octant:(octant + 1) * per_octant], axis=1)
        pieces.append(lax.optimization_barrier(jnp.sum(picked, axis=1)))
    return jnp.concatenate(pieces, axis=0)

def corner_values(padded, layers):
    corners = []
    for corner in range(8):
        step_x, step_y, step_z = (corner >> 2 & 1, corner >> 1 & 1, corner & 1)
        block_values = padded[:, :, step_z:step_z + layers, step_y:step_y + GX, step_x:step_x + GX]
        corners.append(block_values.reshape(3, -1))
    return jnp.stack(corners, axis=1)

def element_update(padded, layers, orient, stress_old, resistance, quad_weights):
    grad_table = jnp.asarray(shape_gradients(), dtype=jnp.float32)
    corners = corner_values(padded, layers)
    gradients = jnp.einsum('cne,qnd->cdqe', corners, grad_table, precision=lax.Precision.HIGHEST)
    strain = [gradients[0, 0], gradients[1, 1], gradients[2, 2], 0.5 * (gradients[1, 2] + gradients[2, 1]), 0.5 * (gradients[0, 2] + gradients[2, 0]), 0.5 * (gradients[0, 1] + gradients[1, 0])]
    volume = strain[0] + strain[1] + strain[2]
    trial_stress = []
    for component in range(6):
        change = 2.0 * SHEAR_MODULUS * strain[component]
        if component < 3:
            change = change + LAMBDA_ELASTIC * volume
        trial_stress.append(stress_old[component] + change)
    frames = orient.reshape(8, 3, 3, -1)
    correction = [jnp.zeros_like(trial_stress[0]) for component in range(6)]
    for system in range(12):
        rotated_dir = [frames[:, row_index, 0] * float(SLIP_DIRECTIONS[system][0]) + frames[:, row_index, 1] * float(SLIP_DIRECTIONS[system][1]) + frames[:, row_index, 2] * float(SLIP_DIRECTIONS[system][2]) for row_index in range(3)]
        rotated_normal = [frames[:, row_index, 0] * float(SLIP_PLANES[system][0]) + frames[:, row_index, 1] * float(SLIP_PLANES[system][1]) + frames[:, row_index, 2] * float(SLIP_PLANES[system][2]) for row_index in range(3)]
        schmid = [rotated_dir[0] * rotated_normal[0], rotated_dir[1] * rotated_normal[1], rotated_dir[2] * rotated_normal[2], 0.5 * (rotated_dir[1] * rotated_normal[2] + rotated_dir[2] * rotated_normal[1]), 0.5 * (rotated_dir[0] * rotated_normal[2] + rotated_dir[2] * rotated_normal[0]), 0.5 * (rotated_dir[0] * rotated_normal[1] + rotated_dir[1] * rotated_normal[0])]
        resolved = trial_stress[0] * schmid[0] + trial_stress[1] * schmid[1] + trial_stress[2] * schmid[2] + 2.0 * (trial_stress[3] * schmid[3] + trial_stress[4] * schmid[4] + trial_stress[5] * schmid[5])
        slip_ratio = resolved / resistance[system]
        slip_step = RATE_STEP * slip_ratio * jnp.abs(slip_ratio)
        correction = [correction[component] + slip_step * schmid[component] for component in range(6)]
    updated = [trial_stress[component] - 2.0 * SHEAR_MODULUS * correction[component] for component in range(6)]
    stress_new = jnp.stack(updated)
    tensor = jnp.stack([jnp.stack([updated[0], updated[5], updated[4]]), jnp.stack([updated[5], updated[1], updated[3]]), jnp.stack([updated[4], updated[3], updated[2]])])
    point_scale = quad_weights.astype(jnp.float32) * (1.0 / (FIXED_POINT * 8.0))
    element_forces = jnp.einsum('cdqe,qnd->cne', tensor * point_scale, grad_table, precision=lax.Precision.HIGHEST)
    component_count = padded.shape[1]
    nodal = jnp.zeros((3, component_count, layers + 1, GX + 1, GX + 1), jnp.float32)
    for corner in range(8):
        step_x, step_y, step_z = (corner >> 2 & 1, corner >> 1 & 1, corner & 1)
        nodal = nodal.at[:, :, step_z:step_z + layers, step_y:step_y + GX, step_x:step_x + GX].add(element_forces[:, corner].reshape(3, component_count, layers, GX, GX))
    return (stress_new, nodal)

def reference(grain_ids, euler_angles, brick_active, brick_owner, brick_element, displacement, stress_old, resistance, quad_weights):
    rotation = rotation_table(euler_angles)
    active = brick_active.astype(jnp.float32)
    block_count = BRICKS // BR
    blocks = jnp.transpose(grain_ids.reshape(CELLS, block_count, BR), (1, 0, 2))
    brick_sums = lax.map(lambda id_block: octant_sums(rotation, id_block), blocks)
    octant_total = jnp.transpose(brick_sums, (1, 0, 2)).reshape(72, BRICKS) * active[None]
    target = (brick_owner[:, 0] * ELEM_DEV + brick_element).astype(jnp.int32)
    gathered = jnp.zeros((72, ELEMS), jnp.float32).at[:, target].add(octant_total)
    counts = jnp.zeros((ELEMS,), jnp.float32).at[target].add(active)
    orient = gathered / (8.0 * jnp.maximum(counts, 1.0))
    layers = N_FE * GZL
    node_field = displacement.reshape(3, N_CA, layers, GX + 1, GX + 1)
    padded = jnp.pad(node_field, ((0, 0), (0, 0), (0, 1), (0, 0), (0, 0)))
    stress_new, nodal = element_update(padded, layers, orient, stress_old, resistance, quad_weights)
    forces = nodal[:, :, :layers].reshape(3, NODE_LAYERS, LAYER_NODES)
    return (stress_new, forces)
```

```python
import functools
import math

import jax
import jax.numpy as jnp
import numpy as np
from jax import lax
from jax.experimental import pallas as pl
from jax.experimental.pallas import tpu as pltpu
from jax.sharding import PartitionSpec as P

GX = 15
NODES = 256
CAP = 40
DEVICES = 128
ROWS = 24
FIXED_STEPS = float(2**20 - 1)

SLIP_PLANES = [
    [value / math.sqrt(3.0) for value in row]
    for row in [[1, 1, 1]] * 3 + [[-1, 1, 1]] * 3 + [[1, -1, 1]] * 3 + [[1, 1, -1]] * 3
]
SLIP_DIRECTIONS = [
    [value / math.sqrt(2.0) for value in row]
    for row in [
        [0, 1, -1],
        [1, 0, -1],
        [1, -1, 0],
        [0, 1, -1],
        [1, 0, 1],
        [1, 1, 0],
        [0, 1, 1],
        [1, 0, -1],
        [1, 1, 0],
        [0, 1, 1],
        [1, 0, 1],
        [1, -1, 0],
    ]
]
LAMBDA_ELASTIC = 1.5
SHEAR_MODULUS = 1.0
RATE_STEP = 0.1
FIXED_POINT = 65536.0
VMEM_LIMIT = 48 << 20


def shape_gradients():
    grad_table = np.zeros((8, 8, 3))
    point_offset = 1.0 / math.sqrt(3.0)
    for quadrature in range(8):
        natural = [
            (2 * (quadrature >> shift_bits & 1) - 1) * point_offset for shift_bits in (2, 1, 0)
        ]
        for corner in range(8):
            sign_list = [2 * (corner >> shift_bits & 1) - 1 for shift_bits in (2, 1, 0)]
            factors = [1.0 + sign_list[axis_id] * natural[axis_id] for axis_id in range(3)]
            for direction in range(3):
                others = 1.0
                for axis_id in range(3):
                    if axis_id != direction:
                        others = others * factors[axis_id]
                grad_table[quadrature, corner, direction] = (
                    2.0 * sign_list[direction] * others / 8.0
                )
    return grad_table


def gradient_matrices():
    table = shape_gradients()
    grads = np.zeros((72, 24), np.float32)
    forces = np.zeros((24, 72), np.float32)
    for comp in range(3):
        for direction in range(3):
            for q in range(8):
                for corner in range(8):
                    value = table[q, corner, direction]
                    grads[(comp * 3 + direction) * 8 + q, comp * 8 + corner] = value
                    forces[comp * 8 + corner, (comp * 3 + direction) * 8 + q] = value
    return grads, forces


def lane_pick(row, lanes):
    return jnp.take_along_axis(row, lanes, axis=1, mode="promise_in_bounds")


def merge_tree(stack, value, index, bits):
    level = 0
    while index & 1:
        value = jnp.where(bits[level], value, stack.pop())
        level += 1
        index >>= 1
    stack.append(value)


def build_table(euler_ref, table_ref):
    half_sum = 0.5 * (euler_ref[0] + euler_ref[2])
    half_diff = 0.5 * (euler_ref[0] - euler_ref[2])
    half_mid = 0.5 * euler_ref[1]
    cos_mid, sin_mid = jnp.cos(half_mid), jnp.sin(half_mid)
    real = cos_mid * jnp.cos(half_sum)
    flip = jnp.where(real < 0.0, -1.0, 1.0)
    scale = flip * FIXED_STEPS / (1.0 + jnp.abs(real))
    first = jnp.round(sin_mid * jnp.cos(half_diff) * scale).astype(jnp.int32)
    second = jnp.round(sin_mid * jnp.sin(half_diff) * scale).astype(jnp.int32)
    third = jnp.round(cos_mid * jnp.sin(half_sum) * scale).astype(jnp.int32)
    word_a = jnp.left_shift(first, 11) | (jnp.right_shift(third, 10) & 0x7FF)
    word_b = jnp.left_shift(second, 11) | (third & 0x3FF)
    for row in range(32):
        table_ref[row] = jnp.broadcast_to(word_a[row : row + 1], (8, 128))
        table_ref[32 + row] = jnp.broadcast_to(word_b[row : row + 1], (8, 128))


def lookup(table_ref, ids):
    lanes = ids & 127
    bits = [(ids & (128 << level)) != 0 for level in range(5)]
    words = ([], [])
    for row in range(32):
        for n, stack in enumerate(words):
            merge_tree(stack, lane_pick(table_ref[n * 32 + row], lanes), row, bits)
    return words[0][0], words[1][0]


def rotation_terms(word_a, word_b):
    a = jnp.right_shift(word_a, 11).astype(jnp.float32)
    b = jnp.right_shift(word_b, 11).astype(jnp.float32)
    c_bits = jnp.right_shift(jnp.left_shift(word_a, 21), 11) | (word_b & 0x3FF)
    c = c_bits.astype(jnp.float32)
    unit = 1.0 / FIXED_STEPS
    square = (a * a + b * b + c * c) * (unit * unit)
    inverse = 1.0 / (1.0 + square)
    inverse_square = inverse * inverse
    quad = inverse_square * (8.0 * unit * unit)
    lin = inverse_square * ((1.0 - square) * (4.0 * unit))
    qa, qb, qc = quad * a, quad * b, quad * c
    return [qa * a, qb * b, qc * c, qa * b, qa * c, qb * c, lin * a, lin * b, lin * c]


def sum_sublanes(parts, row):
    low4 = row < 4
    level = [
        jnp.where(low4, parts[q], parts[q + 4])
        + pltpu.roll(jnp.where(low4, parts[q + 4], parts[q]), 4, 0)
        for q in range(4)
    ]
    for step in (2, 1):
        keep = (row & step) == 0
        merged = []
        for q in range(step):
            other = jnp.where(keep, level[q + step], level[q])
            moved = jnp.where(keep, pltpu.roll(other, 8 - step, 0), pltpu.roll(other, step, 0))
            merged.append(jnp.where(keep, level[q], level[q + step]) + moved)
        level = merged
    return level[0]


def octant_kernel(ids_ref, euler_ref, out_ref, table_ref, part_ref):
    build_table(euler_ref, table_ref)
    row = lax.broadcasted_iota(jnp.int32, (8, 128), 0)
    tiles = ids_ref.shape[0] // 8
    per_octant = ids_ref.shape[0] // 8

    @pl.loop(0, ids_ref.shape[1] // 128)
    def _(block):
        columns = pl.ds(pl.multiple_of(block * 128, 128), 128)
        sums = None
        octant = 0
        for t in range(tiles):
            terms = rotation_terms(*lookup(table_ref, ids_ref[8 * t : 8 * t + 8, columns]))
            end = (octant + 1) * per_octant
            if 8 * t + 8 < end:
                sums = terms if sums is None else [s + v for s, v in zip(sums, terms)]
                continue
            split = end - 8 * t
            inside = row < split
            head = terms if split == 8 else [jnp.where(inside, v, 0.0) for v in terms]
            done = head if sums is None else [s + v for s, v in zip(sums, head)]
            for n in range(9):
                part_ref[n * 8 + octant] = done[n]
            sums = None if split == 8 else [jnp.where(inside, 0.0, v) for v in terms]
            octant += 1
        xx, yy, zz, xy, xz, yz, wx, wy, wz = [
            sum_sublanes([part_ref[n * 8 + q] for q in range(8)], row) for n in range(9)
        ]
        total = float(per_octant)
        entries = [
            total - (yy + zz),
            xy - wz,
            xz + wy,
            xy + wz,
            total - (xx + zz),
            yz - wx,
            xz - wy,
            yz + wx,
            total - (xx + yy),
        ]
        for n in range(9):
            out_ref[n, :, columns] = entries[n]


def octant_totals(grain_ids, euler_angles):
    bricks = grain_ids.shape[1]
    return pl.pallas_call(
        octant_kernel,
        out_shape=jax.ShapeDtypeStruct((9, 8, bricks), jnp.float32),
        in_specs=[pl.BlockSpec(memory_space=pltpu.VMEM)] * 2,
        out_specs=pl.BlockSpec(memory_space=pltpu.VMEM),
        scratch_shapes=[
            pltpu.VMEM((64, 8, 128), jnp.int32),
            pltpu.VMEM((72, 8, 128), jnp.float32),
        ],
        compiler_params=pltpu.CompilerParams(vmem_limit_bytes=VMEM_LIMIT),
        name="octant_totals",
    )(grain_ids, euler_angles.reshape(3, 32, 128))


NT_DIMS = (((1,), (1,)), ((), ()))


def slot_kernel(total_ref, owner_ref, element_ref, active_ref, out_ref, pick_ref, slot_ref):
    span = 256
    device = lax.broadcasted_iota(jnp.int32, (DEVICES, span), 0)
    slot = lax.broadcasted_iota(jnp.int32, (CAP, span), 0)
    brick = lax.broadcasted_iota(jnp.int32, (1, span), 1)
    before = (
        lax.broadcasted_iota(jnp.int32, (span, span), 0)
        < lax.broadcasted_iota(jnp.int32, (span, span), 1)
    ).astype(jnp.bfloat16)
    ones = jnp.ones((span, span), jnp.bfloat16)
    carry = jnp.zeros((DEVICES, span), jnp.float32)
    found = jnp.zeros((3 * CAP, DEVICES), jnp.float32)
    for start in range(0, total_ref.shape[2], span):
        owned = device == owner_ref[:, start : start + span]
        owned_half = owned.astype(jnp.bfloat16)
        earlier = carry + jnp.dot(owned_half, before, preferred_element_type=jnp.float32)
        carry = carry + jnp.dot(owned_half, ones, preferred_element_type=jnp.float32)
        rank = jnp.sum(jnp.where(owned, earlier, 0.0), axis=0, keepdims=True)
        mine = slot == rank.astype(jnp.int32)
        label = jnp.where(
            active_ref[:, start : start + span] > 0, element_ref[:, start : start + span] + 1, 0
        )
        values = [(brick + start) >> 7, (brick + start) & 127, label]
        left = jnp.concatenate(
            [jnp.where(mine, value.astype(jnp.float32), 0.0) for value in values], axis=0
        ).astype(jnp.bfloat16)
        found = found + lax.dot_general(
            left, owned_half, NT_DIMS, preferred_element_type=jnp.float32
        )
    pick_ref[...] = found[: 2 * CAP].astype(jnp.int32)
    words = 72 * CAP
    slot_ref[words : words + CAP] = found[2 * CAP :]
    slot_ref[words + CAP :] = jnp.zeros((slot_ref.shape[0] - words - CAP, 128), jnp.float32)
    blocks = total_ref.shape[2] // 128
    depth = blocks.bit_length() - 1
    tiles = CAP // 8

    @pl.loop(0, 9)
    def _(entry):
        for t in range(tiles):
            lanes = pick_ref[CAP + 8 * t : CAP + 8 * t + 8]
            high = pick_ref[8 * t : 8 * t + 8]
            bits = [(high & (1 << level)) != 0 for level in range(depth)]
            for q in range(8):
                stack = []
                for block in range(blocks):
                    values = jnp.broadcast_to(
                        total_ref[entry, q : q + 1, block * 128 : block * 128 + 128], (8, 128)
                    )
                    merge_tree(stack, lane_pick(values, lanes), block, bits)
                row = pl.multiple_of((entry * 8 + q) * CAP + 8 * t, 8)
                slot_ref[pl.ds(row, 8), :] = stack[0]

    for c in range(ROWS):
        if c < slot_ref.shape[0] // 128:
            flipped = slot_ref[c * 128 : c * 128 + 128].T
        else:
            flipped = jnp.zeros((128, 128), jnp.float32)
        out_ref[pl.ds(c, DEVICES, stride=ROWS), :] = flipped


def slots_to_send(totals, owner, element, active):
    bricks = totals.shape[2]
    return pl.pallas_call(
        slot_kernel,
        out_shape=jax.ShapeDtypeStruct((DEVICES * ROWS, 128), jnp.float32),
        in_specs=[pl.BlockSpec(memory_space=pltpu.VMEM)] * 4,
        out_specs=pl.BlockSpec(memory_space=pltpu.VMEM),
        scratch_shapes=[
            pltpu.VMEM((2 * CAP, 128), jnp.int32),
            pltpu.VMEM(((ROWS - 1) * 128, 128), jnp.float32),
        ],
        compiler_params=pltpu.CompilerParams(vmem_limit_bytes=VMEM_LIMIT),
        name="slots_to_send",
    )(totals, owner.reshape(1, bricks), element.reshape(1, bricks), active.reshape(1, bricks))


def split_three(values):
    high = values.astype(jnp.bfloat16)
    rest = values - high.astype(jnp.float32)
    mid = rest.astype(jnp.bfloat16)
    low = (rest - mid.astype(jnp.float32)).astype(jnp.bfloat16)
    return jnp.concatenate([high, mid, low], axis=0)


def joined_three(product):
    rows = product.shape[0] // 3
    return product[:rows] + product[rows : 2 * rows] + product[2 * rows :]


def element_kernel(
    got_ref,
    below_ref,
    above_ref,
    stress_ref,
    resistance_ref,
    weights_ref,
    grads_ref,
    gather_ref,
    stress_out,
    owned_out,
    top_out,
    slot_ref,
):
    elements = stress_ref.shape[2]
    for c in range(ROWS - 1):
        slot_ref[c * 128 : c * 128 + 128] = got_ref[pl.ds(c, DEVICES, stride=ROWS), :].T
    sums = jnp.zeros((160, NODES), jnp.float32)
    label_value = lax.broadcasted_iota(jnp.int32, (NODES, 128), 0).astype(jnp.float32) + 1.0
    ones = jnp.ones((16, 128), jnp.bfloat16)
    for r in range(0, CAP, 2):
        left, right = [], []
        for n in (r, r + 1):
            values = slot_ref[pl.ds(n, 72, stride=CAP), :]
            high = values.astype(jnp.bfloat16).astype(jnp.float32)
            left.append(
                jnp.concatenate(
                    [jnp.concatenate([high, values - high], axis=0).astype(jnp.bfloat16), ones],
                    axis=0,
                )
            )
            hit = label_value == slot_ref[72 * CAP + n : 72 * CAP + n + 1]
            right.append(hit.astype(jnp.bfloat16))
        sums = sums + lax.dot_general(
            jnp.concatenate(left, axis=1),
            jnp.concatenate(right, axis=1),
            NT_DIMS,
            preferred_element_type=jnp.float32,
        )
    counts = sums[144:145]
    orient = (sums[:72] + sums[72:144]) / (8.0 * jnp.maximum(counts, 1.0))

    node = lax.broadcasted_iota(jnp.int32, (NODES, NODES), 0)
    lane = lax.broadcasted_iota(jnp.int32, (NODES, NODES), 1)
    base = lane
    for bound in range(GX, GX * GX, GX):
        base = base + jnp.where(lane >= bound, 1, 0)
    to_element = ((node == base) & (lane < elements)).astype(jnp.bfloat16)
    rows = []
    for comp in range(3):
        for corner in range(8):
            step_x, step_y, step_z = (corner >> 2 & 1, corner >> 1 & 1, corner & 1)
            source = above_ref if step_z else below_ref
            offset = step_y * (GX + 1) + step_x
            line = source[comp : comp + 1, :]
            rows.append(line if offset == 0 else pltpu.roll(line, NODES - offset, 1))
    corners = joined_three(
        jnp.dot(
            split_three(jnp.concatenate(rows, axis=0)),
            to_element,
            preferred_element_type=jnp.float32,
        )
    )
    gradients = jnp.dot(
        grads_ref[...],
        corners,
        precision=lax.Precision.HIGHEST,
        preferred_element_type=jnp.float32,
    )

    def grad(comp, direction):
        n = (comp * 3 + direction) * 8
        return gradients[n : n + 8, :elements]

    strain = [
        grad(0, 0),
        grad(1, 1),
        grad(2, 2),
        0.5 * (grad(1, 2) + grad(2, 1)),
        0.5 * (grad(0, 2) + grad(2, 0)),
        0.5 * (grad(0, 1) + grad(1, 0)),
    ]
    volume = strain[0] + strain[1] + strain[2]
    trial = []
    for component in range(6):
        change = 2.0 * SHEAR_MODULUS * strain[component]
        if component < 3:
            change = change + LAMBDA_ELASTIC * volume
        trial.append(stress_ref[component] + change)

    def frame(i, j):
        n = (i * 3 + j) * 8
        return orient[n : n + 8, :elements]

    def rotated(vector):
        out = []
        for i in range(3):
            terms = [float(vector[j]) * frame(i, j) for j in range(3) if vector[j] != 0.0]
            out.append(functools.reduce(lambda x, y: x + y, terms))
        return out

    normals = {tuple(vector): rotated(vector) for vector in SLIP_PLANES}
    correction = [jnp.zeros_like(trial[0]) for component in range(6)]
    for system in range(12):
        d = rotated(SLIP_DIRECTIONS[system])
        m = normals[tuple(SLIP_PLANES[system])]
        schmid = [
            d[0] * m[0],
            d[1] * m[1],
            d[2] * m[2],
            0.5 * (d[1] * m[2] + d[2] * m[1]),
            0.5 * (d[0] * m[2] + d[2] * m[0]),
            0.5 * (d[0] * m[1] + d[1] * m[0]),
        ]
        resolved = (
            trial[0] * schmid[0]
            + trial[1] * schmid[1]
            + trial[2] * schmid[2]
            + 2.0 * (trial[3] * schmid[3] + trial[4] * schmid[4] + trial[5] * schmid[5])
        )
        ratio = resolved / resistance_ref[system]
        slip_step = RATE_STEP * ratio * jnp.abs(ratio)
        correction = [
            correction[component] + slip_step * schmid[component] for component in range(6)
        ]
    updated = [
        trial[component] - 2.0 * SHEAR_MODULUS * correction[component] for component in range(6)
    ]
    for component in range(6):
        stress_out[component] = updated[component]
    scale = weights_ref[...].astype(jnp.float32) * (1.0 / (FIXED_POINT * 8.0))
    order = [0, 5, 4, 5, 1, 3, 4, 3, 2]
    pad = jnp.zeros((8, NODES - elements), jnp.float32)
    tensor = jnp.concatenate(
        [jnp.concatenate([updated[component] * scale, pad], axis=1) for component in order], axis=0
    )
    element_forces = jnp.dot(
        gather_ref[...],
        tensor,
        precision=lax.Precision.HIGHEST,
        preferred_element_type=jnp.float32,
    )
    placed = joined_three(
        lax.dot_general(
            split_three(element_forces), to_element, NT_DIMS, preferred_element_type=jnp.float32
        )
    )
    for out, step_z in ((owned_out, 0), (top_out, 1)):
        for comp in range(3):
            line = jnp.zeros((1, NODES), jnp.float32)
            for corner in range(8):
                if (corner & 1) != step_z:
                    continue
                offset = (corner >> 1 & 1) * (GX + 1) + (corner >> 2 & 1)
                part = placed[comp * 8 + corner : comp * 8 + corner + 1]
                line = line + (part if offset == 0 else pltpu.roll(part, offset, 1))
            out[comp : comp + 1, :] = line


def element_update(got, below, above, stress_old, resistance, quad_weights):
    grads, forces = gradient_matrices()
    layer = jax.ShapeDtypeStruct((3, NODES), jnp.float32)
    return pl.pallas_call(
        element_kernel,
        out_shape=(jax.ShapeDtypeStruct(stress_old.shape, jnp.float32), layer, layer),
        in_specs=[pl.BlockSpec(memory_space=pltpu.VMEM)] * 8,
        out_specs=(pl.BlockSpec(memory_space=pltpu.VMEM),) * 3,
        scratch_shapes=[pltpu.VMEM(((ROWS - 1) * 128, 128), jnp.float32)],
        compiler_params=pltpu.CompilerParams(vmem_limit_bytes=VMEM_LIMIT),
        name="element_update",
    )(
        got,
        below,
        above,
        stress_old,
        resistance,
        quad_weights,
        jnp.asarray(grads),
        jnp.asarray(forces),
    )


def passed_along(block, axis, distance):
    devices = range(lax.axis_size(axis))
    route = [(i - distance, i) for i in devices if i - distance in devices]
    return lax.ppermute(block, axis, route)


def body(
    grain_ids,
    euler_angles,
    brick_active,
    brick_owner,
    brick_element,
    displacement,
    stress_old,
    resistance,
    quad_weights,
):
    below = displacement[:, 0]
    above = passed_along(below, "fe", -1)
    totals = octant_totals(grain_ids, euler_angles)
    send = slots_to_send(totals, brick_owner, brick_element, brick_active)
    got = lax.all_to_all(
        send.reshape(DEVICES, ROWS, 128), ("ca", "fe"), split_axis=0, concat_axis=0, tiled=True
    )
    stress_new, owned, top = element_update(
        got.reshape(DEVICES * ROWS, 128), below, above, stress_old, resistance, quad_weights
    )
    forces = owned + passed_along(top, "fe", 1)
    return (stress_new, forces[:, None])


def solution(mesh):
    placed = (
        P(None, ("ca", "fe")),
        P(),
        P(("ca", "fe")),
        P(("ca", "fe"), None),
        P(("ca", "fe")),
        P(None, ("ca", "fe"), None),
        P(None, None, ("ca", "fe")),
        P(None, None, ("ca", "fe")),
        P(None, ("ca", "fe")),
    )
    return jax.shard_map(
        body,
        mesh=mesh,
        in_specs=placed,
        out_specs=(P(None, None, ("ca", "fe")), P(None, ("ca", "fe"), None)),
        check_vma=False,
    )
```

```python
import functools
import math

import jax
import jax.numpy as jnp
import numpy as np
from jax import lax
from jax.experimental import pallas as pl
from jax.experimental.pallas import tpu as pltpu
from jax.sharding import PartitionSpec as P

GX = 15
NODES = 256
CAP = 40
GROUPS = 8
MEMBERS = 16
DEVICES = GROUPS * MEMBERS
CHUNKS = 4
CHUNK_ROWS = 6
FIXED_STEPS = float(2**20 - 1)

SLIP_PLANES = [
    [value / math.sqrt(3.0) for value in row]
    for row in [[1, 1, 1]] * 3 + [[-1, 1, 1]] * 3 + [[1, -1, 1]] * 3 + [[1, 1, -1]] * 3
]
SLIP_DIRECTIONS = [
    [value / math.sqrt(2.0) for value in row]
    for row in [
        [0, 1, -1],
        [1, 0, -1],
        [1, -1, 0],
        [0, 1, -1],
        [1, 0, 1],
        [1, 1, 0],
        [0, 1, 1],
        [1, 0, -1],
        [1, 1, 0],
        [0, 1, 1],
        [1, 0, 1],
        [1, -1, 0],
    ]
]
LAMBDA_ELASTIC = 1.5
SHEAR_MODULUS = 1.0
RATE_STEP = 0.1
FIXED_POINT = 65536.0
VMEM_LIMIT = 48 << 20


def shape_gradients():
    grad_table = np.zeros((8, 8, 3))
    point_offset = 1.0 / math.sqrt(3.0)
    for quadrature in range(8):
        natural = [
            (2 * (quadrature >> shift_bits & 1) - 1) * point_offset for shift_bits in (2, 1, 0)
        ]
        for corner in range(8):
            sign_list = [2 * (corner >> shift_bits & 1) - 1 for shift_bits in (2, 1, 0)]
            factors = [1.0 + sign_list[axis_id] * natural[axis_id] for axis_id in range(3)]
            for direction in range(3):
                others = 1.0
                for axis_id in range(3):
                    if axis_id != direction:
                        others = others * factors[axis_id]
                grad_table[quadrature, corner, direction] = (
                    2.0 * sign_list[direction] * others / 8.0
                )
    return grad_table


def gradient_matrices():
    table = shape_gradients()
    grads = np.zeros((72, 24), np.float32)
    forces = np.zeros((24, 72), np.float32)
    for comp in range(3):
        for direction in range(3):
            for q in range(8):
                for corner in range(8):
                    value = table[q, corner, direction]
                    grads[(comp * 3 + direction) * 8 + q, comp * 8 + corner] = value
                    forces[comp * 8 + corner, (comp * 3 + direction) * 8 + q] = value
    return grads, forces


def lane_pick(row, lanes):
    return jnp.take_along_axis(row, lanes, axis=1, mode="promise_in_bounds")


def merge_tree(stack, value, index, bits):
    level = 0
    while index & 1:
        value = jnp.where(bits[level], value, stack.pop())
        level += 1
        index >>= 1
    stack.append(value)


def build_table(euler_ref, angle_ref, table_ref):
    for angle in range(3):
        for row in range(32):
            angle_ref[angle, row : row + 1] = euler_ref[
                angle : angle + 1, row * 128 : row * 128 + 128
            ]
    half_sum = 0.5 * (angle_ref[0] + angle_ref[2])
    half_diff = 0.5 * (angle_ref[0] - angle_ref[2])
    half_mid = 0.5 * angle_ref[1]
    cos_mid, sin_mid = jnp.cos(half_mid), jnp.sin(half_mid)
    real = cos_mid * jnp.cos(half_sum)
    flip = jnp.where(real < 0.0, -1.0, 1.0)
    scale = flip * FIXED_STEPS / (1.0 + jnp.abs(real))
    first = jnp.round(sin_mid * jnp.cos(half_diff) * scale).astype(jnp.int32)
    second = jnp.round(sin_mid * jnp.sin(half_diff) * scale).astype(jnp.int32)
    third = jnp.round(cos_mid * jnp.sin(half_sum) * scale).astype(jnp.int32)
    word_a = jnp.left_shift(first, 11) | (jnp.right_shift(third, 10) & 0x7FF)
    word_b = jnp.left_shift(second, 11) | (third & 0x3FF)
    for row in range(32):
        table_ref[row] = jnp.broadcast_to(word_a[row : row + 1], (8, 128))
        table_ref[32 + row] = jnp.broadcast_to(word_b[row : row + 1], (8, 128))


def lookup(table_ref, ids):
    lanes = ids & 127
    bits = [(ids & (128 << level)) != 0 for level in range(5)]
    words = ([], [])
    for row in range(32):
        for n, stack in enumerate(words):
            merge_tree(stack, lane_pick(table_ref[n * 32 + row], lanes), row, bits)
    return words[0][0], words[1][0]


def rotation_terms(word_a, word_b):
    a = jnp.right_shift(word_a, 11).astype(jnp.float32)
    b = jnp.right_shift(word_b, 11).astype(jnp.float32)
    c_bits = jnp.right_shift(jnp.left_shift(word_a, 21), 11) | (word_b & 0x3FF)
    c = c_bits.astype(jnp.float32)
    unit = 1.0 / FIXED_STEPS
    square = (a * a + b * b + c * c) * (unit * unit)
    inverse = 1.0 / (1.0 + square)
    inverse_square = inverse * inverse
    quad = inverse_square * (8.0 * unit * unit)
    lin = inverse_square * ((1.0 - square) * (4.0 * unit))
    qa, qb, qc = quad * a, quad * b, quad * c
    return [qa * a, qb * b, qc * c, qa * b, qa * c, qb * c, lin * a, lin * b, lin * c]


def octant_entries(terms, per_octant):
    xx, yy, zz, xy, xz, yz, wx, wy, wz = terms
    share = per_octant / 8.0
    return [
        share - (yy + zz),
        xy - wz,
        xz + wy,
        xy + wz,
        share - (xx + zz),
        yz - wx,
        xz - wy,
        yz + wx,
        share - (xx + yy),
    ]


def swapped(values, step, keep):
    return jnp.where(keep, pltpu.roll(values, 8 - step, 0), pltpu.roll(values, step, 0))


def sum_sublanes(parts, row):
    half = len(parts) // 2
    low4 = row < 4
    level = [
        jnp.where(low4, parts[n], parts[n + half])
        + pltpu.roll(jnp.where(low4, parts[n + half], parts[n]), 4, 0)
        for n in range(half)
    ]
    for step in (2, 1):
        keep = (row & step) == 0
        if len(level) == 1:
            level = [level[0] + swapped(level[0], step, keep)]
            continue
        half = len(level) // 2
        level = [
            jnp.where(keep, level[n], level[n + half])
            + swapped(jnp.where(keep, level[n + half], level[n]), step, keep)
            for n in range(half)
        ]
    return level[0]


NT_DIMS = (((1,), (1,)), ((), ()))
MESH = pl.DeviceIdType.MESH


def find_slots(owner_ref, element_ref, active_ref):
    span = 256
    device = lax.broadcasted_iota(jnp.int32, (DEVICES, span), 0)
    slot = lax.broadcasted_iota(jnp.int32, (CAP, span), 0)
    brick = lax.broadcasted_iota(jnp.int32, (1, span), 1)
    before = (
        lax.broadcasted_iota(jnp.int32, (span, span), 0)
        < lax.broadcasted_iota(jnp.int32, (span, span), 1)
    ).astype(jnp.bfloat16)
    ones = jnp.ones((span, span), jnp.bfloat16)
    carry = jnp.zeros((DEVICES, span), jnp.float32)
    found = jnp.zeros((3 * CAP, DEVICES), jnp.float32)
    for start in range(0, owner_ref.shape[1], span):
        owner = owner_ref[:, start : start + span]
        owned = device == ((owner & (MEMBERS - 1)) * GROUPS + jnp.right_shift(owner, 4))
        owned_half = owned.astype(jnp.bfloat16)
        earlier = carry + jnp.dot(owned_half, before, preferred_element_type=jnp.float32)
        carry = carry + jnp.dot(owned_half, ones, preferred_element_type=jnp.float32)
        rank = jnp.sum(jnp.where(owned, earlier, 0.0), axis=0, keepdims=True)
        mine = slot == rank.astype(jnp.int32)
        label = jnp.where(
            active_ref[:, start : start + span] > 0, element_ref[:, start : start + span] + 1, 0
        )
        values = [jnp.right_shift(brick + start, 7), (brick + start) & 127, label]
        left = jnp.concatenate(
            [jnp.where(mine, value.astype(jnp.float32), 0.0) for value in values], axis=0
        ).astype(jnp.bfloat16)
        found = found + lax.dot_general(
            left, owned_half, NT_DIMS, preferred_element_type=jnp.float32
        )
    return found


def exchange_kernel(
    ids_hbm,
    euler_ref,
    owner_ref,
    element_ref,
    active_ref,
    below_ref,
    sums_ref,
    above_ref,
    ids_ref,
    angle_ref,
    table_ref,
    carry_ref,
    total_ref,
    pick_ref,
    slot_ref,
    out1_ref,
    in1_ref,
    out2_ref,
    in2_ref,
    got_ref,
    land_ref,
    ids_sem,
    send1_sem,
    recv1_sem,
    send2_sem,
    recv2_sem,
    layer_sem,
):
    ca, fe = lax.axis_index("ca"), lax.axis_index("fe")
    barrier = pltpu.get_barrier_semaphore()

    def member(i):
        return lax.rem(fe + i, MEMBERS)

    def group(i):
        return lax.rem(ca + i, GROUPS)

    @pl.loop(1, MEMBERS)
    def _(i):
        pl.semaphore_signal(barrier, inc=1, device_id=(ca, member(i)), device_id_type=MESH)

    @pl.loop(1, GROUPS)
    def _(i):
        pl.semaphore_signal(barrier, inc=1, device_id=(group(i), fe), device_id_type=MESH)

    row = lax.broadcasted_iota(jnp.int32, (8, 128), 0)
    cells = ids_hbm.shape[0]
    per_octant = cells // 8
    tiles = cells // 8
    step_tiles = 7
    blocks = ids_hbm.shape[1] // 128

    def ids_copy(p):
        rows = pl.ds(p * 8 * step_tiles, min(8 * step_tiles, cells - p * 8 * step_tiles))
        return pltpu.make_async_copy(ids_hbm.at[rows], ids_ref.at[rows], ids_sem.at[p])

    for p in range(CHUNKS):
        ids_copy(p).start()

    def hop1(p, i):
        there = pl.ds(pl.multiple_of(member(i) * GROUPS, 8), GROUPS)
        here = pl.ds(pl.multiple_of(fe * GROUPS, 8), GROUPS)
        return pltpu.make_async_remote_copy(
            src_ref=out1_ref.at[p, :, there],
            dst_ref=in1_ref.at[p, :, here],
            send_sem=send1_sem.at[p, i],
            recv_sem=recv1_sem.at[p, i],
            device_id=(ca, member(i)),
            device_id_type=MESH,
        )

    def hop2(p, i):
        there = pl.ds(pl.multiple_of(group(i) * MEMBERS, 8), MEMBERS)
        here = pl.ds(pl.multiple_of(ca * MEMBERS, 8), MEMBERS)
        return pltpu.make_async_remote_copy(
            src_ref=out2_ref.at[p, :, there],
            dst_ref=in2_ref.at[p, :, here],
            send_sem=send2_sem.at[p, i],
            recv_sem=recv2_sem.at[p, i],
            device_id=(group(i), fe),
            device_id_type=MESH,
        )

    def layer_copy():
        return pltpu.make_async_remote_copy(
            src_ref=below_ref,
            dst_ref=land_ref,
            send_sem=layer_sem.at[0],
            recv_sem=layer_sem.at[1],
            device_id=(ca, lax.rem(fe + MEMBERS - 1, MEMBERS)),
            device_id_type=MESH,
        )

    def start1(p):
        @pl.loop(1, MEMBERS)
        def _(i):
            hop1(p, i).start()

        here = pl.ds(pl.multiple_of(fe * GROUPS, 8), GROUPS)
        in1_ref[p, :, here] = out1_ref[p, :, here]

    def pass_on(p):
        @pl.loop(1, MEMBERS)
        def _(i):
            hop1(p, i).wait_recv()

        for c in range(CHUNK_ROWS):
            for g in range(GROUPS):
                out2_ref[p, c, g * MEMBERS : g * MEMBERS + MEMBERS] = in1_ref[
                    p, c, pl.ds(g, MEMBERS, stride=GROUPS), :
                ]

        @pl.loop(1, GROUPS)
        def _(i):
            hop2(p, i).start()

        here = pl.ds(pl.multiple_of(ca * MEMBERS, 8), MEMBERS)
        in2_ref[p, :, here] = out2_ref[p, :, here]

    def take_in(p):
        @pl.loop(1, GROUPS)
        def _(i):
            hop2(p, i).wait_recv()

        for c in range(CHUNK_ROWS):
            got_ref[p, c * 128 : c * 128 + 128] = in2_ref[p, c].T

    build_table(euler_ref, angle_ref, table_ref)
    found = find_slots(owner_ref, element_ref, active_ref)
    pick_ref[...] = found[: 2 * CAP].astype(jnp.int32)
    got_ref[:, CHUNK_ROWS * 128 :] = jnp.zeros(
        (CHUNKS, got_ref.shape[1] - CHUNK_ROWS * 128, 128), jnp.float32
    )
    depth = blocks.bit_length() - 1

    for p in range(CHUNKS):
        ids_copy(p).wait()

        @pl.loop(0, blocks)
        def _(block, p=p):
            columns = pl.ds(pl.multiple_of(block * 128, 128), 128)
            octant = 2 * p
            sums = None if p == 0 else [carry_ref[block, n] for n in range(9)]
            entries = []
            for t in range(step_tiles * p, min(step_tiles * p + step_tiles, tiles)):
                terms = rotation_terms(*lookup(table_ref, ids_ref[8 * t : 8 * t + 8, columns]))
                end = (octant + 1) * per_octant
                if 8 * t + 8 < end:
                    sums = terms if sums is None else [s + v for s, v in zip(sums, terms)]
                    continue
                split = end - 8 * t
                inside = row < split
                head = terms if split == 8 else [jnp.where(inside, v, 0.0) for v in terms]
                done = head if sums is None else [s + v for s, v in zip(sums, head)]
                entries.append(octant_entries(done, per_octant))
                sums = None if split == 8 else [jnp.where(inside, 0.0, v) for v in terms]
                octant += 1
            if sums is not None:
                for n in range(9):
                    carry_ref[block, n] = sums[n]
            parts = [entries[n & 1][n >> 1] for n in range(18)]
            for n in range(3):
                total_ref[n, :, columns] = sum_sublanes(parts[8 * n : 8 * n + 8], row)

        @pl.loop(0, CAP // 8)
        def _(t):
            lanes = pick_ref[pl.ds(pl.multiple_of(CAP + 8 * t, 8), 8)]
            high = pick_ref[pl.ds(pl.multiple_of(8 * t, 8), 8)]
            bits = [(high & (1 << level)) != 0 for level in range(depth)]
            for m in range(18):
                line = m % 8 if m < 16 else 4 * (m - 16)
                stack = []
                for block in range(blocks):
                    values = jnp.broadcast_to(
                        total_ref[m // 8, line : line + 1, block * 128 : block * 128 + 128],
                        (8, 128),
                    )
                    merge_tree(stack, lane_pick(values, lanes), block, bits)
                slot_ref[pl.ds(pl.multiple_of(m * CAP + 8 * t, 8), 8), :] = stack[0]

        if p == 0:
            slot_ref[18 * CAP : 19 * CAP] = found[2 * CAP :]
            slot_ref[19 * CAP :] = jnp.zeros((slot_ref.shape[0] - 19 * CAP, 128), jnp.float32)
        for c in range(CHUNK_ROWS):
            out1_ref[p, c] = slot_ref[c * 128 : c * 128 + 128].T
        if p == 0:
            pl.semaphore_wait(barrier, MEMBERS + GROUPS - 2)
            layer_copy().start()
        start1(p)
        if p >= 1:
            pass_on(p - 1)
        if p >= 2:
            take_in(p - 2)

    layer_copy().wait()
    above_ref[...] = jnp.where(fe == MEMBERS - 1, 0.0, land_ref[...])
    pass_on(CHUNKS - 1)
    take_in(CHUNKS - 2)
    take_in(CHUNKS - 1)
    got_ref[0, 19 * CAP : 20 * CAP] = jnp.ones((CAP, 128), jnp.float32)

    label_value = lax.broadcasted_iota(jnp.int32, (NODES, 128), 0).astype(jnp.float32) + 1.0
    sums = jnp.zeros((8 * 24, NODES), jnp.float32)
    for r in range(0, CAP, 2):
        left, right = [], []
        for n in (r, r + 1):
            values = jnp.concatenate(
                [got_ref[p, pl.ds(n, 24, stride=CAP), :] for p in range(CHUNKS)], axis=0
            )
            high = values.astype(jnp.bfloat16).astype(jnp.float32)
            left.append(jnp.concatenate([high, values - high], axis=0).astype(jnp.bfloat16))
            hit = label_value == got_ref[0, 18 * CAP + n : 18 * CAP + n + 1, :]
            right.append(hit.astype(jnp.bfloat16))
        sums = sums + lax.dot_general(
            jnp.concatenate(left, axis=1),
            jnp.concatenate(right, axis=1),
            NT_DIMS,
            preferred_element_type=jnp.float32,
        )
    sums_ref[...] = sums[:96] + sums[96:]
    for p in range(CHUNKS):

        @pl.loop(1, MEMBERS)
        def _(i, p=p):
            hop1(p, i).wait_send()

        @pl.loop(1, GROUPS)
        def _(i, p=p):
            hop2(p, i).wait_send()


def exchanged_sums(grain_ids, euler_angles, owner, element, active, below):
    bricks = grain_ids.shape[1]
    hop = pltpu.VMEM((CHUNKS, CHUNK_ROWS, DEVICES, 128), jnp.float32)
    vmem = pl.BlockSpec(memory_space=pltpu.VMEM)
    return pl.pallas_call(
        exchange_kernel,
        out_shape=(
            jax.ShapeDtypeStruct((96, NODES), jnp.float32),
            jax.ShapeDtypeStruct((3, NODES), jnp.float32),
        ),
        in_specs=[pl.BlockSpec(memory_space=pl.ANY)] + [vmem] * 5,
        out_specs=(vmem, vmem),
        scratch_shapes=[
            pltpu.VMEM(grain_ids.shape, jnp.int32),
            pltpu.VMEM((3, 32, 128), jnp.float32),
            pltpu.VMEM((64, 8, 128), jnp.int32),
            pltpu.VMEM((bricks // 128, 9, 8, 128), jnp.float32),
            pltpu.VMEM((3, 8, bricks), jnp.float32),
            pltpu.VMEM((2 * CAP, 128), jnp.int32),
            pltpu.VMEM((CHUNK_ROWS * 128, 128), jnp.float32),
            hop,
            hop,
            hop,
            hop,
            pltpu.VMEM((CHUNKS, 24 * CAP, 128), jnp.float32),
            pltpu.VMEM((3, NODES), jnp.float32),
            pltpu.SemaphoreType.DMA((CHUNKS,)),
            pltpu.SemaphoreType.DMA((CHUNKS, MEMBERS)),
            pltpu.SemaphoreType.DMA((CHUNKS, MEMBERS)),
            pltpu.SemaphoreType.DMA((CHUNKS, GROUPS)),
            pltpu.SemaphoreType.DMA((CHUNKS, GROUPS)),
            pltpu.SemaphoreType.DMA((2,)),
        ],
        compiler_params=pltpu.CompilerParams(
            vmem_limit_bytes=VMEM_LIMIT, collective_id=0, has_side_effects=True
        ),
        name="exchanged_sums",
    )(
        grain_ids,
        euler_angles,
        owner.reshape(1, bricks),
        element.reshape(1, bricks),
        active.reshape(1, bricks),
        below,
    )


def split_three(values):
    high = values.astype(jnp.bfloat16)
    rest = values - high.astype(jnp.float32)
    mid = rest.astype(jnp.bfloat16)
    low = (rest - mid.astype(jnp.float32)).astype(jnp.bfloat16)
    return jnp.concatenate([high, mid, low], axis=0)


def joined_three(product):
    rows = product.shape[0] // 3
    return product[:rows] + product[rows : 2 * rows] + product[2 * rows :]


def element_kernel(
    sums_ref,
    below_ref,
    above_ref,
    stress_ref,
    resistance_ref,
    weights_ref,
    grads_ref,
    gather_ref,
    stress_out,
    owned_out,
    top_out,
):
    elements = stress_ref.shape[2]
    counts = sums_ref[19:20, :]
    weight = 1.0 / (8.0 * jnp.maximum(counts, 1.0))
    frames = []
    for n in range(9):
        lines = [sums_ref[24 * p + 2 * n : 24 * p + 2 * n + 2, :] for p in range(CHUNKS)]
        frames.append((jnp.concatenate(lines, axis=0) * weight)[:, :elements])

    node = lax.broadcasted_iota(jnp.int32, (NODES, NODES), 0)
    lane = lax.broadcasted_iota(jnp.int32, (NODES, NODES), 1)
    base = lane
    for bound in range(GX, GX * GX, GX):
        base = base + jnp.where(lane >= bound, 1, 0)
    to_element = ((node == base) & (lane < elements)).astype(jnp.bfloat16)
    rows = []
    for comp in range(3):
        for corner in range(8):
            step_x, step_y, step_z = (corner >> 2 & 1, corner >> 1 & 1, corner & 1)
            source = above_ref if step_z else below_ref
            offset = step_y * (GX + 1) + step_x
            line = source[comp : comp + 1, :]
            rows.append(line if offset == 0 else pltpu.roll(line, NODES - offset, 1))
    corners = joined_three(
        jnp.dot(
            split_three(jnp.concatenate(rows, axis=0)),
            to_element,
            preferred_element_type=jnp.float32,
        )
    )
    gradients = jnp.dot(
        grads_ref[...],
        corners,
        precision=lax.Precision.HIGHEST,
        preferred_element_type=jnp.float32,
    )

    def grad(comp, direction):
        n = (comp * 3 + direction) * 8
        return gradients[n : n + 8, :elements]

    strain = [
        grad(0, 0),
        grad(1, 1),
        grad(2, 2),
        0.5 * (grad(1, 2) + grad(2, 1)),
        0.5 * (grad(0, 2) + grad(2, 0)),
        0.5 * (grad(0, 1) + grad(1, 0)),
    ]
    volume = strain[0] + strain[1] + strain[2]
    trial = []
    for component in range(6):
        change = 2.0 * SHEAR_MODULUS * strain[component]
        if component < 3:
            change = change + LAMBDA_ELASTIC * volume
        trial.append(stress_ref[component] + change)

    def frame(i, j):
        return frames[i * 3 + j]

    def rotated(vector):
        out = []
        for i in range(3):
            terms = [float(vector[j]) * frame(i, j) for j in range(3) if vector[j] != 0.0]
            out.append(functools.reduce(lambda x, y: x + y, terms))
        return out

    normals = {tuple(vector): rotated(vector) for vector in SLIP_PLANES}
    correction = [jnp.zeros_like(trial[0]) for component in range(6)]
    for system in range(12):
        d = rotated(SLIP_DIRECTIONS[system])
        m = normals[tuple(SLIP_PLANES[system])]
        schmid = [
            d[0] * m[0],
            d[1] * m[1],
            d[2] * m[2],
            0.5 * (d[1] * m[2] + d[2] * m[1]),
            0.5 * (d[0] * m[2] + d[2] * m[0]),
            0.5 * (d[0] * m[1] + d[1] * m[0]),
        ]
        resolved = (
            trial[0] * schmid[0]
            + trial[1] * schmid[1]
            + trial[2] * schmid[2]
            + 2.0 * (trial[3] * schmid[3] + trial[4] * schmid[4] + trial[5] * schmid[5])
        )
        ratio = resolved / resistance_ref[system]
        slip_step = RATE_STEP * ratio * jnp.abs(ratio)
        correction = [
            correction[component] + slip_step * schmid[component] for component in range(6)
        ]
    updated = [
        trial[component] - 2.0 * SHEAR_MODULUS * correction[component] for component in range(6)
    ]
    for component in range(6):
        stress_out[component] = updated[component]
    scale = weights_ref[...].astype(jnp.float32) * (1.0 / (FIXED_POINT * 8.0))
    order = [0, 5, 4, 5, 1, 3, 4, 3, 2]
    pad = jnp.zeros((8, NODES - elements), jnp.float32)
    tensor = jnp.concatenate(
        [jnp.concatenate([updated[component] * scale, pad], axis=1) for component in order], axis=0
    )
    element_forces = jnp.dot(
        gather_ref[...],
        tensor,
        precision=lax.Precision.HIGHEST,
        preferred_element_type=jnp.float32,
    )
    placed = joined_three(
        lax.dot_general(
            split_three(element_forces), to_element, NT_DIMS, preferred_element_type=jnp.float32
        )
    )
    for out, step_z in ((owned_out, 0), (top_out, 1)):
        for comp in range(3):
            line = jnp.zeros((1, NODES), jnp.float32)
            for corner in range(8):
                if (corner & 1) != step_z:
                    continue
                offset = (corner >> 1 & 1) * (GX + 1) + (corner >> 2 & 1)
                part = placed[comp * 8 + corner : comp * 8 + corner + 1]
                line = line + (part if offset == 0 else pltpu.roll(part, offset, 1))
            out[comp : comp + 1, :] = line


def element_update(sums, below, above, stress_old, resistance, quad_weights):
    grads, forces = gradient_matrices()
    layer = jax.ShapeDtypeStruct((3, NODES), jnp.float32)
    return pl.pallas_call(
        element_kernel,
        out_shape=(jax.ShapeDtypeStruct(stress_old.shape, jnp.float32), layer, layer),
        in_specs=[pl.BlockSpec(memory_space=pltpu.VMEM)] * 8,
        out_specs=(pl.BlockSpec(memory_space=pltpu.VMEM),) * 3,
        compiler_params=pltpu.CompilerParams(vmem_limit_bytes=VMEM_LIMIT),
        name="element_update",
    )(
        sums,
        below,
        above,
        stress_old,
        resistance,
        quad_weights,
        jnp.asarray(grads),
        jnp.asarray(forces),
    )


def passed_along(block, axis, distance):
    devices = range(lax.axis_size(axis))
    route = [(i - distance, i) for i in devices if i - distance in devices]
    return lax.ppermute(block, axis, route)


def body(
    grain_ids,
    euler_angles,
    brick_active,
    brick_owner,
    brick_element,
    displacement,
    stress_old,
    resistance,
    quad_weights,
):
    below = displacement[:, 0]
    sums, above = exchanged_sums(
        grain_ids, euler_angles, brick_owner, brick_element, brick_active, below
    )
    stress_new, owned, top = element_update(
        sums, below, above, stress_old, resistance, quad_weights
    )
    forces = owned + passed_along(top, "fe", 1)
    return (stress_new, forces[:, None])


def solution(mesh):
    placed = (
        P(None, ("ca", "fe")),
        P(),
        P(("ca", "fe")),
        P(("ca", "fe"), None),
        P(("ca", "fe")),
        P(None, ("ca", "fe"), None),
        P(None, None, ("ca", "fe")),
        P(None, None, ("ca", "fe")),
        P(None, ("ca", "fe")),
    )
    return jax.shard_map(
        body,
        mesh=mesh,
        in_specs=placed,
        out_specs=(P(None, None, ("ca", "fe")), P(None, ("ca", "fe"), None)),
        check_vma=False,
    )
```

```python
import functools
import math

import jax
import jax.numpy as jnp
import numpy as np
from jax import lax
from jax.experimental import pallas as pl
from jax.experimental.pallas import tpu as pltpu
from jax.sharding import PartitionSpec as P

GX = 15
NODES = 256
CAP = 40
GROUPS = 8
MEMBERS = 16
DEVICES = GROUPS * MEMBERS
FIXED_STEPS = float(2**20 - 1)

SLIP_PLANES = [
    [value / math.sqrt(3.0) for value in row]
    for row in [[1, 1, 1]] * 3 + [[-1, 1, 1]] * 3 + [[1, -1, 1]] * 3 + [[1, 1, -1]] * 3
]
SLIP_DIRECTIONS = [
    [value / math.sqrt(2.0) for value in row]
    for row in [
        [0, 1, -1],
        [1, 0, -1],
        [1, -1, 0],
        [0, 1, -1],
        [1, 0, 1],
        [1, 1, 0],
        [0, 1, 1],
        [1, 0, -1],
        [1, 1, 0],
        [0, 1, 1],
        [1, 0, 1],
        [1, -1, 0],
    ]
]
LAMBDA_ELASTIC = 1.5
SHEAR_MODULUS = 1.0
RATE_STEP = 0.1
FIXED_POINT = 65536.0
EXCHANGE_VMEM = 63 << 20


def shape_gradients():
    grad_table = np.zeros((8, 8, 3))
    point_offset = 1.0 / math.sqrt(3.0)
    for quadrature in range(8):
        natural = [
            (2 * (quadrature >> shift_bits & 1) - 1) * point_offset for shift_bits in (2, 1, 0)
        ]
        for corner in range(8):
            sign_list = [2 * (corner >> shift_bits & 1) - 1 for shift_bits in (2, 1, 0)]
            factors = [1.0 + sign_list[axis_id] * natural[axis_id] for axis_id in range(3)]
            for direction in range(3):
                others = 1.0
                for axis_id in range(3):
                    if axis_id != direction:
                        others = others * factors[axis_id]
                grad_table[quadrature, corner, direction] = (
                    2.0 * sign_list[direction] * others / 8.0
                )
    return grad_table


def gradient_matrices():
    table = shape_gradients()
    grads = np.zeros((72, 24), np.float32)
    forces = np.zeros((24, 72), np.float32)
    for comp in range(3):
        for direction in range(3):
            for q in range(8):
                for corner in range(8):
                    value = table[q, corner, direction]
                    grads[(comp * 3 + direction) * 8 + q, comp * 8 + corner] = value
                    forces[comp * 8 + corner, (comp * 3 + direction) * 8 + q] = value
    return grads, forces


def lane_pick(row, lanes):
    return jnp.take_along_axis(row, lanes, axis=1, mode="promise_in_bounds")


def merge_tree(stack, value, index, bits):
    level = 0
    while index & 1:
        value = jnp.where(bits[level], value, stack.pop())
        level += 1
        index >>= 1
    stack.append(value)


def build_table(euler_ref, angle_ref, table_ref):
    for angle in range(3):
        for row in range(32):
            angle_ref[angle, row : row + 1] = euler_ref[
                angle : angle + 1, row * 128 : row * 128 + 128
            ]
    half_sum = 0.5 * (angle_ref[0] + angle_ref[2])
    half_diff = 0.5 * (angle_ref[0] - angle_ref[2])
    half_mid = 0.5 * angle_ref[1]
    cos_mid, sin_mid = jnp.cos(half_mid), jnp.sin(half_mid)
    real = cos_mid * jnp.cos(half_sum)
    flip = jnp.where(real < 0.0, -1.0, 1.0)
    scale = flip * FIXED_STEPS / (1.0 + jnp.abs(real))
    first = jnp.round(sin_mid * jnp.cos(half_diff) * scale).astype(jnp.int32)
    second = jnp.round(sin_mid * jnp.sin(half_diff) * scale).astype(jnp.int32)
    third = jnp.round(cos_mid * jnp.sin(half_sum) * scale).astype(jnp.int32)
    word_a = jnp.left_shift(first, 11) | (jnp.right_shift(third, 10) & 0x7FF)
    word_b = jnp.left_shift(second, 11) | (third & 0x3FF)
    for row in range(32):
        table_ref[row] = jnp.broadcast_to(word_a[row : row + 1], (8, 128))
        table_ref[32 + row] = jnp.broadcast_to(word_b[row : row + 1], (8, 128))


def lookup(table_ref, ids):
    lanes = ids & 127
    bits = [(ids & (128 << level)) != 0 for level in range(5)]
    words = ([], [])
    for row in range(32):
        for n, stack in enumerate(words):
            merge_tree(stack, lane_pick(table_ref[n * 32 + row], lanes), row, bits)
    return words[0][0], words[1][0]


def rotation_terms(word_a, word_b):
    a = jnp.right_shift(word_a, 11).astype(jnp.float32)
    b = jnp.right_shift(word_b, 11).astype(jnp.float32)
    c_bits = jnp.right_shift(jnp.left_shift(word_a, 21), 11) | (word_b & 0x3FF)
    c = c_bits.astype(jnp.float32)
    unit = 1.0 / FIXED_STEPS
    square = (a * a + b * b + c * c) * (unit * unit)
    inverse = 1.0 / (1.0 + square)
    inverse_square = inverse * inverse
    quad = inverse_square * (8.0 * unit * unit)
    lin = inverse_square * ((1.0 - square) * (4.0 * unit))
    qa, qb, qc = quad * a, quad * b, quad * c
    return [qa * a, qb * b, qc * c, qa * b, qa * c, qb * c, lin * a, lin * b, lin * c]


def octant_entries(terms, per_octant):
    xx, yy, zz, xy, xz, yz, wx, wy, wz = terms
    share = per_octant / 8.0
    return [
        share - (yy + zz),
        xy - wz,
        xz + wy,
        xy + wz,
        share - (xx + zz),
        yz - wx,
        xz - wy,
        yz + wx,
        share - (xx + yy),
    ]


def swapped(values, step, keep):
    return jnp.where(keep, pltpu.roll(values, 8 - step, 0), pltpu.roll(values, step, 0))


def sum_sublanes(parts, row):
    half = len(parts) // 2
    low4 = row < 4
    level = [
        jnp.where(low4, parts[n], parts[n + half])
        + pltpu.roll(jnp.where(low4, parts[n + half], parts[n]), 4, 0)
        for n in range(half)
    ]
    for step in (2, 1):
        keep = (row & step) == 0
        if len(level) == 1:
            level = [level[0] + swapped(level[0], step, keep)]
            continue
        half = len(level) // 2
        level = [
            jnp.where(keep, level[n], level[n + half])
            + swapped(jnp.where(keep, level[n + half], level[n]), step, keep)
            for n in range(half)
        ]
    return level[0]


NT_DIMS = (((1,), (1,)), ((), ()))
MESH = pl.DeviceIdType.MESH
OCTANTS = 8
CHUNKS = ((0, 2), (2, 4), (4, 6), (6, 7), (7, 8))
UNROLL = 4
WORDS = 384
ENTRY_ROWS = 8 * CAP
LABEL_ROWS = 368


def find_slots(owner_ref, element_ref, active_ref, owned_ref, rank_ref, single_ref, label_ref):
    span = 256
    device = lax.broadcasted_iota(jnp.int32, (DEVICES, span), 0)
    before = (
        lax.broadcasted_iota(jnp.int32, (span, span), 0)
        < lax.broadcasted_iota(jnp.int32, (span, span), 1)
    ).astype(jnp.bfloat16)
    ones = jnp.ones((span, span), jnp.bfloat16)
    slot = lax.broadcasted_iota(jnp.int32, (48, span), 0).astype(jnp.float32)
    carry = jnp.zeros((DEVICES, span), jnp.float32)
    for start in range(0, owner_ref.shape[1], span):
        owner = owner_ref[:, start : start + span]
        owned = device == ((owner & (MEMBERS - 1)) * GROUPS + jnp.right_shift(owner, 4))
        owned_half = owned.astype(jnp.bfloat16)
        earlier = carry + jnp.dot(owned_half, before, preferred_element_type=jnp.float32)
        carry = carry + jnp.dot(owned_half, ones, preferred_element_type=jnp.float32)
        rank = jnp.sum(jnp.where(owned, earlier, 0.0), axis=0, keepdims=True)
        label = jnp.where(
            active_ref[:, start : start + span] > 0, element_ref[:, start : start + span] + 1, 0
        ).astype(jnp.float32)
        single = jnp.where(slot == rank, 1.0, 0.0)
        labels = (single * label).astype(jnp.bfloat16)
        single = single.astype(jnp.bfloat16)
        eight = jnp.broadcast_to(rank, (8, span))
        for half in range(span // 128):
            lanes = slice(half * 128, half * 128 + 128)
            block = start // 128 + half
            place = (block % UNROLL) * 256
            owned_ref[block // UNROLL, :, place : place + 128] = owned_half[:, lanes]
            owned_ref[block // UNROLL, :, place + 128 : place + 256] = owned_half[:, lanes]
            single_ref[block] = single[:, lanes]
            label_ref[block] = labels[:, lanes]
            for pair in range(CAP // 2):
                both = [
                    jnp.where(eight[:, lanes] == float(2 * pair + n), 1.0, 0.0) for n in range(2)
                ]
                rank_ref[block, 16 * pair : 16 * pair + 16] = jnp.concatenate(
                    both, axis=0
                ).astype(jnp.bfloat16)


def halves(values):
    high = values.astype(jnp.bfloat16).astype(jnp.float32)
    out = []
    for part in (high, values - high):
        out.append(jnp.concatenate([part, part], axis=0).astype(jnp.bfloat16))
    return out


def split_three(values):
    high = values.astype(jnp.bfloat16)
    rest = values - high.astype(jnp.float32)
    mid = rest.astype(jnp.bfloat16)
    low = (rest - mid.astype(jnp.float32)).astype(jnp.bfloat16)
    return jnp.concatenate([high, mid, low], axis=0)


def joined_three(product):
    rows = product.shape[0] // 3
    return product[:rows] + product[rows : 2 * rows] + product[2 * rows :]


def element_places(elements):
    node = lax.broadcasted_iota(jnp.int32, (NODES, NODES), 0)
    lane = lax.broadcasted_iota(jnp.int32, (NODES, NODES), 1)
    base = lane
    for bound in range(GX, GX * GX, GX):
        base = base + jnp.where(lane >= bound, 1, 0)
    return ((node == base) & (lane < elements)).astype(jnp.bfloat16)


def trial_stress(below_ref, above_ref, stress_ref, grads_ref):
    elements = stress_ref.shape[2]
    to_element = element_places(elements)
    rows = []
    for comp in range(3):
        for corner in range(8):
            step_x, step_y, step_z = (corner >> 2 & 1, corner >> 1 & 1, corner & 1)
            source = above_ref if step_z else below_ref
            offset = step_y * (GX + 1) + step_x
            line = source[comp]
            rows.append(line if offset == 0 else pltpu.roll(line, NODES - offset, 1))
    corners = joined_three(
        jnp.dot(
            split_three(jnp.concatenate(rows, axis=0)),
            to_element,
            preferred_element_type=jnp.float32,
        )
    )
    gradients = jnp.dot(
        grads_ref[...],
        corners,
        precision=lax.Precision.HIGHEST,
        preferred_element_type=jnp.float32,
    )

    def grad(comp, direction):
        n = (comp * 3 + direction) * 8
        return gradients[n : n + 8, :elements]

    strain = [
        grad(0, 0),
        grad(1, 1),
        grad(2, 2),
        0.5 * (grad(1, 2) + grad(2, 1)),
        0.5 * (grad(0, 2) + grad(2, 0)),
        0.5 * (grad(0, 1) + grad(1, 0)),
    ]
    volume = strain[0] + strain[1] + strain[2]
    trial = []
    for component in range(6):
        change = 2.0 * SHEAR_MODULUS * strain[component]
        if component < 3:
            change = change + LAMBDA_ELASTIC * volume
        trial.append(stress_ref[component] + change)
    return trial


def stress_update(sums_ref, trial, resistance_ref):
    elements = resistance_ref.shape[2]
    weights = [1.0 / (8.0 * jnp.maximum(sums_ref[half, 72:73], 1.0)) for half in range(2)]
    frames = []
    for n in range(9):
        rows = pl.ds(n, OCTANTS, stride=8) if n < 8 else pl.ds(64, OCTANTS)
        parts = [sums_ref[half, rows, :] * weights[half] for half in range(2)]
        frames.append(jnp.concatenate(parts, axis=1)[:, :elements])

    def frame(i, j):
        return frames[i * 3 + j]

    def rotated(vector):
        out = []
        for i in range(3):
            terms = [float(vector[j]) * frame(i, j) for j in range(3) if vector[j] != 0.0]
            out.append(functools.reduce(lambda x, y: x + y, terms))
        return out

    normals = {tuple(vector): rotated(vector) for vector in SLIP_PLANES}
    correction = [jnp.zeros_like(trial[0]) for component in range(6)]
    for system in range(12):
        d = rotated(SLIP_DIRECTIONS[system])
        m = normals[tuple(SLIP_PLANES[system])]
        schmid = [
            d[0] * m[0],
            d[1] * m[1],
            d[2] * m[2],
            0.5 * (d[1] * m[2] + d[2] * m[1]),
            0.5 * (d[0] * m[2] + d[2] * m[0]),
            0.5 * (d[0] * m[1] + d[1] * m[0]),
        ]
        resolved = (
            trial[0] * schmid[0]
            + trial[1] * schmid[1]
            + trial[2] * schmid[2]
            + 2.0 * (trial[3] * schmid[3] + trial[4] * schmid[4] + trial[5] * schmid[5])
        )
        ratio = resolved / resistance_ref[system]
        slip_step = RATE_STEP * ratio * jnp.abs(ratio)
        correction = [
            correction[component] + slip_step * schmid[component] for component in range(6)
        ]
    updated = [
        trial[component] - 2.0 * SHEAR_MODULUS * correction[component] for component in range(6)
    ]
    return updated


def nodal_parts(updated, weights_ref, gather_ref):
    elements = weights_ref.shape[1]
    to_element = element_places(elements)
    scale = weights_ref[...].astype(jnp.float32) * (1.0 / (FIXED_POINT * 8.0))
    order = [0, 5, 4, 5, 1, 3, 4, 3, 2]
    pad = jnp.zeros((8, NODES - elements), jnp.float32)
    tensor = jnp.concatenate(
        [jnp.concatenate([updated[component] * scale, pad], axis=1) for component in order], axis=0
    )
    element_forces = jnp.dot(
        gather_ref[...],
        tensor,
        precision=lax.Precision.HIGHEST,
        preferred_element_type=jnp.float32,
    )
    placed = joined_three(
        lax.dot_general(
            split_three(element_forces), to_element, NT_DIMS, preferred_element_type=jnp.float32
        )
    )
    return placed


def layer_forces(placed, comp, step_z):
    line = jnp.zeros((1, NODES), jnp.float32)
    for corner in range(8):
        if (corner & 1) != step_z:
            continue
        offset = (corner >> 1 & 1) * (GX + 1) + (corner >> 2 & 1)
        part = placed[comp * 8 + corner : comp * 8 + corner + 1]
        line = line + (part if offset == 0 else pltpu.roll(part, offset, 1))
    return line


def exchange_kernel(
    ids_hbm,
    euler_hbm,
    owner_hbm,
    element_hbm,
    active_hbm,
    below_hbm,
    stress_hbm,
    resistance_hbm,
    weights_hbm,
    grads_hbm,
    gather_hbm,
    stress_out,
    forces_out,
    ids_ref,
    euler_ref,
    owner_ref,
    element_ref,
    active_ref,
    below_ref,
    angle_ref,
    table_ref,
    carry_ref,
    owned_ref,
    rank_ref,
    single_ref,
    label_ref,
    part_ref,
    wide_ref,
    acc_ref,
    out1_ref,
    in1_ref,
    out2_ref,
    in2_ref,
    got_ref,
    last_ref,
    sums_ref,
    stress_ref,
    resistance_ref,
    weights_ref,
    grads_ref,
    gather_ref,
    land_ref,
    above_ref,
    top_ref,
    under_ref,
    trial_ref,
    ids_sem,
    small_sem,
    send1_sem,
    recv1_sem,
    send2_sem,
    recv2_sem,
    layer_sem,
):
    ca, fe = lax.axis_index("ca"), lax.axis_index("fe")
    barrier = pltpu.get_barrier_semaphore()

    def member(i):
        return lax.rem(fe + i, MEMBERS)

    def group(i):
        return lax.rem(ca + i, GROUPS)

    row = lax.broadcasted_iota(jnp.int32, (8, 128), 0)
    cells = ids_hbm.shape[0]
    per_octant = cells // OCTANTS
    tiles = cells // 8
    blocks = ids_hbm.shape[1] // 128
    steps = blocks // UNROLL
    id_cuts = (0, 32, 56, 112, 168, 216)

    def ids_copy(n):
        rows = pl.ds(id_cuts[n], id_cuts[n + 1] - id_cuts[n])
        return pltpu.make_async_copy(ids_hbm.at[rows], ids_ref.at[rows], ids_sem.at[n])

    small = [
        pltpu.make_async_copy(source, target, small_sem.at[n])
        for n, (source, target) in enumerate(
            [
                (owner_hbm, owner_ref),
                (element_hbm, element_ref),
                (active_hbm, active_ref),
                (euler_hbm, euler_ref),
                (below_hbm, below_ref),
                (stress_hbm, stress_ref),
                (resistance_hbm, resistance_ref),
                (weights_hbm, weights_ref),
                (grads_hbm, grads_ref),
                (gather_hbm, gather_ref),
            ]
        )
    ]
    for copy in small[:5]:
        copy.start()
    for n in range(len(id_cuts) - 1):
        ids_copy(n).start()
    for copy in small[5:]:
        copy.start()

    @pl.loop(1, MEMBERS)
    def _(i):
        pl.semaphore_signal(barrier, inc=1, device_id=(ca, member(i)), device_id_type=MESH)

    @pl.loop(1, GROUPS)
    def _(i):
        pl.semaphore_signal(barrier, inc=1, device_id=(group(i), fe), device_id_type=MESH)

    def hop1(p, i):
        there = pl.ds(pl.multiple_of(member(i) * GROUPS, 8), GROUPS)
        here = pl.ds(pl.multiple_of(fe * GROUPS, 8), GROUPS)
        octants = pl.ds(CHUNKS[p][0], CHUNKS[p][1] - CHUNKS[p][0])
        return pltpu.make_async_remote_copy(
            src_ref=out1_ref.at[octants, :, there],
            dst_ref=in1_ref.at[octants, :, here],
            send_sem=send1_sem.at[p, i],
            recv_sem=recv1_sem.at[p, i],
            device_id=(ca, member(i)),
            device_id_type=MESH,
        )

    def hop2(p, i):
        there = pl.ds(pl.multiple_of(group(i) * MEMBERS, 8), MEMBERS)
        here = pl.ds(pl.multiple_of(ca * MEMBERS, 8), MEMBERS)
        octants = pl.ds(CHUNKS[p][0], CHUNKS[p][1] - CHUNKS[p][0])
        return pltpu.make_async_remote_copy(
            src_ref=out2_ref.at[octants, :, there],
            dst_ref=in2_ref.at[octants, :, here],
            send_sem=send2_sem.at[p, i],
            recv_sem=recv2_sem.at[p, i],
            device_id=(group(i), fe),
            device_id_type=MESH,
        )

    def layer_copy():
        return pltpu.make_async_remote_copy(
            src_ref=below_ref,
            dst_ref=land_ref,
            send_sem=layer_sem.at[0],
            recv_sem=layer_sem.at[1],
            device_id=(ca, lax.rem(fe + MEMBERS - 1, MEMBERS)),
            device_id_type=MESH,
        )

    def top_copy():
        return pltpu.make_async_remote_copy(
            src_ref=top_ref,
            dst_ref=under_ref,
            send_sem=layer_sem.at[2],
            recv_sem=layer_sem.at[3],
            device_id=(ca, member(1)),
            device_id_type=MESH,
        )

    def start1(p):
        if p == 0:
            pl.semaphore_wait(barrier, MEMBERS + GROUPS - 2)
            layer_copy().start()

        @pl.loop(1, MEMBERS)
        def _(i):
            hop1(p, i).start()

        here = pl.ds(pl.multiple_of(fe * GROUPS, 8), GROUPS)
        for q in range(*CHUNKS[p]):
            in1_ref[q, :, here] = out1_ref[q, :, here]

    def pass_on(p):
        @pl.loop(1, MEMBERS)
        def _(i):
            hop1(p, i).wait_recv()

        for q in range(*CHUNKS[p]):
            for c in range(WORDS // 128):
                for g in range(GROUPS):
                    out2_ref[q, c, g * MEMBERS : g * MEMBERS + MEMBERS] = in1_ref[
                        q, c, pl.ds(g, MEMBERS, stride=GROUPS), :
                    ]

        @pl.loop(1, GROUPS)
        def _(i):
            hop2(p, i).start()

        here = pl.ds(pl.multiple_of(ca * MEMBERS, 8), MEMBERS)
        for q in range(*CHUNKS[p]):
            in2_ref[q, :, here] = out2_ref[q, :, here]

    def take_in(p):
        @pl.loop(1, GROUPS)
        def _(i):
            hop2(p, i).wait_recv()

        for q in range(*CHUNKS[p]):
            for c in range(WORDS // 128):
                flipped = in2_ref[q, c].T
                got_ref[q, c * 128 : c * 128 + 128] = flipped
                if c == 2:
                    last_ref[pl.ds(q, CAP, stride=OCTANTS), :] = flipped[
                        ENTRY_ROWS - 256 : ENTRY_ROWS - 256 + CAP
                    ]

    part_ref[...] = jnp.zeros(part_ref.shape, jnp.float32)
    wide_ref[...] = jnp.zeros(wide_ref.shape, jnp.bfloat16)
    acc_ref[...] = jnp.zeros(acc_ref.shape, jnp.float32)
    for copy in small[:5]:
        copy.wait()
    build_table(euler_ref, angle_ref, table_ref)
    find_slots(owner_ref, element_ref, active_ref, owned_ref, rank_ref, single_ref, label_ref)

    def spread(block, buffer, u, q):
        parts = [part_ref[buffer, u, n] for n in range(9)]
        single = parts[8]
        for shift in (4, 2, 1):
            single = single + pltpu.roll(single, shift, 0)
        main_halves = halves(sum_sublanes(parts[:8], row))
        single_halves = halves(single)
        for n in range(2):
            lanes = slice(u * 256 + n * 128, u * 256 + n * 128 + 128)
            for pair in range(CAP // 2):
                rows = slice(16 * pair, 16 * pair + 16)
                wide_ref[rows, lanes] = rank_ref[block, rows] * main_halves[n]
            for part in range(3):
                rows = slice(16 * part, 16 * part + 16)
                target = slice(ENTRY_ROWS + 16 * part, ENTRY_ROWS + 16 * part + 16)
                wide_ref[target, lanes] = single_ref[block, rows] * single_halves[n]
        if isinstance(q, int) and q >= 3:
            return
        rows = pl.ds(pl.multiple_of(16 * q, 16), 16)
        wide_ref[LABEL_ROWS:, u * 256 : u * 256 + 128] = label_ref[block, rows]

    def place(step):
        acc_ref[...] += lax.dot_general(
            owned_ref[step], wide_ref[...], NT_DIMS, preferred_element_type=jnp.float32
        )

    def finish(q):
        for c in range(WORDS // 128):
            out1_ref[q, c] = acc_ref[:, c * 128 : c * 128 + 128]
        acc_ref[...] = jnp.zeros(acc_ref.shape, jnp.float32)

    todo = {q: [] for q in range(OCTANTS + 1)}
    for p, (_, stop) in enumerate(CHUNKS):
        todo[stop].append((start1, p))
        todo[min(stop + 1, OCTANTS)].append((pass_on, p))
        todo[min(stop + 3, OCTANTS)].append((take_in, p))
    arrived = 0

    for q in range(OCTANTS):
        first = (q * per_octant) // 8
        stop = -(-((q + 1) * per_octant) // 8)
        fresh = first if first * 8 == q * per_octant else first + 1
        while id_cuts[arrived] < stop * 8:
            ids_copy(arrived).wait()
            arrived += 1

        @pl.loop(0, steps)
        def _(step, q=q, fresh=fresh, stop=stop):
            buffer = step & 1
            before = lax.rem(step + steps - 1, steps)
            label_octant = jnp.where(step == 0, max(q - 1, 0), min(q, 2)) if q < 4 else q
            for u in range(UNROLL):
                spread(before * UNROLL + u, 1 - buffer, u, label_octant)
                if u == UNROLL - 1:
                    place(before)
                block = step * UNROLL + u
                columns = pl.ds(pl.multiple_of(block * 128, 128), 128)
                sums = None if q == 0 else [carry_ref[block, n] for n in range(9)]
                for t in range(fresh, stop):
                    terms = rotation_terms(
                        *lookup(table_ref, ids_ref[8 * t : 8 * t + 8, columns])
                    )
                    split = (q + 1) * per_octant - 8 * t
                    if split < 8:
                        inside = row < split
                        for n in range(9):
                            carry_ref[block, n] = jnp.where(inside, 0.0, terms[n])
                        terms = [jnp.where(inside, v, 0.0) for v in terms]
                    sums = terms if sums is None else [s + v for s, v in zip(sums, terms)]
                for n, entry in enumerate(octant_entries(sums, per_octant)):
                    part_ref[buffer, u, n] = entry

            @pl.when(step == 0)
            def _():
                if q > 0:
                    finish(q - 1)
                else:
                    acc_ref[...] = jnp.zeros(acc_ref.shape, jnp.float32)
                for action, p in todo[q]:
                    action(p)

    for u in range(UNROLL):
        spread((steps - 1) * UNROLL + u, 1, u, OCTANTS - 1)
    place(steps - 1)
    finish(OCTANTS - 1)
    rest = sorted(todo[OCTANTS], key=lambda item: ORDER[item[0].__name__] + item[1])
    for action, p in rest[:1]:
        action(p)
    for copy in small[5:]:
        copy.wait()
    layer_copy().wait()
    above_ref[...] = jnp.where(fe == MEMBERS - 1, 0.0, land_ref[...])
    for n, trial in enumerate(trial_stress(below_ref, above_ref, stress_ref, grads_ref)):
        trial_ref[n] = trial
    for action, p in rest[1:]:
        action(p)

    label_value = lax.broadcasted_iota(jnp.int32, (NODES, 128), 0).astype(jnp.float32) + 1.0
    ones = jnp.ones((16, 128), jnp.bfloat16)
    sums = jnp.zeros((160, NODES), jnp.float32)
    for r in range(0, CAP, 2):
        left, right = [], []
        for n in (r, r + 1):
            values = jnp.concatenate(
                [got_ref[q, 8 * n : 8 * n + 8] for q in range(OCTANTS)]
                + [last_ref[8 * n : 8 * n + 8]],
                axis=0,
            )
            high = values.astype(jnp.bfloat16).astype(jnp.float32)
            both = jnp.concatenate([high, values - high], axis=0).astype(jnp.bfloat16)
            left.append(jnp.concatenate([both, ones], axis=0))
            line = LABEL_ROWS + n % 16
            hit = label_value == got_ref[n // 16, line : line + 1, :]
            right.append(hit.astype(jnp.bfloat16))
        sums = sums + lax.dot_general(
            jnp.concatenate(left, axis=1),
            jnp.concatenate(right, axis=1),
            NT_DIMS,
            preferred_element_type=jnp.float32,
        )
    for half in range(2):
        lanes = slice(half * 128, half * 128 + 128)
        sums_ref[half, :72] = sums[:72, lanes] + sums[72:144, lanes]
        sums_ref[half, 72:80] = sums[144:152, lanes]
    trial = [trial_ref[n] for n in range(6)]
    updated = stress_update(sums_ref, trial, resistance_ref)
    placed = nodal_parts(updated, weights_ref, gather_ref)
    for comp in range(3):
        top_ref[comp] = layer_forces(placed, comp, 1)
    top_copy().start()
    for component in range(6):
        stress_out[component] = updated[component]
    owned = [layer_forces(placed, comp, 0) for comp in range(3)]
    for p in range(len(CHUNKS)):

        @pl.loop(1, MEMBERS)
        def _(i, p=p):
            hop1(p, i).wait_send()

        @pl.loop(1, GROUPS)
        def _(i, p=p):
            hop2(p, i).wait_send()

    top_copy().wait()
    for comp in range(3):
        forces_out[comp] = owned[comp] + jnp.where(fe == 0, 0.0, under_ref[comp])


ORDER = {"start1": 0, "pass_on": 10, "take_in": 20}


def fused_step(
    grain_ids, euler_angles, owner, element, active, below, stress_old, resistance, quad_weights
):
    grads, forces = gradient_matrices()
    bricks = grain_ids.shape[1]
    blocks = bricks // 128
    hop = pltpu.VMEM((OCTANTS, WORDS // 128, DEVICES, 128), jnp.float32)
    vmem = pl.BlockSpec(memory_space=pltpu.VMEM)
    line = pltpu.VMEM((1, bricks), jnp.int32)
    layer = pltpu.VMEM(below.shape, jnp.float32)
    chunks = len(CHUNKS)
    return pl.pallas_call(
        exchange_kernel,
        out_shape=(
            jax.ShapeDtypeStruct(stress_old.shape, jnp.float32),
            jax.ShapeDtypeStruct(below.shape, jnp.float32),
        ),
        in_specs=[pl.BlockSpec(memory_space=pltpu.HBM)] * 11,
        out_specs=(vmem, vmem),
        scratch_shapes=[
            pltpu.VMEM(grain_ids.shape, jnp.int32),
            pltpu.VMEM(euler_angles.shape, jnp.float32),
            line,
            line,
            line,
            pltpu.VMEM(below.shape, jnp.float32),
            pltpu.VMEM((3, 32, 128), jnp.float32),
            pltpu.VMEM((64, 8, 128), jnp.int32),
            pltpu.VMEM((blocks, 9, 8, 128), jnp.float32),
            pltpu.VMEM((blocks // UNROLL, DEVICES, 256 * UNROLL), jnp.bfloat16),
            pltpu.VMEM((blocks, ENTRY_ROWS, 128), jnp.bfloat16),
            pltpu.VMEM((blocks, 48, 128), jnp.bfloat16),
            pltpu.VMEM((blocks, 48, 128), jnp.bfloat16),
            pltpu.VMEM((2, UNROLL, 9, 8, 128), jnp.float32),
            pltpu.VMEM((WORDS, 256 * UNROLL), jnp.bfloat16),
            pltpu.VMEM((DEVICES, WORDS), jnp.float32),
            hop,
            hop,
            hop,
            hop,
            pltpu.VMEM((OCTANTS, WORDS, 128), jnp.float32),
            pltpu.VMEM((OCTANTS * CAP, 128), jnp.float32),
            pltpu.VMEM((2, 80, 128), jnp.float32),
            pltpu.VMEM(stress_old.shape, jnp.float32),
            pltpu.VMEM(resistance.shape, jnp.float32),
            pltpu.VMEM(quad_weights.shape, jnp.int32),
            pltpu.VMEM(grads.shape, jnp.float32),
            pltpu.VMEM(forces.shape, jnp.float32),
            layer,
            layer,
            layer,
            layer,
            pltpu.VMEM(stress_old.shape, jnp.float32),
            pltpu.SemaphoreType.DMA((5,)),
            pltpu.SemaphoreType.DMA((10,)),
            pltpu.SemaphoreType.DMA((chunks, MEMBERS)),
            pltpu.SemaphoreType.DMA((chunks, MEMBERS)),
            pltpu.SemaphoreType.DMA((chunks, GROUPS)),
            pltpu.SemaphoreType.DMA((chunks, GROUPS)),
            pltpu.SemaphoreType.DMA((4,)),
        ],
        compiler_params=pltpu.CompilerParams(
            vmem_limit_bytes=EXCHANGE_VMEM, collective_id=0, has_side_effects=True
        ),
        name="fused_step",
    )(
        grain_ids,
        euler_angles,
        owner.reshape(1, bricks),
        element.reshape(1, bricks),
        active.reshape(1, bricks),
        below,
        stress_old,
        resistance,
        quad_weights,
        jnp.asarray(grads),
        jnp.asarray(forces),
    )


def body(
    grain_ids,
    euler_angles,
    brick_active,
    brick_owner,
    brick_element,
    displacement,
    stress_old,
    resistance,
    quad_weights,
):
    return fused_step(
        grain_ids,
        euler_angles,
        brick_owner,
        brick_element,
        brick_active,
        displacement,
        stress_old,
        resistance,
        quad_weights,
    )


def solution(mesh):
    placed = (
        P(None, ("ca", "fe")),
        P(),
        P(("ca", "fe")),
        P(("ca", "fe"), None),
        P(("ca", "fe")),
        P(None, ("ca", "fe"), None),
        P(None, None, ("ca", "fe")),
        P(None, None, ("ca", "fe")),
        P(None, ("ca", "fe")),
    )
    return jax.shard_map(
        body,
        mesh=mesh,
        in_specs=placed,
        out_specs=(P(None, None, ("ca", "fe")), P(None, ("ca", "fe"), None)),
        check_vma=False,
    )
```

```python
import functools
import math

import jax
import jax.numpy as jnp
import numpy as np
from jax import lax
from jax.experimental import pallas as pl
from jax.experimental.pallas import tpu as pltpu
from jax.sharding import PartitionSpec as P

GX = 15
NODES = 256
CAP = 40
GROUPS = 8
MEMBERS = 16
DEVICES = GROUPS * MEMBERS
FIXED_STEPS = float(2**20 - 1)

SLIP_PLANES = [
    [value / math.sqrt(3.0) for value in row]
    for row in [[1, 1, 1]] * 3 + [[-1, 1, 1]] * 3 + [[1, -1, 1]] * 3 + [[1, 1, -1]] * 3
]
SLIP_DIRECTIONS = [
    [value / math.sqrt(2.0) for value in row]
    for row in [
        [0, 1, -1],
        [1, 0, -1],
        [1, -1, 0],
        [0, 1, -1],
        [1, 0, 1],
        [1, 1, 0],
        [0, 1, 1],
        [1, 0, -1],
        [1, 1, 0],
        [0, 1, 1],
        [1, 0, 1],
        [1, -1, 0],
    ]
]
LAMBDA_ELASTIC = 1.5
SHEAR_MODULUS = 1.0
RATE_STEP = 0.1
FIXED_POINT = 65536.0
EXCHANGE_VMEM = 63 << 20


def shape_gradients():
    grad_table = np.zeros((8, 8, 3))
    point_offset = 1.0 / math.sqrt(3.0)
    for quadrature in range(8):
        natural = [
            (2 * (quadrature >> shift_bits & 1) - 1) * point_offset for shift_bits in (2, 1, 0)
        ]
        for corner in range(8):
            sign_list = [2 * (corner >> shift_bits & 1) - 1 for shift_bits in (2, 1, 0)]
            factors = [1.0 + sign_list[axis_id] * natural[axis_id] for axis_id in range(3)]
            for direction in range(3):
                others = 1.0
                for axis_id in range(3):
                    if axis_id != direction:
                        others = others * factors[axis_id]
                grad_table[quadrature, corner, direction] = (
                    2.0 * sign_list[direction] * others / 8.0
                )
    return grad_table


def gradient_matrices():
    table = shape_gradients()
    grads = np.zeros((72, 24), np.float32)
    forces = np.zeros((24, 72), np.float32)
    for comp in range(3):
        for direction in range(3):
            for q in range(8):
                for corner in range(8):
                    value = table[q, corner, direction]
                    grads[(comp * 3 + direction) * 8 + q, comp * 8 + corner] = value
                    forces[comp * 8 + corner, (comp * 3 + direction) * 8 + q] = value
    return grads, forces


def lane_pick(row, lanes):
    return jnp.take_along_axis(row, lanes, axis=1, mode="promise_in_bounds")


def merge_tree(stack, value, index, bits):
    level = 0
    while index & 1:
        value = jnp.where(bits[level], value, stack.pop())
        level += 1
        index >>= 1
    stack.append(value)


def build_table(euler_ref, angle_ref, table_ref):
    for angle in range(3):
        for row in range(32):
            angle_ref[angle, row : row + 1] = euler_ref[
                angle : angle + 1, row * 128 : row * 128 + 128
            ]
    half_sum = 0.5 * (angle_ref[0] + angle_ref[2])
    half_diff = 0.5 * (angle_ref[0] - angle_ref[2])
    half_mid = 0.5 * angle_ref[1]
    cos_mid, sin_mid = jnp.cos(half_mid), jnp.sin(half_mid)
    real = cos_mid * jnp.cos(half_sum)
    flip = jnp.where(real < 0.0, -1.0, 1.0)
    scale = flip * FIXED_STEPS / (1.0 + jnp.abs(real))
    first = jnp.round(sin_mid * jnp.cos(half_diff) * scale).astype(jnp.int32)
    second = jnp.round(sin_mid * jnp.sin(half_diff) * scale).astype(jnp.int32)
    third = jnp.round(cos_mid * jnp.sin(half_sum) * scale).astype(jnp.int32)
    word_a = jnp.left_shift(first, 11) | (jnp.right_shift(third, 10) & 0x7FF)
    word_b = jnp.left_shift(second, 11) | (third & 0x3FF)
    for row in range(32):
        table_ref[row] = jnp.broadcast_to(word_a[row : row + 1], (8, 128))
        table_ref[32 + row] = jnp.broadcast_to(word_b[row : row + 1], (8, 128))


def lookup(table_ref, ids):
    lanes = ids & 127
    bits = [(ids & (128 << level)) != 0 for level in range(5)]
    words = ([], [])
    for row in range(32):
        for n, stack in enumerate(words):
            merge_tree(stack, lane_pick(table_ref[n * 32 + row], lanes), row, bits)
    return words[0][0], words[1][0]


def rotation_terms(word_a, word_b):
    a = jnp.right_shift(word_a, 11).astype(jnp.float32)
    b = jnp.right_shift(word_b, 11).astype(jnp.float32)
    c_bits = jnp.right_shift(jnp.left_shift(word_a, 21), 11) | (word_b & 0x3FF)
    c = c_bits.astype(jnp.float32)
    unit = 1.0 / FIXED_STEPS
    square = (a * a + b * b + c * c) * (unit * unit)
    inverse = 1.0 / (1.0 + square)
    inverse_square = inverse * inverse
    quad = inverse_square * (8.0 * unit * unit)
    lin = inverse_square * ((1.0 - square) * (4.0 * unit))
    qa, qb, qc = quad * a, quad * b, quad * c
    return [qa * a, qb * b, qc * c, qa * b, qa * c, qb * c, lin * a, lin * b, lin * c]


def octant_entries(terms, per_octant):
    xx, yy, zz, xy, xz, yz, wx, wy, wz = terms
    share = per_octant / 8.0
    return [
        share - (yy + zz),
        xy - wz,
        xz + wy,
        xy + wz,
        share - (xx + zz),
        yz - wx,
        xz - wy,
        yz + wx,
        share - (xx + yy),
    ]


NT_DIMS = (((1,), (1,)), ((), ()))
MESH = pl.DeviceIdType.MESH
OCTANTS = 8
CHUNKS = ((0, 2), (2, 4), (4, 5), (5, 6), (6, 7), (7, 8))
UNROLL = 4
WORDS = 384
ENTRY_ROWS = 8 * CAP
LABEL_ROWS = 368


def find_slots(owner_ref, element_ref, active_ref, owned_ref, rank_ref, single_ref, label_ref):
    span = 256
    device = lax.broadcasted_iota(jnp.int32, (DEVICES, span), 0)
    before = (
        lax.broadcasted_iota(jnp.int32, (span, span), 0)
        < lax.broadcasted_iota(jnp.int32, (span, span), 1)
    ).astype(jnp.bfloat16)
    ones = jnp.ones((span, span), jnp.bfloat16)
    slot = lax.broadcasted_iota(jnp.int32, (48, span), 0).astype(jnp.float32)
    carry = jnp.zeros((DEVICES, span), jnp.float32)
    for start in range(0, owner_ref.shape[1], span):
        owner = owner_ref[:, start : start + span]
        owned = device == ((owner & (MEMBERS - 1)) * GROUPS + jnp.right_shift(owner, 4))
        owned_half = owned.astype(jnp.bfloat16)
        earlier = carry + jnp.dot(owned_half, before, preferred_element_type=jnp.float32)
        carry = carry + jnp.dot(owned_half, ones, preferred_element_type=jnp.float32)
        rank = jnp.sum(jnp.where(owned, earlier, 0.0), axis=0, keepdims=True)
        label = jnp.where(
            active_ref[:, start : start + span] > 0, element_ref[:, start : start + span] + 1, 0
        ).astype(jnp.float32)
        single = jnp.where(slot == rank, 1.0, 0.0)
        labels = (single * label).astype(jnp.bfloat16)
        single = single.astype(jnp.bfloat16)
        eight = jnp.broadcast_to(rank, (8, span))
        for half in range(span // 128):
            lanes = slice(half * 128, half * 128 + 128)
            block = start // 128 + half
            place = (block % UNROLL) * 256
            owned_ref[block // UNROLL, :, place : place + 128] = owned_half[:, lanes]
            owned_ref[block // UNROLL, :, place + 128 : place + 256] = owned_half[:, lanes]
            single_ref[block] = single[:, lanes]
            label_ref[block] = labels[:, lanes]
            for pair in range(CAP // 2):
                both = [
                    jnp.where(eight[:, lanes] == float(2 * pair + n), 1.0, 0.0) for n in range(2)
                ]
                rank_ref[block, 16 * pair : 16 * pair + 16] = jnp.concatenate(
                    both, axis=0
                ).astype(jnp.bfloat16)


def halves(values):
    high = values.astype(jnp.bfloat16).astype(jnp.float32)
    out = []
    for part in (high, values - high):
        out.append(jnp.concatenate([part, part], axis=0).astype(jnp.bfloat16))
    return out


def split_three(values):
    high = values.astype(jnp.bfloat16)
    rest = values - high.astype(jnp.float32)
    mid = rest.astype(jnp.bfloat16)
    low = (rest - mid.astype(jnp.float32)).astype(jnp.bfloat16)
    return jnp.concatenate([high, mid, low], axis=0)


def joined_three(product):
    rows = product.shape[0] // 3
    return product[:rows] + product[rows : 2 * rows] + product[2 * rows :]


def element_places(elements):
    node = lax.broadcasted_iota(jnp.int32, (NODES, NODES), 0)
    lane = lax.broadcasted_iota(jnp.int32, (NODES, NODES), 1)
    base = lane
    for bound in range(GX, GX * GX, GX):
        base = base + jnp.where(lane >= bound, 1, 0)
    return ((node == base) & (lane < elements)).astype(jnp.bfloat16)


def trial_stress(below_ref, above_ref, stress_ref, grads_ref):
    elements = stress_ref.shape[2]
    to_element = element_places(elements)
    rows = []
    for comp in range(3):
        for corner in range(8):
            step_x, step_y, step_z = (corner >> 2 & 1, corner >> 1 & 1, corner & 1)
            source = above_ref if step_z else below_ref
            offset = step_y * (GX + 1) + step_x
            line = source[comp]
            rows.append(line if offset == 0 else pltpu.roll(line, NODES - offset, 1))
    corners = joined_three(
        jnp.dot(
            split_three(jnp.concatenate(rows, axis=0)),
            to_element,
            preferred_element_type=jnp.float32,
        )
    )
    gradients = jnp.dot(
        grads_ref[...],
        corners,
        precision=lax.Precision.HIGHEST,
        preferred_element_type=jnp.float32,
    )

    def grad(comp, direction):
        n = (comp * 3 + direction) * 8
        return gradients[n : n + 8, :elements]

    strain = [
        grad(0, 0),
        grad(1, 1),
        grad(2, 2),
        0.5 * (grad(1, 2) + grad(2, 1)),
        0.5 * (grad(0, 2) + grad(2, 0)),
        0.5 * (grad(0, 1) + grad(1, 0)),
    ]
    volume = strain[0] + strain[1] + strain[2]
    trial = []
    for component in range(6):
        change = 2.0 * SHEAR_MODULUS * strain[component]
        if component < 3:
            change = change + LAMBDA_ELASTIC * volume
        trial.append(stress_ref[component] + change)
    return trial


def stress_update(sums_ref, trial, resistance_ref):
    elements = resistance_ref.shape[2]
    weights = [1.0 / (8.0 * jnp.maximum(sums_ref[half, 72:73], 1.0)) for half in range(2)]
    frames = []
    for n in range(9):
        rows = pl.ds(n, OCTANTS, stride=8) if n < 8 else pl.ds(64, OCTANTS)
        parts = [sums_ref[half, rows, :] * weights[half] for half in range(2)]
        frames.append(jnp.concatenate(parts, axis=1)[:, :elements])

    def frame(i, j):
        return frames[i * 3 + j]

    def rotated(vector):
        out = []
        for i in range(3):
            terms = [float(vector[j]) * frame(i, j) for j in range(3) if vector[j] != 0.0]
            out.append(functools.reduce(lambda x, y: x + y, terms))
        return out

    normals = {tuple(vector): rotated(vector) for vector in SLIP_PLANES}
    correction = [jnp.zeros_like(trial[0]) for component in range(6)]
    for system in range(12):
        d = rotated(SLIP_DIRECTIONS[system])
        m = normals[tuple(SLIP_PLANES[system])]
        schmid = [
            d[0] * m[0],
            d[1] * m[1],
            d[2] * m[2],
            0.5 * (d[1] * m[2] + d[2] * m[1]),
            0.5 * (d[0] * m[2] + d[2] * m[0]),
            0.5 * (d[0] * m[1] + d[1] * m[0]),
        ]
        resolved = (
            trial[0] * schmid[0]
            + trial[1] * schmid[1]
            + trial[2] * schmid[2]
            + 2.0 * (trial[3] * schmid[3] + trial[4] * schmid[4] + trial[5] * schmid[5])
        )
        ratio = resolved / resistance_ref[system]
        slip_step = RATE_STEP * ratio * jnp.abs(ratio)
        correction = [
            correction[component] + slip_step * schmid[component] for component in range(6)
        ]
    updated = [
        trial[component] - 2.0 * SHEAR_MODULUS * correction[component] for component in range(6)
    ]
    return updated


def nodal_parts(updated, weights_ref, gather_ref):
    elements = weights_ref.shape[1]
    to_element = element_places(elements)
    scale = weights_ref[...].astype(jnp.float32) * (1.0 / (FIXED_POINT * 8.0))
    order = [0, 5, 4, 5, 1, 3, 4, 3, 2]
    pad = jnp.zeros((8, NODES - elements), jnp.float32)
    tensor = jnp.concatenate(
        [jnp.concatenate([updated[component] * scale, pad], axis=1) for component in order], axis=0
    )
    element_forces = jnp.dot(
        gather_ref[...],
        tensor,
        precision=lax.Precision.HIGHEST,
        preferred_element_type=jnp.float32,
    )
    placed = joined_three(
        lax.dot_general(
            split_three(element_forces), to_element, NT_DIMS, preferred_element_type=jnp.float32
        )
    )
    return placed


def layer_forces(placed, comp, step_z):
    line = jnp.zeros((1, NODES), jnp.float32)
    for corner in range(8):
        if (corner & 1) != step_z:
            continue
        offset = (corner >> 1 & 1) * (GX + 1) + (corner >> 2 & 1)
        part = placed[comp * 8 + corner : comp * 8 + corner + 1]
        line = line + (part if offset == 0 else pltpu.roll(part, offset, 1))
    return line


def exchange_kernel(
    ids_hbm,
    euler_hbm,
    owner_hbm,
    element_hbm,
    active_hbm,
    below_hbm,
    stress_hbm,
    resistance_hbm,
    weights_hbm,
    grads_hbm,
    gather_hbm,
    stress_out,
    forces_out,
    ids_ref,
    euler_ref,
    owner_ref,
    element_ref,
    active_ref,
    below_ref,
    angle_ref,
    table_ref,
    carry_ref,
    owned_ref,
    rank_ref,
    single_ref,
    label_ref,
    part_ref,
    pool_ref,
    stage_ref,
    wide_ref,
    acc_ref,
    out1_ref,
    in1_ref,
    out2_ref,
    in2_ref,
    got_ref,
    last_ref,
    hit_ref,
    sums_ref,
    stress_ref,
    resistance_ref,
    weights_ref,
    grads_ref,
    gather_ref,
    land_ref,
    above_ref,
    top_ref,
    under_ref,
    trial_ref,
    ids_sem,
    small_sem,
    send1_sem,
    recv1_sem,
    send2_sem,
    recv2_sem,
    layer_sem,
):
    ca, fe = lax.axis_index("ca"), lax.axis_index("fe")
    barrier = pltpu.get_barrier_semaphore()

    def member(i):
        return lax.rem(fe + i, MEMBERS)

    def group(i):
        return lax.rem(ca + i, GROUPS)

    row = lax.broadcasted_iota(jnp.int32, (8, 128), 0)
    cells = ids_hbm.shape[0]
    per_octant = cells // OCTANTS
    tiles = cells // 8
    blocks = ids_hbm.shape[1] // 128
    steps = blocks // UNROLL
    id_cuts = (0, 32, 56, 112, 168, 216)

    def ids_copy(n):
        rows = pl.ds(id_cuts[n], id_cuts[n + 1] - id_cuts[n])
        return pltpu.make_async_copy(ids_hbm.at[rows], ids_ref.at[rows], ids_sem.at[n])

    small = [
        pltpu.make_async_copy(source, target, small_sem.at[n])
        for n, (source, target) in enumerate(
            [
                (owner_hbm, owner_ref),
                (element_hbm, element_ref),
                (active_hbm, active_ref),
                (euler_hbm, euler_ref),
                (below_hbm, below_ref),
                (stress_hbm, stress_ref),
                (resistance_hbm, resistance_ref),
                (weights_hbm, weights_ref),
                (grads_hbm, grads_ref),
                (gather_hbm, gather_ref),
            ]
        )
    ]
    for copy in small[:5]:
        copy.start()
    for n in range(len(id_cuts) - 1):
        ids_copy(n).start()
    for copy in small[5:]:
        copy.start()

    @pl.loop(1, MEMBERS)
    def _(i):
        pl.semaphore_signal(barrier, inc=1, device_id=(ca, member(i)), device_id_type=MESH)

    @pl.loop(1, GROUPS)
    def _(i):
        pl.semaphore_signal(barrier, inc=1, device_id=(group(i), fe), device_id_type=MESH)

    def hop1(p, i):
        there = pl.ds(pl.multiple_of(member(i) * GROUPS, 8), GROUPS)
        here = pl.ds(pl.multiple_of(fe * GROUPS, 8), GROUPS)
        octants = pl.ds(CHUNKS[p][0], CHUNKS[p][1] - CHUNKS[p][0])
        return pltpu.make_async_remote_copy(
            src_ref=out1_ref.at[octants, :, there],
            dst_ref=in1_ref.at[octants, :, here],
            send_sem=send1_sem.at[p, i],
            recv_sem=recv1_sem.at[p, i],
            device_id=(ca, member(i)),
            device_id_type=MESH,
        )

    def hop2(p, i):
        there = pl.ds(pl.multiple_of(group(i) * MEMBERS, 8), MEMBERS)
        here = pl.ds(pl.multiple_of(ca * MEMBERS, 8), MEMBERS)
        octants = pl.ds(CHUNKS[p][0], CHUNKS[p][1] - CHUNKS[p][0])
        return pltpu.make_async_remote_copy(
            src_ref=out2_ref.at[octants, :, there],
            dst_ref=in2_ref.at[octants, :, here],
            send_sem=send2_sem.at[p, i],
            recv_sem=recv2_sem.at[p, i],
            device_id=(group(i), fe),
            device_id_type=MESH,
        )

    def layer_copy():
        return pltpu.make_async_remote_copy(
            src_ref=below_ref,
            dst_ref=land_ref,
            send_sem=layer_sem.at[0],
            recv_sem=layer_sem.at[1],
            device_id=(ca, lax.rem(fe + MEMBERS - 1, MEMBERS)),
            device_id_type=MESH,
        )

    def top_copy():
        return pltpu.make_async_remote_copy(
            src_ref=top_ref,
            dst_ref=under_ref,
            send_sem=layer_sem.at[2],
            recv_sem=layer_sem.at[3],
            device_id=(ca, member(1)),
            device_id_type=MESH,
        )

    def start1(p):
        if p == 0:
            pl.semaphore_wait(barrier, MEMBERS + GROUPS - 2)
            layer_copy().start()

        @pl.loop(1, MEMBERS)
        def _(i):
            hop1(p, i).start()

        here = pl.ds(pl.multiple_of(fe * GROUPS, 8), GROUPS)
        for q in range(*CHUNKS[p]):
            in1_ref[q, :, here] = out1_ref[q, :, here]

    def pass_on(p):
        @pl.loop(1, MEMBERS)
        def _(i):
            hop1(p, i).wait_recv()

        for q in range(*CHUNKS[p]):
            for c in range(WORDS // 128):
                for g in range(GROUPS):
                    out2_ref[q, c, g * MEMBERS : g * MEMBERS + MEMBERS] = in1_ref[
                        q, c, pl.ds(g, MEMBERS, stride=GROUPS), :
                    ]

        @pl.loop(1, GROUPS)
        def _(i):
            hop2(p, i).start()

        here = pl.ds(pl.multiple_of(ca * MEMBERS, 8), MEMBERS)
        for q in range(*CHUNKS[p]):
            in2_ref[q, :, here] = out2_ref[q, :, here]

    def take_in(p):
        @pl.loop(1, GROUPS)
        def _(i):
            hop2(p, i).wait_recv()

        for q in range(*CHUNKS[p]):
            for c in range(WORDS // 128):
                flipped = in2_ref[q, c].T
                got_ref[q, c * 128 : c * 128 + 128] = flipped
                if c == 2:
                    last_ref[pl.ds(q, CAP, stride=OCTANTS), :] = flipped[
                        ENTRY_ROWS - 256 : ENTRY_ROWS - 256 + CAP
                    ]

    part_ref[...] = jnp.zeros(part_ref.shape, jnp.bfloat16)
    target = jnp.minimum(lax.broadcasted_iota(jnp.int32, (16, 160), 0), 8)
    source = lax.broadcasted_iota(jnp.int32, (16, 160), 1)
    source = jnp.right_shift(jnp.where(source >= 80, source - 80, source), 3)
    pool_ref[...] = jnp.where(target == source, 1.0, 0.0).astype(jnp.bfloat16)
    wide_ref[...] = jnp.zeros(wide_ref.shape, jnp.bfloat16)
    acc_ref[...] = jnp.zeros(acc_ref.shape, jnp.float32)
    for copy in small[:5]:
        copy.wait()
    build_table(euler_ref, angle_ref, table_ref)
    find_slots(owner_ref, element_ref, active_ref, owned_ref, rank_ref, single_ref, label_ref)

    def keep_parts(u, entries):
        stacked = jnp.concatenate(entries + [jnp.zeros((8, 128), jnp.float32)], axis=0)
        high = stacked.astype(jnp.bfloat16)
        lanes = slice(u * 128, u * 128 + 128)
        part_ref[:80, lanes] = high
        part_ref[80:, lanes] = (stacked - high.astype(jnp.float32)).astype(jnp.bfloat16)

    def totals():
        return jnp.dot(pool_ref[...], part_ref[...], preferred_element_type=jnp.float32)

    def spread(block, u, q, total):
        columns = slice(u * 128, u * 128 + 128)
        main_halves = halves(total[:8, columns])
        single_halves = halves(total[8:, columns])
        for n in range(2):
            lanes = slice(u * 256 + n * 128, u * 256 + n * 128 + 128)
            for pair in range(CAP // 2):
                rows = slice(16 * pair, 16 * pair + 16)
                wide_ref[rows, lanes] = rank_ref[block, rows] * main_halves[n]
            for part in range(3):
                rows = slice(16 * part, 16 * part + 16)
                target = slice(ENTRY_ROWS + 16 * part, ENTRY_ROWS + 16 * part + 16)
                wide_ref[target, lanes] = single_ref[block, rows] * single_halves[n]
        if isinstance(q, int) and q >= 3:
            return
        rows = pl.ds(pl.multiple_of(16 * q, 16), 16)
        wide_ref[LABEL_ROWS:, u * 256 : u * 256 + 128] = label_ref[block, rows]

    def place(step):
        acc_ref[...] += lax.dot_general(
            owned_ref[step], wide_ref[...], NT_DIMS, preferred_element_type=jnp.float32
        )

    def finish(q):
        for c in range(WORDS // 128):
            out1_ref[q, c] = acc_ref[:, c * 128 : c * 128 + 128]
        acc_ref[...] = jnp.zeros(acc_ref.shape, jnp.float32)

    todo = {}
    for action, times in (
        (start1, ((2, 0), (4, 0), (5, 0), (6, 0), (7, 0), (8, 0))),
        (pass_on, ((3, 1), (5, 1), (6, 0), (7, 0), (7, 3), (8, 0))),
        (take_in, ((4, 3), (6, 3), (7, 3), (8, 0), (8, 0), (8, 0))),
    ):
        for p, time in enumerate(times):
            todo.setdefault(time, []).append((action, p))
    arrived = 0

    for q in range(OCTANTS):
        first = (q * per_octant) // 8
        stop = -(-((q + 1) * per_octant) // 8)
        fresh = first if first * 8 == q * per_octant else first + 1
        while id_cuts[arrived] < stop * 8:
            ids_copy(arrived).wait()
            arrived += 1

        @pl.loop(0, steps)
        def _(step, q=q, fresh=fresh, stop=stop):
            before = lax.rem(step + steps - 1, steps)
            label_octant = jnp.where(step == 0, max(q - 1, 0), min(q, 2)) if q < 4 else q
            if q > 0:
                for u in range(UNROLL):
                    stage_ref[0, u] = carry_ref[step * UNROLL + u]
            total = totals()
            for u in range(UNROLL):
                spread(before * UNROLL + u, u, label_octant, total)
                if u == UNROLL - 1:
                    place(before)
                block = step * UNROLL + u
                columns = pl.ds(pl.multiple_of(block * 128, 128), 128)
                sums = None if q == 0 else [stage_ref[0, u, n] for n in range(9)]
                for t in range(fresh, stop):
                    terms = rotation_terms(
                        *lookup(table_ref, ids_ref[8 * t : 8 * t + 8, columns])
                    )
                    split = (q + 1) * per_octant - 8 * t
                    if split < 8:
                        inside = row < split
                        for n in range(9):
                            stage_ref[1, u, n] = jnp.where(inside, 0.0, terms[n])
                        terms = [jnp.where(inside, v, 0.0) for v in terms]
                    sums = terms if sums is None else [s + v for s, v in zip(sums, terms)]
                keep_parts(u, octant_entries(sums, per_octant))

            if q < OCTANTS - 1:
                for u in range(UNROLL):
                    carry_ref[step * UNROLL + u] = stage_ref[1, u]

            @pl.when(step == 0)
            def _():
                if q > 0:
                    finish(q - 1)
                else:
                    acc_ref[...] = jnp.zeros(acc_ref.shape, jnp.float32)

            for late in range(4):
                if (q, late) in todo:

                    @pl.when(step == late * steps // 4)
                    def _(late=late):
                        for action, p in todo[q, late]:
                            action(p)

    total = totals()
    for u in range(UNROLL):
        spread((steps - 1) * UNROLL + u, u, OCTANTS - 1, total)
    place(steps - 1)
    finish(OCTANTS - 1)
    rest = sorted(todo[OCTANTS, 0], key=lambda item: ORDER[item[0].__name__] + item[1])
    for action, p in rest[:1]:
        action(p)
    for copy in small[5:]:
        copy.wait()
    layer_copy().wait()
    above_ref[...] = jnp.where(fe == MEMBERS - 1, 0.0, land_ref[...])
    for n, trial in enumerate(trial_stress(below_ref, above_ref, stress_ref, grads_ref)):
        trial_ref[n] = trial
    for action, p in rest[1:-1]:
        action(p)

    ones = jnp.ones((16, 128), jnp.bfloat16)

    def owner_sums(octants, last, rows):
        sums = jnp.zeros((rows, NODES), jnp.float32)
        for r in range(0, CAP, 2):
            left = []
            for n in (r, r + 1):
                values = [got_ref[q, 8 * n : 8 * n + 8] for q in octants]
                if last:
                    values.append(last_ref[8 * n : 8 * n + 8])
                values = jnp.concatenate(values, axis=0)
                high = values.astype(jnp.bfloat16).astype(jnp.float32)
                both = jnp.concatenate([high, values - high], axis=0).astype(jnp.bfloat16)
                left.append(both if last else jnp.concatenate([both, ones], axis=0))
            sums = sums + lax.dot_general(
                jnp.concatenate(left, axis=1),
                hit_ref[r // 2],
                NT_DIMS,
                preferred_element_type=jnp.float32,
            )
        return sums

    label_value = lax.broadcasted_iota(jnp.int32, (NODES, 128), 0).astype(jnp.float32) + 1.0
    for n in range(CAP):
        line = LABEL_ROWS + n % 16
        hit = label_value == got_ref[n // 16, line : line + 1, :]
        lanes = slice((n & 1) * 128, (n & 1) * 128 + 128)
        hit_ref[n // 2, :, lanes] = hit.astype(jnp.bfloat16)
    early = owner_sums(range(OCTANTS - 1), False, 128)
    action, p = rest[-1]
    action(p)
    late = owner_sums([OCTANTS - 1], True, 32)
    for half in range(2):
        lanes = slice(half * 128, half * 128 + 128)
        sums_ref[half, :56] = early[:56, lanes] + early[56:112, lanes]
        sums_ref[half, 56:72] = late[:16, lanes] + late[16:32, lanes]
        sums_ref[half, 72:80] = early[112:120, lanes]
    trial = [trial_ref[n] for n in range(6)]
    updated = stress_update(sums_ref, trial, resistance_ref)
    placed = nodal_parts(updated, weights_ref, gather_ref)
    for comp in range(3):
        top_ref[comp] = layer_forces(placed, comp, 1)
    top_copy().start()
    for component in range(6):
        stress_out[component] = updated[component]
    owned = [layer_forces(placed, comp, 0) for comp in range(3)]
    for p in range(len(CHUNKS)):

        @pl.loop(1, MEMBERS)
        def _(i, p=p):
            hop1(p, i).wait_send()

        @pl.loop(1, GROUPS)
        def _(i, p=p):
            hop2(p, i).wait_send()

    top_copy().wait()
    for comp in range(3):
        forces_out[comp] = owned[comp] + jnp.where(fe == 0, 0.0, under_ref[comp])


ORDER = {"start1": 0, "pass_on": 10, "take_in": 20}


def fused_step(
    grain_ids, euler_angles, owner, element, active, below, stress_old, resistance, quad_weights
):
    grads, forces = gradient_matrices()
    bricks = grain_ids.shape[1]
    blocks = bricks // 128
    hop = pltpu.VMEM((OCTANTS, WORDS // 128, DEVICES, 128), jnp.float32)
    vmem = pl.BlockSpec(memory_space=pltpu.VMEM)
    line = pltpu.VMEM((1, bricks), jnp.int32)
    layer = pltpu.VMEM(below.shape, jnp.float32)
    chunks = len(CHUNKS)
    return pl.pallas_call(
        exchange_kernel,
        out_shape=(
            jax.ShapeDtypeStruct(stress_old.shape, jnp.float32),
            jax.ShapeDtypeStruct(below.shape, jnp.float32),
        ),
        in_specs=[pl.BlockSpec(memory_space=pltpu.HBM)] * 11,
        out_specs=(vmem, vmem),
        scratch_shapes=[
            pltpu.VMEM(grain_ids.shape, jnp.int32),
            pltpu.VMEM(euler_angles.shape, jnp.float32),
            line,
            line,
            line,
            pltpu.VMEM(below.shape, jnp.float32),
            pltpu.VMEM((3, 32, 128), jnp.float32),
            pltpu.VMEM((64, 8, 128), jnp.int32),
            pltpu.VMEM((blocks, 9, 8, 128), jnp.float32),
            pltpu.VMEM((blocks // UNROLL, DEVICES, 256 * UNROLL), jnp.bfloat16),
            pltpu.VMEM((blocks, ENTRY_ROWS, 128), jnp.bfloat16),
            pltpu.VMEM((blocks, 48, 128), jnp.bfloat16),
            pltpu.VMEM((blocks, 48, 128), jnp.bfloat16),
            pltpu.VMEM((160, 128 * UNROLL), jnp.bfloat16),
            pltpu.VMEM((16, 160), jnp.bfloat16),
            pltpu.VMEM((2, UNROLL, 9, 8, 128), jnp.float32),
            pltpu.VMEM((WORDS, 256 * UNROLL), jnp.bfloat16),
            pltpu.VMEM((DEVICES, WORDS), jnp.float32),
            hop,
            hop,
            hop,
            hop,
            pltpu.VMEM((OCTANTS, WORDS, 128), jnp.float32),
            pltpu.VMEM((OCTANTS * CAP, 128), jnp.float32),
            pltpu.VMEM((CAP // 2, NODES, 256), jnp.bfloat16),
            pltpu.VMEM((2, 80, 128), jnp.float32),
            pltpu.VMEM(stress_old.shape, jnp.float32),
            pltpu.VMEM(resistance.shape, jnp.float32),
            pltpu.VMEM(quad_weights.shape, jnp.int32),
            pltpu.VMEM(grads.shape, jnp.float32),
            pltpu.VMEM(forces.shape, jnp.float32),
            layer,
            layer,
            layer,
            layer,
            pltpu.VMEM(stress_old.shape, jnp.float32),
            pltpu.SemaphoreType.DMA((5,)),
            pltpu.SemaphoreType.DMA((10,)),
            pltpu.SemaphoreType.DMA((chunks, MEMBERS)),
            pltpu.SemaphoreType.DMA((chunks, MEMBERS)),
            pltpu.SemaphoreType.DMA((chunks, GROUPS)),
            pltpu.SemaphoreType.DMA((chunks, GROUPS)),
            pltpu.SemaphoreType.DMA((4,)),
        ],
        compiler_params=pltpu.CompilerParams(
            vmem_limit_bytes=EXCHANGE_VMEM, collective_id=0, has_side_effects=True
        ),
        name="fused_step",
    )(
        grain_ids,
        euler_angles,
        owner.reshape(1, bricks),
        element.reshape(1, bricks),
        active.reshape(1, bricks),
        below,
        stress_old,
        resistance,
        quad_weights,
        jnp.asarray(grads),
        jnp.asarray(forces),
    )


def handing_kernel(stress_in, forces_in, stress_out, forces_out, sem):
    copies = [
        pltpu.make_async_copy(stress_in, stress_out, sem.at[0]),
        pltpu.make_async_copy(forces_in, forces_out, sem.at[1]),
    ]
    for copy in copies:
        copy.start()
    for copy in copies:
        copy.wait()


def handed_out(stress, forces):
    hbm = pl.BlockSpec(memory_space=pltpu.HBM)
    return pl.pallas_call(
        handing_kernel,
        out_shape=tuple(jax.ShapeDtypeStruct(x.shape, x.dtype) for x in (stress, forces)),
        in_specs=[hbm, hbm],
        out_specs=(hbm, hbm),
        scratch_shapes=[pltpu.SemaphoreType.DMA((2,))],
        name="handed_out",
    )(stress, forces)


def body(
    grain_ids,
    euler_angles,
    brick_active,
    brick_owner,
    brick_element,
    displacement,
    stress_old,
    resistance,
    quad_weights,
):
    return handed_out(
        *fused_step(
            grain_ids,
            euler_angles,
            brick_owner,
            brick_element,
            brick_active,
            displacement,
            stress_old,
            resistance,
            quad_weights,
        )
    )


def solution(mesh):
    placed = (
        P(None, ("ca", "fe")),
        P(),
        P(("ca", "fe")),
        P(("ca", "fe"), None),
        P(("ca", "fe")),
        P(None, ("ca", "fe"), None),
        P(None, None, ("ca", "fe")),
        P(None, None, ("ca", "fe")),
        P(None, ("ca", "fe")),
    )
    return jax.shard_map(
        body,
        mesh=mesh,
        in_specs=placed,
        out_specs=(P(None, None, ("ca", "fe")), P(None, ("ca", "fe"), None)),
        check_vma=False,
    )
```

```python
import collections
import functools
import math

import jax
import jax.numpy as jnp
import numpy as np
from jax import lax
from jax.experimental import pallas as pl
from jax.experimental.pallas import tpu as pltpu
from jax.sharding import PartitionSpec as P

GX = 15
NODES = 256
CAP = 40
GROUPS = 8
MEMBERS = 16
DEVICES = GROUPS * MEMBERS
FIXED_STEPS = float(2**20 - 1)

SLIP_PLANES = [
    [value / math.sqrt(3.0) for value in row]
    for row in [[1, 1, 1]] * 3 + [[-1, 1, 1]] * 3 + [[1, -1, 1]] * 3 + [[1, 1, -1]] * 3
]
SLIP_DIRECTIONS = [
    [value / math.sqrt(2.0) for value in row]
    for row in [
        [0, 1, -1],
        [1, 0, -1],
        [1, -1, 0],
        [0, 1, -1],
        [1, 0, 1],
        [1, 1, 0],
        [0, 1, 1],
        [1, 0, -1],
        [1, 1, 0],
        [0, 1, 1],
        [1, 0, 1],
        [1, -1, 0],
    ]
]
LAMBDA_ELASTIC = 1.5
SHEAR_MODULUS = 1.0
RATE_STEP = 0.1
FIXED_POINT = 65536.0
EXCHANGE_VMEM = 63 << 20


def shape_gradients():
    grad_table = np.zeros((8, 8, 3))
    point_offset = 1.0 / math.sqrt(3.0)
    for quadrature in range(8):
        natural = [
            (2 * (quadrature >> shift_bits & 1) - 1) * point_offset for shift_bits in (2, 1, 0)
        ]
        for corner in range(8):
            sign_list = [2 * (corner >> shift_bits & 1) - 1 for shift_bits in (2, 1, 0)]
            factors = [1.0 + sign_list[axis_id] * natural[axis_id] for axis_id in range(3)]
            for direction in range(3):
                others = 1.0
                for axis_id in range(3):
                    if axis_id != direction:
                        others = others * factors[axis_id]
                grad_table[quadrature, corner, direction] = (
                    2.0 * sign_list[direction] * others / 8.0
                )
    return grad_table


def gradient_matrices():
    table = shape_gradients()
    grads = np.zeros((72, 24), np.float32)
    forces = np.zeros((24, 72), np.float32)
    for comp in range(3):
        for direction in range(3):
            for q in range(8):
                for corner in range(8):
                    value = table[q, corner, direction]
                    grads[(comp * 3 + direction) * 8 + q, comp * 8 + corner] = value
                    forces[comp * 8 + corner, (comp * 3 + direction) * 8 + q] = value
    return grads, forces


def lane_pick(row, lanes):
    return jnp.take_along_axis(row, lanes, axis=1, mode="promise_in_bounds")


def merge_tree(stack, value, index, bits):
    level = 0
    while index & 1:
        value = jnp.where(bits[level], value, stack.pop())
        level += 1
        index >>= 1
    stack.append(value)


def build_table(euler_ref, angle_ref, table_ref):
    for angle in range(3):
        for row in range(32):
            angle_ref[angle, row : row + 1] = euler_ref[
                angle : angle + 1, row * 128 : row * 128 + 128
            ]
    half_sum = 0.5 * (angle_ref[0] + angle_ref[2])
    half_diff = 0.5 * (angle_ref[0] - angle_ref[2])
    half_mid = 0.5 * angle_ref[1]
    cos_mid, sin_mid = jnp.cos(half_mid), jnp.sin(half_mid)
    real = cos_mid * jnp.cos(half_sum)
    flip = jnp.where(real < 0.0, -1.0, 1.0)
    scale = flip * FIXED_STEPS / (1.0 + jnp.abs(real))
    first = jnp.round(sin_mid * jnp.cos(half_diff) * scale).astype(jnp.int32)
    second = jnp.round(sin_mid * jnp.sin(half_diff) * scale).astype(jnp.int32)
    third = jnp.round(cos_mid * jnp.sin(half_sum) * scale).astype(jnp.int32)
    word_a = jnp.left_shift(first, 11) | (jnp.right_shift(third, 10) & 0x7FF)
    word_b = jnp.left_shift(second, 11) | (third & 0x3FF)
    for row in range(32):
        table_ref[row] = jnp.broadcast_to(word_a[row : row + 1], (8, 128))
        table_ref[32 + row] = jnp.broadcast_to(word_b[row : row + 1], (8, 128))


def lookup(table_ref, ids, work):
    lanes = ids & 127
    bits = [(ids & (128 << level)) != 0 for level in range(5)]
    words = ([], [])
    for row in range(32):
        for n, stack in enumerate(words):
            merge_tree(stack, lane_pick(table_ref[n * 32 + row], lanes), row, bits)
        if work and row % 3 == 2:
            work.popleft()()
    return words[0][0], words[1][0]


def rotation_terms(word_a, word_b):
    a = jnp.right_shift(word_a, 11).astype(jnp.float32)
    b = jnp.right_shift(word_b, 11).astype(jnp.float32)
    c_bits = jnp.right_shift(jnp.left_shift(word_a, 21), 11) | (word_b & 0x3FF)
    c = c_bits.astype(jnp.float32)
    unit = 1.0 / FIXED_STEPS
    square = (a * a + b * b + c * c) * (unit * unit)
    inverse = 1.0 / (1.0 + square)
    inverse_square = inverse * inverse
    quad = inverse_square * (8.0 * unit * unit)
    lin = inverse_square * ((1.0 - square) * (4.0 * unit))
    qa, qb, qc = quad * a, quad * b, quad * c
    return [qa * a, qb * b, qc * c, qa * b, qa * c, qb * c, lin * a, lin * b, lin * c]


def octant_entries(terms, per_octant):
    xx, yy, zz, xy, xz, yz, wx, wy, wz = terms
    share = per_octant / 8.0
    return [
        share - (yy + zz),
        xy - wz,
        xz + wy,
        xy + wz,
        share - (xx + zz),
        yz - wx,
        xz - wy,
        yz + wx,
        share - (xx + yy),
    ]


NT_DIMS = (((1,), (1,)), ((), ()))
MESH = pl.DeviceIdType.MESH
OCTANTS = 8
CHUNKS = ((0, 2), (2, 4), (4, 5), (5, 6), (6, 7), (7, 8))
UNROLL = 4
WORDS = 384
ENTRY_ROWS = 8 * CAP
LABEL_ROWS = 368


def find_slots(owner_ref, element_ref, active_ref, owned_ref, rank_ref, single_ref, label_ref):
    span = 256
    device = lax.broadcasted_iota(jnp.int32, (DEVICES, span), 0)
    before = (
        lax.broadcasted_iota(jnp.int32, (span, span), 0)
        < lax.broadcasted_iota(jnp.int32, (span, span), 1)
    ).astype(jnp.bfloat16)
    ones = jnp.ones((span, span), jnp.bfloat16)
    slot = lax.broadcasted_iota(jnp.int32, (48, span), 0).astype(jnp.float32)
    carry = jnp.zeros((DEVICES, span), jnp.float32)
    for start in range(0, owner_ref.shape[1], span):
        owner = owner_ref[:, start : start + span]
        owned = device == ((owner & (MEMBERS - 1)) * GROUPS + jnp.right_shift(owner, 4))
        owned_half = owned.astype(jnp.bfloat16)
        earlier = carry + jnp.dot(owned_half, before, preferred_element_type=jnp.float32)
        carry = carry + jnp.dot(owned_half, ones, preferred_element_type=jnp.float32)
        rank = jnp.sum(jnp.where(owned, earlier, 0.0), axis=0, keepdims=True)
        label = jnp.where(
            active_ref[:, start : start + span] > 0, element_ref[:, start : start + span] + 1, 0
        ).astype(jnp.float32)
        single = jnp.where(slot == rank, 1.0, 0.0)
        labels = (single * label).astype(jnp.bfloat16)
        single = single.astype(jnp.bfloat16)
        eight = jnp.broadcast_to(rank, (8, span))
        for half in range(span // 128):
            lanes = slice(half * 128, half * 128 + 128)
            block = start // 128 + half
            place = (block % UNROLL) * 256
            owned_ref[block // UNROLL, :, place : place + 128] = owned_half[:, lanes]
            owned_ref[block // UNROLL, :, place + 128 : place + 256] = owned_half[:, lanes]
            single_ref[block] = single[:, lanes]
            label_ref[block] = labels[:, lanes]
            for pair in range(CAP // 2):
                both = [
                    jnp.where(eight[:, lanes] == float(2 * pair + n), 1.0, 0.0) for n in range(2)
                ]
                rank_ref[block, 16 * pair : 16 * pair + 16] = jnp.concatenate(
                    both, axis=0
                ).astype(jnp.bfloat16)


def halves(values):
    high = values.astype(jnp.bfloat16).astype(jnp.float32)
    out = []
    for part in (high, values - high):
        out.append(jnp.concatenate([part, part], axis=0).astype(jnp.bfloat16))
    return out


def split_three(values):
    high = values.astype(jnp.bfloat16)
    rest = values - high.astype(jnp.float32)
    mid = rest.astype(jnp.bfloat16)
    low = (rest - mid.astype(jnp.float32)).astype(jnp.bfloat16)
    return jnp.concatenate([high, mid, low], axis=0)


def joined_three(product):
    rows = product.shape[0] // 3
    return product[:rows] + product[rows : 2 * rows] + product[2 * rows :]


def element_places(elements):
    node = lax.broadcasted_iota(jnp.int32, (NODES, NODES), 0)
    lane = lax.broadcasted_iota(jnp.int32, (NODES, NODES), 1)
    base = lane
    for bound in range(GX, GX * GX, GX):
        base = base + jnp.where(lane >= bound, 1, 0)
    return ((node == base) & (lane < elements)).astype(jnp.bfloat16)


def trial_stress(below_ref, above_ref, stress_ref, grads_ref):
    elements = stress_ref.shape[2]
    to_element = element_places(elements)
    rows = []
    for comp in range(3):
        for corner in range(8):
            step_x, step_y, step_z = (corner >> 2 & 1, corner >> 1 & 1, corner & 1)
            source = above_ref if step_z else below_ref
            offset = step_y * (GX + 1) + step_x
            line = source[comp]
            rows.append(line if offset == 0 else pltpu.roll(line, NODES - offset, 1))
    corners = joined_three(
        jnp.dot(
            split_three(jnp.concatenate(rows, axis=0)),
            to_element,
            preferred_element_type=jnp.float32,
        )
    )
    gradients = jnp.dot(
        grads_ref[...],
        corners,
        precision=lax.Precision.HIGHEST,
        preferred_element_type=jnp.float32,
    )

    def grad(comp, direction):
        n = (comp * 3 + direction) * 8
        return gradients[n : n + 8, :elements]

    strain = [
        grad(0, 0),
        grad(1, 1),
        grad(2, 2),
        0.5 * (grad(1, 2) + grad(2, 1)),
        0.5 * (grad(0, 2) + grad(2, 0)),
        0.5 * (grad(0, 1) + grad(1, 0)),
    ]
    volume = strain[0] + strain[1] + strain[2]
    trial = []
    for component in range(6):
        change = 2.0 * SHEAR_MODULUS * strain[component]
        if component < 3:
            change = change + LAMBDA_ELASTIC * volume
        trial.append(stress_ref[component] + change)
    return trial


def stress_update(sums_ref, trial, resistance_ref):
    elements = resistance_ref.shape[2]
    weights = [1.0 / (8.0 * jnp.maximum(sums_ref[half, 72:73], 1.0)) for half in range(2)]
    frames = []
    for n in range(9):
        rows = pl.ds(n, OCTANTS, stride=8) if n < 8 else pl.ds(64, OCTANTS)
        parts = [sums_ref[half, rows, :] * weights[half] for half in range(2)]
        frames.append(jnp.concatenate(parts, axis=1)[:, :elements])

    def frame(i, j):
        return frames[i * 3 + j]

    def rotated(vector):
        out = []
        for i in range(3):
            terms = [float(vector[j]) * frame(i, j) for j in range(3) if vector[j] != 0.0]
            out.append(functools.reduce(lambda x, y: x + y, terms))
        return out

    normals = {tuple(vector): rotated(vector) for vector in SLIP_PLANES}
    correction = [jnp.zeros_like(trial[0]) for component in range(6)]
    for system in range(12):
        d = rotated(SLIP_DIRECTIONS[system])
        m = normals[tuple(SLIP_PLANES[system])]
        schmid = [
            d[0] * m[0],
            d[1] * m[1],
            d[2] * m[2],
            0.5 * (d[1] * m[2] + d[2] * m[1]),
            0.5 * (d[0] * m[2] + d[2] * m[0]),
            0.5 * (d[0] * m[1] + d[1] * m[0]),
        ]
        resolved = (
            trial[0] * schmid[0]
            + trial[1] * schmid[1]
            + trial[2] * schmid[2]
            + 2.0 * (trial[3] * schmid[3] + trial[4] * schmid[4] + trial[5] * schmid[5])
        )
        ratio = resolved / resistance_ref[system]
        slip_step = RATE_STEP * ratio * jnp.abs(ratio)
        correction = [
            correction[component] + slip_step * schmid[component] for component in range(6)
        ]
    updated = [
        trial[component] - 2.0 * SHEAR_MODULUS * correction[component] for component in range(6)
    ]
    return updated


def nodal_parts(updated, weights_ref, gather_ref):
    elements = weights_ref.shape[1]
    to_element = element_places(elements)
    scale = weights_ref[...].astype(jnp.float32) * (1.0 / (FIXED_POINT * 8.0))
    order = [0, 5, 4, 5, 1, 3, 4, 3, 2]
    pad = jnp.zeros((8, NODES - elements), jnp.float32)
    tensor = jnp.concatenate(
        [jnp.concatenate([updated[component] * scale, pad], axis=1) for component in order], axis=0
    )
    element_forces = jnp.dot(
        gather_ref[...],
        tensor,
        precision=lax.Precision.HIGHEST,
        preferred_element_type=jnp.float32,
    )
    placed = joined_three(
        lax.dot_general(
            split_three(element_forces), to_element, NT_DIMS, preferred_element_type=jnp.float32
        )
    )
    return placed


def layer_forces(placed, comp, step_z):
    line = jnp.zeros((1, NODES), jnp.float32)
    for corner in range(8):
        if (corner & 1) != step_z:
            continue
        offset = (corner >> 1 & 1) * (GX + 1) + (corner >> 2 & 1)
        part = placed[comp * 8 + corner : comp * 8 + corner + 1]
        line = line + (part if offset == 0 else pltpu.roll(part, offset, 1))
    return line


def exchange_kernel(
    ids_hbm,
    euler_hbm,
    owner_hbm,
    element_hbm,
    active_hbm,
    below_hbm,
    stress_hbm,
    resistance_hbm,
    weights_hbm,
    grads_hbm,
    gather_hbm,
    stress_out,
    forces_out,
    ids_ref,
    euler_ref,
    owner_ref,
    element_ref,
    active_ref,
    below_ref,
    angle_ref,
    table_ref,
    carry_ref,
    owned_ref,
    rank_ref,
    single_ref,
    label_ref,
    part_ref,
    pool_ref,
    stage_ref,
    wide_ref,
    acc_ref,
    out1_ref,
    in1_ref,
    out2_ref,
    in2_ref,
    got_ref,
    last_ref,
    hit_ref,
    sums_ref,
    stress_ref,
    resistance_ref,
    weights_ref,
    grads_ref,
    gather_ref,
    land_ref,
    above_ref,
    top_ref,
    under_ref,
    trial_ref,
    ids_sem,
    small_sem,
    send1_sem,
    recv1_sem,
    send2_sem,
    recv2_sem,
    layer_sem,
):
    ca, fe = lax.axis_index("ca"), lax.axis_index("fe")
    barrier = pltpu.get_barrier_semaphore()

    def member(i):
        return lax.rem(fe + i, MEMBERS)

    def group(i):
        return lax.rem(ca + i, GROUPS)

    row = lax.broadcasted_iota(jnp.int32, (8, 128), 0)
    cells = ids_hbm.shape[0]
    per_octant = cells // OCTANTS
    tiles = cells // 8
    blocks = ids_hbm.shape[1] // 128
    steps = blocks // UNROLL
    id_cuts = (0, 32, 56, 112, 168, 216)

    def ids_copy(n):
        rows = pl.ds(id_cuts[n], id_cuts[n + 1] - id_cuts[n])
        return pltpu.make_async_copy(ids_hbm.at[rows], ids_ref.at[rows], ids_sem.at[n])

    small = [
        pltpu.make_async_copy(source, target, small_sem.at[n])
        for n, (source, target) in enumerate(
            [
                (owner_hbm, owner_ref),
                (element_hbm, element_ref),
                (active_hbm, active_ref),
                (euler_hbm, euler_ref),
                (below_hbm, below_ref),
                (stress_hbm, stress_ref),
                (resistance_hbm, resistance_ref),
                (weights_hbm, weights_ref),
                (grads_hbm, grads_ref),
                (gather_hbm, gather_ref),
            ]
        )
    ]
    for copy in small[:5]:
        copy.start()
    for n in range(len(id_cuts) - 1):
        ids_copy(n).start()
    for copy in small[5:]:
        copy.start()

    @pl.loop(1, MEMBERS)
    def _(i):
        pl.semaphore_signal(barrier, inc=1, device_id=(ca, member(i)), device_id_type=MESH)

    @pl.loop(1, GROUPS)
    def _(i):
        pl.semaphore_signal(barrier, inc=1, device_id=(group(i), fe), device_id_type=MESH)

    def hop1(p, i):
        there = pl.ds(pl.multiple_of(member(i) * GROUPS, 8), GROUPS)
        here = pl.ds(pl.multiple_of(fe * GROUPS, 8), GROUPS)
        octants = pl.ds(CHUNKS[p][0], CHUNKS[p][1] - CHUNKS[p][0])
        return pltpu.make_async_remote_copy(
            src_ref=out1_ref.at[octants, :, there],
            dst_ref=in1_ref.at[octants, :, here],
            send_sem=send1_sem.at[p],
            recv_sem=recv1_sem.at[p],
            device_id=(ca, member(i)),
            device_id_type=MESH,
        )

    def hop2(p, i):
        there = pl.ds(pl.multiple_of(group(i) * MEMBERS, 8), MEMBERS)
        here = pl.ds(pl.multiple_of(ca * MEMBERS, 8), MEMBERS)
        octants = pl.ds(CHUNKS[p][0], CHUNKS[p][1] - CHUNKS[p][0])
        return pltpu.make_async_remote_copy(
            src_ref=out2_ref.at[octants, :, there],
            dst_ref=in2_ref.at[octants, :, here],
            send_sem=send2_sem.at[p],
            recv_sem=recv2_sem.at[p],
            device_id=(group(i), fe),
            device_id_type=MESH,
        )

    def all1(p):
        octants = pl.ds(CHUNKS[p][0], CHUNKS[p][1] - CHUNKS[p][0])
        rows = pl.ds(0, DEVICES - GROUPS)
        return pltpu.make_async_remote_copy(
            src_ref=out1_ref.at[octants, :, rows],
            dst_ref=in1_ref.at[octants, :, rows],
            send_sem=send1_sem.at[p],
            recv_sem=recv1_sem.at[p],
            device_id=(ca, member(1)),
            device_id_type=MESH,
        )

    def all2(p):
        octants = pl.ds(CHUNKS[p][0], CHUNKS[p][1] - CHUNKS[p][0])
        rows = pl.ds(0, DEVICES - MEMBERS)
        return pltpu.make_async_remote_copy(
            src_ref=out2_ref.at[octants, :, rows],
            dst_ref=in2_ref.at[octants, :, rows],
            send_sem=send2_sem.at[p],
            recv_sem=recv2_sem.at[p],
            device_id=(group(1), fe),
            device_id_type=MESH,
        )

    def layer_copy():
        return pltpu.make_async_remote_copy(
            src_ref=below_ref,
            dst_ref=land_ref,
            send_sem=layer_sem.at[0],
            recv_sem=layer_sem.at[1],
            device_id=(ca, lax.rem(fe + MEMBERS - 1, MEMBERS)),
            device_id_type=MESH,
        )

    def top_copy():
        return pltpu.make_async_remote_copy(
            src_ref=top_ref,
            dst_ref=under_ref,
            send_sem=layer_sem.at[2],
            recv_sem=layer_sem.at[3],
            device_id=(ca, member(1)),
            device_id_type=MESH,
        )

    def start1(p):
        if p == 0:
            pl.semaphore_wait(barrier, MEMBERS + GROUPS - 2)
            layer_copy().start()

        for i in range(1, MEMBERS):
            hop1(p, i).start()

        here = pl.ds(pl.multiple_of(fe * GROUPS, 8), GROUPS)
        for q in range(*CHUNKS[p]):
            in1_ref[q, :, here] = out1_ref[q, :, here]

    def pass_on(p):
        all1(p).wait_recv()

        for q in range(*CHUNKS[p]):
            for c in range(WORDS // 128):
                for g in range(GROUPS):
                    out2_ref[q, c, g * MEMBERS : g * MEMBERS + MEMBERS] = in1_ref[
                        q, c, pl.ds(g, MEMBERS, stride=GROUPS), :
                    ]

        for i in range(1, GROUPS):
            hop2(p, i).start()

        here = pl.ds(pl.multiple_of(ca * MEMBERS, 8), MEMBERS)
        for q in range(*CHUNKS[p]):
            in2_ref[q, :, here] = out2_ref[q, :, here]

    def take_in(p):
        all2(p).wait_recv()

        for q in range(*CHUNKS[p]):
            for c in range(WORDS // 128):
                flipped = in2_ref[q, c].T
                got_ref[q, c * 128 : c * 128 + 128] = flipped
                if c == 2:
                    last_ref[pl.ds(q, CAP, stride=OCTANTS), :] = flipped[
                        ENTRY_ROWS - 256 : ENTRY_ROWS - 256 + CAP
                    ]

    part_ref[...] = jnp.zeros(part_ref.shape, jnp.bfloat16)
    target = jnp.minimum(lax.broadcasted_iota(jnp.int32, (16, 160), 0), 8)
    source = lax.broadcasted_iota(jnp.int32, (16, 160), 1)
    source = jnp.right_shift(jnp.where(source >= 80, source - 80, source), 3)
    pool_ref[...] = jnp.where(target == source, 1.0, 0.0).astype(jnp.bfloat16)
    wide_ref[...] = jnp.zeros(wide_ref.shape, jnp.bfloat16)
    acc_ref[...] = jnp.zeros(acc_ref.shape, jnp.float32)
    for copy in small[:5]:
        copy.wait()
    build_table(euler_ref, angle_ref, table_ref)
    find_slots(owner_ref, element_ref, active_ref, owned_ref, rank_ref, single_ref, label_ref)

    def keep_parts(u, entries):
        stacked = jnp.concatenate(entries + [jnp.zeros((8, 128), jnp.float32)], axis=0)
        high = stacked.astype(jnp.bfloat16)
        lanes = slice(u * 128, u * 128 + 128)
        part_ref[:80, lanes] = high
        part_ref[80:, lanes] = (stacked - high.astype(jnp.float32)).astype(jnp.bfloat16)

    def totals(out):
        out["sum"] = jnp.dot(pool_ref[...], part_ref[...], preferred_element_type=jnp.float32)

    def spread(block, u, q, total):
        parts = {}

        def split():
            columns = slice(u * 128, u * 128 + 128)
            parts["main"] = halves(total["sum"][:8, columns])
            parts["single"] = halves(total["sum"][8:, columns])

        def main(n, first):
            lanes = slice(u * 256 + n * 128, u * 256 + n * 128 + 128)
            for pair in range(first, first + 5):
                rows = slice(16 * pair, 16 * pair + 16)
                wide_ref[rows, lanes] = rank_ref[block, rows] * parts["main"][n]

        def single(n):
            lanes = slice(u * 256 + n * 128, u * 256 + n * 128 + 128)
            for part in range(3):
                rows = slice(16 * part, 16 * part + 16)
                target = slice(ENTRY_ROWS + 16 * part, ENTRY_ROWS + 16 * part + 16)
                wide_ref[target, lanes] = single_ref[block, rows] * parts["single"][n]
            if n == 0 and not (isinstance(q, int) and q >= 3):
                rows = pl.ds(pl.multiple_of(16 * q, 16), 16)
                wide_ref[LABEL_ROWS:, u * 256 : u * 256 + 128] = label_ref[block, rows]

        yield split
        for n in range(2):
            for first in range(0, CAP // 2, 5):
                yield functools.partial(main, n, first)
            yield functools.partial(single, n)

    def place(step):
        acc_ref[...] += lax.dot_general(
            owned_ref[step], wide_ref[...], NT_DIMS, preferred_element_type=jnp.float32
        )

    def finish(q):
        for c in range(WORDS // 128):
            out1_ref[q, c] = acc_ref[:, c * 128 : c * 128 + 128]
        acc_ref[...] = jnp.zeros(acc_ref.shape, jnp.float32)

    todo = {}
    for action, times in (
        (start1, ((2, 0), (4, 0), (5, 0), (6, 0), (7, 0), (8, 0))),
        (pass_on, ((3, 1), (5, 1), (6, 0), (7, 0), (7, 3), (8, 0))),
        (take_in, ((4, 3), (6, 3), (7, 3), (8, 0), (8, 0), (8, 0))),
    ):
        for p, time in enumerate(times):
            todo.setdefault(time, []).append((action, p))
    arrived = 0

    for q in range(OCTANTS):
        first = (q * per_octant) // 8
        stop = -(-((q + 1) * per_octant) // 8)
        fresh = first if first * 8 == q * per_octant else first + 1
        while id_cuts[arrived] < stop * 8:
            ids_copy(arrived).wait()
            arrived += 1

        @pl.loop(0, steps)
        def _(step, q=q, fresh=fresh, stop=stop):
            before = lax.rem(step + steps - 1, steps)
            label_octant = jnp.where(step == 0, max(q - 1, 0), min(q, 2)) if q < 4 else q
            if q > 0:
                for u in range(UNROLL):
                    stage_ref[0, u] = carry_ref[step * UNROLL + u]
            total = {}
            work = collections.deque()
            totals(total)
            for u in range(UNROLL):
                work.extend(spread(before * UNROLL + u, u, label_octant, total))
            work.append(functools.partial(place, before))
            state = {}

            def decode(u, t, words):
                terms = rotation_terms(*words)
                split = (q + 1) * per_octant - 8 * t
                if split < 8:
                    inside = row < split
                    for n in range(9):
                        stage_ref[1, u, n] = jnp.where(inside, 0.0, terms[n])
                    terms = [jnp.where(inside, v, 0.0) for v in terms]
                if t == fresh:
                    if q > 0:
                        terms = [stage_ref[0, u, n] + v for n, v in enumerate(terms)]
                else:
                    terms = [s + v for s, v in zip(state[u], terms)]
                state[u] = terms
                if t == stop - 1:
                    keep_parts(u, octant_entries(terms, per_octant))

            for u in range(UNROLL):
                columns = pl.ds(pl.multiple_of((step * UNROLL + u) * 128, 128), 128)
                for t in range(fresh, stop):
                    words = lookup(table_ref, ids_ref[8 * t : 8 * t + 8, columns], work)
                    work.appendleft(functools.partial(decode, u, t, words))
            while work:
                work.popleft()()

            if q < OCTANTS - 1:
                for u in range(UNROLL):
                    carry_ref[step * UNROLL + u] = stage_ref[1, u]

            @pl.when(step == 0)
            def _():
                if q > 0:
                    finish(q - 1)
                else:
                    acc_ref[...] = jnp.zeros(acc_ref.shape, jnp.float32)

            for late in range(4):
                if (q, late) in todo:

                    @pl.when(step == late * steps // 4)
                    def _(late=late):
                        for action, p in todo[q, late]:
                            action(p)

    total = {}
    totals(total)
    for u in range(UNROLL):
        for part in spread((steps - 1) * UNROLL + u, u, OCTANTS - 1, total):
            part()
    place(steps - 1)
    finish(OCTANTS - 1)
    rest = sorted(todo[OCTANTS, 0], key=lambda item: ORDER[item[0].__name__] + item[1])
    for action, p in rest[:1]:
        action(p)
    for copy in small[5:]:
        copy.wait()
    layer_copy().wait()
    above_ref[...] = jnp.where(fe == MEMBERS - 1, 0.0, land_ref[...])
    for n, trial in enumerate(trial_stress(below_ref, above_ref, stress_ref, grads_ref)):
        trial_ref[n] = trial
    for action, p in rest[1:-1]:
        action(p)

    ones = jnp.ones((16, 128), jnp.bfloat16)

    def owner_sums(octants, last, rows):
        sums = jnp.zeros((rows, NODES), jnp.float32)
        for r in range(0, CAP, 2):
            left = []
            for n in (r, r + 1):
                values = [got_ref[q, 8 * n : 8 * n + 8] for q in octants]
                if last:
                    values.append(last_ref[8 * n : 8 * n + 8])
                values = jnp.concatenate(values, axis=0)
                high = values.astype(jnp.bfloat16).astype(jnp.float32)
                both = jnp.concatenate([high, values - high], axis=0).astype(jnp.bfloat16)
                left.append(both if last else jnp.concatenate([both, ones], axis=0))
            sums = sums + lax.dot_general(
                jnp.concatenate(left, axis=1),
                hit_ref[r // 2],
                NT_DIMS,
                preferred_element_type=jnp.float32,
            )
        return sums

    label_value = lax.broadcasted_iota(jnp.int32, (NODES, 128), 0).astype(jnp.float32) + 1.0
    for n in range(CAP):
        line = LABEL_ROWS + n % 16
        hit = label_value == got_ref[n // 16, line : line + 1, :]
        lanes = slice((n & 1) * 128, (n & 1) * 128 + 128)
        hit_ref[n // 2, :, lanes] = hit.astype(jnp.bfloat16)
    early = owner_sums(range(OCTANTS - 1), False, 128)
    action, p = rest[-1]
    action(p)
    late = owner_sums([OCTANTS - 1], True, 32)
    for half in range(2):
        lanes = slice(half * 128, half * 128 + 128)
        sums_ref[half, :56] = early[:56, lanes] + early[56:112, lanes]
        sums_ref[half, 56:72] = late[:16, lanes] + late[16:32, lanes]
        sums_ref[half, 72:80] = early[112:120, lanes]
    trial = [trial_ref[n] for n in range(6)]
    updated = stress_update(sums_ref, trial, resistance_ref)
    placed = nodal_parts(updated, weights_ref, gather_ref)
    for comp in range(3):
        top_ref[comp] = layer_forces(placed, comp, 1)
    top_copy().start()
    for component in range(6):
        stress_out[component] = updated[component]
    owned = [layer_forces(placed, comp, 0) for comp in range(3)]
    for p in range(len(CHUNKS)):
        all1(p).wait_send()
        all2(p).wait_send()

    top_copy().wait()
    for comp in range(3):
        forces_out[comp] = owned[comp] + jnp.where(fe == 0, 0.0, under_ref[comp])


ORDER = {"start1": 0, "pass_on": 10, "take_in": 20}


def fused_step(
    grain_ids, euler_angles, owner, element, active, below, stress_old, resistance, quad_weights
):
    grads, forces = gradient_matrices()
    bricks = grain_ids.shape[1]
    blocks = bricks // 128
    hop = pltpu.VMEM((OCTANTS, WORDS // 128, DEVICES, 128), jnp.float32)
    vmem = pl.BlockSpec(memory_space=pltpu.VMEM)
    line = pltpu.VMEM((1, bricks), jnp.int32)
    layer = pltpu.VMEM(below.shape, jnp.float32)
    chunks = len(CHUNKS)
    return pl.pallas_call(
        exchange_kernel,
        out_shape=(
            jax.ShapeDtypeStruct(stress_old.shape, jnp.float32),
            jax.ShapeDtypeStruct(below.shape, jnp.float32),
        ),
        in_specs=[pl.BlockSpec(memory_space=pltpu.HBM)] * 11,
        out_specs=(vmem, vmem),
        scratch_shapes=[
            pltpu.VMEM(grain_ids.shape, jnp.int32),
            pltpu.VMEM(euler_angles.shape, jnp.float32),
            line,
            line,
            line,
            pltpu.VMEM(below.shape, jnp.float32),
            pltpu.VMEM((3, 32, 128), jnp.float32),
            pltpu.VMEM((64, 8, 128), jnp.int32),
            pltpu.VMEM((blocks, 9, 8, 128), jnp.float32),
            pltpu.VMEM((blocks // UNROLL, DEVICES, 256 * UNROLL), jnp.bfloat16),
            pltpu.VMEM((blocks, ENTRY_ROWS, 128), jnp.bfloat16),
            pltpu.VMEM((blocks, 48, 128), jnp.bfloat16),
            pltpu.VMEM((blocks, 48, 128), jnp.bfloat16),
            pltpu.VMEM((160, 128 * UNROLL), jnp.bfloat16),
            pltpu.VMEM((16, 160), jnp.bfloat16),
            pltpu.VMEM((2, UNROLL, 9, 8, 128), jnp.float32),
            pltpu.VMEM((WORDS, 256 * UNROLL), jnp.bfloat16),
            pltpu.VMEM((DEVICES, WORDS), jnp.float32),
            hop,
            hop,
            hop,
            hop,
            pltpu.VMEM((OCTANTS, WORDS, 128), jnp.float32),
            pltpu.VMEM((OCTANTS * CAP, 128), jnp.float32),
            pltpu.VMEM((CAP // 2, NODES, 256), jnp.bfloat16),
            pltpu.VMEM((2, 80, 128), jnp.float32),
            pltpu.VMEM(stress_old.shape, jnp.float32),
            pltpu.VMEM(resistance.shape, jnp.float32),
            pltpu.VMEM(quad_weights.shape, jnp.int32),
            pltpu.VMEM(grads.shape, jnp.float32),
            pltpu.VMEM(forces.shape, jnp.float32),
            layer,
            layer,
            layer,
            layer,
            pltpu.VMEM(stress_old.shape, jnp.float32),
            pltpu.SemaphoreType.DMA((5,)),
            pltpu.SemaphoreType.DMA((10,)),
            pltpu.SemaphoreType.DMA((chunks,)),
            pltpu.SemaphoreType.DMA((chunks,)),
            pltpu.SemaphoreType.DMA((chunks,)),
            pltpu.SemaphoreType.DMA((chunks,)),
            pltpu.SemaphoreType.DMA((4,)),
        ],
        compiler_params=pltpu.CompilerParams(
            vmem_limit_bytes=EXCHANGE_VMEM, collective_id=0, has_side_effects=True
        ),
        name="fused_step",
    )(
        grain_ids,
        euler_angles,
        owner.reshape(1, bricks),
        element.reshape(1, bricks),
        active.reshape(1, bricks),
        below,
        stress_old,
        resistance,
        quad_weights,
        jnp.asarray(grads),
        jnp.asarray(forces),
    )


def handing_kernel(stress_in, forces_in, stress_out, forces_out, stress_ref, forces_ref, sem):
    for hop, pairs in enumerate(
        (
            ((stress_in, stress_ref), (forces_in, forces_ref)),
            ((stress_ref, stress_out), (forces_ref, forces_out)),
        )
    ):
        copies = [
            pltpu.make_async_copy(source, target, sem.at[hop, n])
            for n, (source, target) in enumerate(pairs)
        ]
        for copy in copies:
            copy.start()
        for copy in copies:
            copy.wait()


def handed_out(stress, forces):
    hbm = pl.BlockSpec(memory_space=pltpu.HBM)
    return pl.pallas_call(
        handing_kernel,
        out_shape=tuple(jax.ShapeDtypeStruct(x.shape, x.dtype) for x in (stress, forces)),
        in_specs=[hbm, hbm],
        out_specs=(hbm, hbm),
        scratch_shapes=[
            pltpu.VMEM(stress.shape, stress.dtype),
            pltpu.VMEM(forces.shape, forces.dtype),
            pltpu.SemaphoreType.DMA((2, 2)),
        ],
        name="handed_out",
    )(stress, forces)


def body(
    grain_ids,
    euler_angles,
    brick_active,
    brick_owner,
    brick_element,
    displacement,
    stress_old,
    resistance,
    quad_weights,
):
    return handed_out(
        *fused_step(
            grain_ids,
            euler_angles,
            brick_owner,
            brick_element,
            brick_active,
            displacement,
            stress_old,
            resistance,
            quad_weights,
        )
    )


def solution(mesh):
    placed = (
        P(None, ("ca", "fe")),
        P(),
        P(("ca", "fe")),
        P(("ca", "fe"), None),
        P(("ca", "fe")),
        P(None, ("ca", "fe"), None),
        P(None, None, ("ca", "fe")),
        P(None, None, ("ca", "fe")),
        P(None, ("ca", "fe")),
    )
    return jax.shard_map(
        body,
        mesh=mesh,
        in_specs=placed,
        out_specs=(P(None, None, ("ca", "fe")), P(None, ("ca", "fe"), None)),
        check_vma=False,
    )
```

```python
import collections
import functools
import math

import jax
import jax.numpy as jnp
import numpy as np
from jax import lax
from jax.experimental import pallas as pl
from jax.experimental.pallas import tpu as pltpu
from jax.sharding import PartitionSpec as P

GX = 15
NODES = 256
CAP = 40
GROUPS = 8
MEMBERS = 16
DEVICES = GROUPS * MEMBERS
FIXED_STEPS = float(2**20 - 1)

SLIP_PLANES = [
    [value / math.sqrt(3.0) for value in row]
    for row in [[1, 1, 1]] * 3 + [[-1, 1, 1]] * 3 + [[1, -1, 1]] * 3 + [[1, 1, -1]] * 3
]
SLIP_DIRECTIONS = [
    [value / math.sqrt(2.0) for value in row]
    for row in [
        [0, 1, -1],
        [1, 0, -1],
        [1, -1, 0],
        [0, 1, -1],
        [1, 0, 1],
        [1, 1, 0],
        [0, 1, 1],
        [1, 0, -1],
        [1, 1, 0],
        [0, 1, 1],
        [1, 0, 1],
        [1, -1, 0],
    ]
]
LAMBDA_ELASTIC = 1.5
SHEAR_MODULUS = 1.0
RATE_STEP = 0.1
FIXED_POINT = 65536.0
EXCHANGE_VMEM = 63 << 20


def shape_gradients():
    grad_table = np.zeros((8, 8, 3))
    point_offset = 1.0 / math.sqrt(3.0)
    for quadrature in range(8):
        natural = [
            (2 * (quadrature >> shift_bits & 1) - 1) * point_offset for shift_bits in (2, 1, 0)
        ]
        for corner in range(8):
            sign_list = [2 * (corner >> shift_bits & 1) - 1 for shift_bits in (2, 1, 0)]
            factors = [1.0 + sign_list[axis_id] * natural[axis_id] for axis_id in range(3)]
            for direction in range(3):
                others = 1.0
                for axis_id in range(3):
                    if axis_id != direction:
                        others = others * factors[axis_id]
                grad_table[quadrature, corner, direction] = (
                    2.0 * sign_list[direction] * others / 8.0
                )
    return grad_table


def gradient_matrices():
    table = shape_gradients()
    grads = np.zeros((72, 24), np.float32)
    forces = np.zeros((24, 72), np.float32)
    for comp in range(3):
        for direction in range(3):
            for q in range(8):
                for corner in range(8):
                    value = table[q, corner, direction]
                    grads[(comp * 3 + direction) * 8 + q, comp * 8 + corner] = value
                    forces[comp * 8 + corner, (comp * 3 + direction) * 8 + q] = value
    return grads, forces


def lane_pick(row, lanes):
    return jnp.take_along_axis(row, lanes, axis=1, mode="promise_in_bounds")


def merge_tree(stack, value, index, bits):
    level = 0
    while index & 1:
        value = jnp.where(bits[level], value, stack.pop())
        level += 1
        index >>= 1
    stack.append(value)


def build_table(euler_ref, angle_ref, table_ref):
    for angle in range(3):
        for row in range(32):
            angle_ref[angle, row : row + 1] = euler_ref[
                angle : angle + 1, row * 128 : row * 128 + 128
            ]
    half_sum = 0.5 * (angle_ref[0] + angle_ref[2])
    half_diff = 0.5 * (angle_ref[0] - angle_ref[2])
    half_mid = 0.5 * angle_ref[1]
    cos_mid, sin_mid = jnp.cos(half_mid), jnp.sin(half_mid)
    real = cos_mid * jnp.cos(half_sum)
    flip = jnp.where(real < 0.0, -1.0, 1.0)
    scale = flip * FIXED_STEPS / (1.0 + jnp.abs(real))
    first = jnp.round(sin_mid * jnp.cos(half_diff) * scale).astype(jnp.int32)
    second = jnp.round(sin_mid * jnp.sin(half_diff) * scale).astype(jnp.int32)
    third = jnp.round(cos_mid * jnp.sin(half_sum) * scale).astype(jnp.int32)
    word_a = jnp.left_shift(first, 11) | (jnp.right_shift(third, 10) & 0x7FF)
    word_b = jnp.left_shift(second, 11) | (third & 0x3FF)
    for row in range(32):
        table_ref[row] = jnp.broadcast_to(word_a[row : row + 1], (8, 128))
        table_ref[32 + row] = jnp.broadcast_to(word_b[row : row + 1], (8, 128))


def lookup(table_ref, ids, work):
    lanes = ids & 127
    bits = [(ids & (128 << level)) != 0 for level in range(5)]
    words = ([], [])
    for n, stack in enumerate(words):
        for row in range(32):
            merge_tree(stack, lane_pick(table_ref[n * 32 + row], lanes), row, bits)
            if work and row % 5 == 4:
                work.popleft()()
    return words[0][0], words[1][0]


def rotation_terms(word_a, word_b):
    a = jnp.right_shift(word_a, 11).astype(jnp.float32)
    b = jnp.right_shift(word_b, 11).astype(jnp.float32)
    c_bits = jnp.right_shift(jnp.left_shift(word_a, 21), 11) | (word_b & 0x3FF)
    c = c_bits.astype(jnp.float32)
    unit = 1.0 / FIXED_STEPS
    square = (a * a + b * b + c * c) * (unit * unit)
    inverse = 1.0 / (1.0 + square)
    inverse_square = inverse * inverse
    quad = inverse_square * (8.0 * unit * unit)
    lin = inverse_square * ((1.0 - square) * (4.0 * unit))
    qa, qb, qc = quad * a, quad * b, quad * c
    return [qa * a, qb * b, qc * c, qa * b, qa * c, qb * c, lin * a, lin * b, lin * c]


def octant_entries(terms, per_octant):
    xx, yy, zz, xy, xz, yz, wx, wy, wz = terms
    share = per_octant / 8.0
    return [
        share - (yy + zz),
        xy - wz,
        xz + wy,
        xy + wz,
        share - (xx + zz),
        yz - wx,
        xz - wy,
        yz + wx,
        share - (xx + yy),
    ]


NT_DIMS = (((1,), (1,)), ((), ()))
MESH = pl.DeviceIdType.MESH
OCTANTS = 8
CHUNKS = ((0, 2), (2, 4), (4, 5), (5, 6), (6, 7), (7, 8))
UNROLL = 4
WORDS = 384
ENTRY_ROWS = 8 * CAP
LABEL_ROWS = 368


def find_slots(owner_ref, element_ref, active_ref, owned_ref, rank_ref, single_ref, label_ref):
    span = 256
    device = lax.broadcasted_iota(jnp.int32, (DEVICES, span), 0)
    before = (
        lax.broadcasted_iota(jnp.int32, (span, span), 0)
        < lax.broadcasted_iota(jnp.int32, (span, span), 1)
    ).astype(jnp.bfloat16)
    ones = jnp.ones((span, span), jnp.bfloat16)
    slot = lax.broadcasted_iota(jnp.int32, (48, span), 0).astype(jnp.float32)
    carry = jnp.zeros((DEVICES, span), jnp.float32)
    for start in range(0, owner_ref.shape[1], span):
        owner = owner_ref[:, start : start + span]
        owned = device == ((owner & (MEMBERS - 1)) * GROUPS + jnp.right_shift(owner, 4))
        owned_half = owned.astype(jnp.bfloat16)
        earlier = carry + jnp.dot(owned_half, before, preferred_element_type=jnp.float32)
        carry = carry + jnp.dot(owned_half, ones, preferred_element_type=jnp.float32)
        rank = jnp.sum(jnp.where(owned, earlier, 0.0), axis=0, keepdims=True)
        label = jnp.where(
            active_ref[:, start : start + span] > 0, element_ref[:, start : start + span] + 1, 0
        ).astype(jnp.float32)
        single = jnp.where(slot == rank, 1.0, 0.0)
        labels = (single * label).astype(jnp.bfloat16)
        single = single.astype(jnp.bfloat16)
        eight = jnp.broadcast_to(rank, (8, span))
        for half in range(span // 128):
            lanes = slice(half * 128, half * 128 + 128)
            block = start // 128 + half
            place = (block % UNROLL) * 256
            owned_ref[block // UNROLL, :, place : place + 128] = owned_half[:, lanes]
            owned_ref[block // UNROLL, :, place + 128 : place + 256] = owned_half[:, lanes]
            single_ref[block] = single[:, lanes]
            label_ref[block] = labels[:, lanes]
            for pair in range(CAP // 2):
                both = [
                    jnp.where(eight[:, lanes] == float(2 * pair + n), 1.0, 0.0) for n in range(2)
                ]
                rank_ref[block, 16 * pair : 16 * pair + 16] = jnp.concatenate(
                    both, axis=0
                ).astype(jnp.bfloat16)


def halves(values):
    high = values.astype(jnp.bfloat16).astype(jnp.float32)
    out = []
    for part in (high, values - high):
        out.append(jnp.concatenate([part, part], axis=0).astype(jnp.bfloat16))
    return out


def split_three(values):
    high = values.astype(jnp.bfloat16)
    rest = values - high.astype(jnp.float32)
    mid = rest.astype(jnp.bfloat16)
    low = (rest - mid.astype(jnp.float32)).astype(jnp.bfloat16)
    return jnp.concatenate([high, mid, low], axis=0)


def joined_three(product):
    rows = product.shape[0] // 3
    return product[:rows] + product[rows : 2 * rows] + product[2 * rows :]


def element_places(elements):
    node = lax.broadcasted_iota(jnp.int32, (NODES, NODES), 0)
    lane = lax.broadcasted_iota(jnp.int32, (NODES, NODES), 1)
    base = lane
    for bound in range(GX, GX * GX, GX):
        base = base + jnp.where(lane >= bound, 1, 0)
    return ((node == base) & (lane < elements)).astype(jnp.bfloat16)


def trial_stress(below_ref, above_ref, stress_ref, grads_ref):
    elements = stress_ref.shape[2]
    to_element = element_places(elements)
    rows = []
    for comp in range(3):
        for corner in range(8):
            step_x, step_y, step_z = (corner >> 2 & 1, corner >> 1 & 1, corner & 1)
            source = above_ref if step_z else below_ref
            offset = step_y * (GX + 1) + step_x
            line = source[comp]
            rows.append(line if offset == 0 else pltpu.roll(line, NODES - offset, 1))
    corners = joined_three(
        jnp.dot(
            split_three(jnp.concatenate(rows, axis=0)),
            to_element,
            preferred_element_type=jnp.float32,
        )
    )
    gradients = jnp.dot(
        grads_ref[...],
        corners,
        precision=lax.Precision.HIGHEST,
        preferred_element_type=jnp.float32,
    )

    def grad(comp, direction):
        n = (comp * 3 + direction) * 8
        return gradients[n : n + 8, :elements]

    strain = [
        grad(0, 0),
        grad(1, 1),
        grad(2, 2),
        0.5 * (grad(1, 2) + grad(2, 1)),
        0.5 * (grad(0, 2) + grad(2, 0)),
        0.5 * (grad(0, 1) + grad(1, 0)),
    ]
    volume = strain[0] + strain[1] + strain[2]
    trial = []
    for component in range(6):
        change = 2.0 * SHEAR_MODULUS * strain[component]
        if component < 3:
            change = change + LAMBDA_ELASTIC * volume
        trial.append(stress_ref[component] + change)
    return trial


def stress_update(sums_ref, trial, resistance_ref):
    elements = resistance_ref.shape[2]
    weights = [1.0 / (8.0 * jnp.maximum(sums_ref[half, 72:73], 1.0)) for half in range(2)]
    frames = []
    for n in range(9):
        rows = pl.ds(n, OCTANTS, stride=8) if n < 8 else pl.ds(64, OCTANTS)
        parts = [sums_ref[half, rows, :] * weights[half] for half in range(2)]
        frames.append(jnp.concatenate(parts, axis=1)[:, :elements])

    def frame(i, j):
        return frames[i * 3 + j]

    def rotated(vector):
        out = []
        for i in range(3):
            terms = [float(vector[j]) * frame(i, j) for j in range(3) if vector[j] != 0.0]
            out.append(functools.reduce(lambda x, y: x + y, terms))
        return out

    normals = {tuple(vector): rotated(vector) for vector in SLIP_PLANES}
    correction = [jnp.zeros_like(trial[0]) for component in range(6)]
    for system in range(12):
        d = rotated(SLIP_DIRECTIONS[system])
        m = normals[tuple(SLIP_PLANES[system])]
        schmid = [
            d[0] * m[0],
            d[1] * m[1],
            d[2] * m[2],
            0.5 * (d[1] * m[2] + d[2] * m[1]),
            0.5 * (d[0] * m[2] + d[2] * m[0]),
            0.5 * (d[0] * m[1] + d[1] * m[0]),
        ]
        resolved = (
            trial[0] * schmid[0]
            + trial[1] * schmid[1]
            + trial[2] * schmid[2]
            + 2.0 * (trial[3] * schmid[3] + trial[4] * schmid[4] + trial[5] * schmid[5])
        )
        ratio = resolved / resistance_ref[system]
        slip_step = RATE_STEP * ratio * jnp.abs(ratio)
        correction = [
            correction[component] + slip_step * schmid[component] for component in range(6)
        ]
    updated = [
        trial[component] - 2.0 * SHEAR_MODULUS * correction[component] for component in range(6)
    ]
    return updated


def nodal_parts(updated, weights_ref, gather_ref):
    elements = weights_ref.shape[1]
    to_element = element_places(elements)
    scale = weights_ref[...].astype(jnp.float32) * (1.0 / (FIXED_POINT * 8.0))
    order = [0, 5, 4, 5, 1, 3, 4, 3, 2]
    pad = jnp.zeros((8, NODES - elements), jnp.float32)
    tensor = jnp.concatenate(
        [jnp.concatenate([updated[component] * scale, pad], axis=1) for component in order], axis=0
    )
    element_forces = jnp.dot(
        gather_ref[...],
        tensor,
        precision=lax.Precision.HIGHEST,
        preferred_element_type=jnp.float32,
    )
    placed = joined_three(
        lax.dot_general(
            split_three(element_forces), to_element, NT_DIMS, preferred_element_type=jnp.float32
        )
    )
    return placed


def layer_forces(placed, comp, step_z):
    line = jnp.zeros((1, NODES), jnp.float32)
    for corner in range(8):
        if (corner & 1) != step_z:
            continue
        offset = (corner >> 1 & 1) * (GX + 1) + (corner >> 2 & 1)
        part = placed[comp * 8 + corner : comp * 8 + corner + 1]
        line = line + (part if offset == 0 else pltpu.roll(part, offset, 1))
    return line


def exchange_kernel(
    ids_hbm,
    euler_hbm,
    owner_hbm,
    element_hbm,
    active_hbm,
    below_hbm,
    stress_hbm,
    resistance_hbm,
    weights_hbm,
    grads_hbm,
    gather_hbm,
    stress_out,
    forces_out,
    ids_ref,
    euler_ref,
    owner_ref,
    element_ref,
    active_ref,
    below_ref,
    angle_ref,
    table_ref,
    carry_ref,
    owned_ref,
    rank_ref,
    single_ref,
    label_ref,
    part_ref,
    pool_ref,
    pend_ref,
    open_ref,
    stage_ref,
    wide_ref,
    acc_ref,
    out1_ref,
    in1_ref,
    out2_ref,
    in2_ref,
    got_ref,
    last_ref,
    hit_ref,
    sums_ref,
    stress_ref,
    resistance_ref,
    weights_ref,
    grads_ref,
    gather_ref,
    land_ref,
    above_ref,
    top_ref,
    under_ref,
    trial_ref,
    ids_sem,
    small_sem,
    send1_sem,
    recv1_sem,
    send2_sem,
    recv2_sem,
    layer_sem,
):
    ca, fe = lax.axis_index("ca"), lax.axis_index("fe")
    barrier = pltpu.get_barrier_semaphore()

    def member(i):
        return lax.rem(fe + i, MEMBERS)

    def group(i):
        return lax.rem(ca + i, GROUPS)

    row = lax.broadcasted_iota(jnp.int32, (8, 128), 0)
    cells = ids_hbm.shape[0]
    per_octant = cells // OCTANTS
    tiles = cells // 8
    blocks = ids_hbm.shape[1] // 128
    steps = blocks // UNROLL
    id_cuts = (0, 32, 56, 112, 168, 216)

    def ids_copy(n):
        rows = pl.ds(id_cuts[n], id_cuts[n + 1] - id_cuts[n])
        return pltpu.make_async_copy(ids_hbm.at[rows], ids_ref.at[rows], ids_sem.at[n])

    small = [
        pltpu.make_async_copy(source, target, small_sem.at[n])
        for n, (source, target) in enumerate(
            [
                (owner_hbm, owner_ref),
                (element_hbm, element_ref),
                (active_hbm, active_ref),
                (euler_hbm, euler_ref),
                (below_hbm, below_ref),
                (stress_hbm, stress_ref),
                (resistance_hbm, resistance_ref),
                (weights_hbm, weights_ref),
                (grads_hbm, grads_ref),
                (gather_hbm, gather_ref),
            ]
        )
    ]
    for copy in small[:5]:
        copy.start()
    for n in range(len(id_cuts) - 1):
        ids_copy(n).start()
    for copy in small[5:]:
        copy.start()

    @pl.loop(1, MEMBERS)
    def _(i):
        pl.semaphore_signal(barrier, inc=1, device_id=(ca, member(i)), device_id_type=MESH)

    @pl.loop(1, GROUPS)
    def _(i):
        pl.semaphore_signal(barrier, inc=1, device_id=(group(i), fe), device_id_type=MESH)

    def hop1(p, i):
        there = pl.ds(pl.multiple_of(member(i) * GROUPS, 8), GROUPS)
        here = pl.ds(pl.multiple_of(fe * GROUPS, 8), GROUPS)
        octants = pl.ds(CHUNKS[p][0], CHUNKS[p][1] - CHUNKS[p][0])
        return pltpu.make_async_remote_copy(
            src_ref=out1_ref.at[octants, :, there],
            dst_ref=in1_ref.at[octants, :, here],
            send_sem=send1_sem.at[p],
            recv_sem=recv1_sem.at[p],
            device_id=(ca, member(i)),
            device_id_type=MESH,
        )

    def hop2(p, i):
        there = pl.ds(pl.multiple_of(group(i) * MEMBERS, 8), MEMBERS)
        here = pl.ds(pl.multiple_of(ca * MEMBERS, 8), MEMBERS)
        octants = pl.ds(CHUNKS[p][0], CHUNKS[p][1] - CHUNKS[p][0])
        return pltpu.make_async_remote_copy(
            src_ref=out2_ref.at[octants, :, there],
            dst_ref=in2_ref.at[octants, :, here],
            send_sem=send2_sem.at[p],
            recv_sem=recv2_sem.at[p],
            device_id=(group(i), fe),
            device_id_type=MESH,
        )

    def all1(p):
        octants = pl.ds(CHUNKS[p][0], CHUNKS[p][1] - CHUNKS[p][0])
        rows = pl.ds(0, DEVICES - GROUPS)
        return pltpu.make_async_remote_copy(
            src_ref=out1_ref.at[octants, :, rows],
            dst_ref=in1_ref.at[octants, :, rows],
            send_sem=send1_sem.at[p],
            recv_sem=recv1_sem.at[p],
            device_id=(ca, member(1)),
            device_id_type=MESH,
        )

    def all2(p):
        octants = pl.ds(CHUNKS[p][0], CHUNKS[p][1] - CHUNKS[p][0])
        rows = pl.ds(0, DEVICES - MEMBERS)
        return pltpu.make_async_remote_copy(
            src_ref=out2_ref.at[octants, :, rows],
            dst_ref=in2_ref.at[octants, :, rows],
            send_sem=send2_sem.at[p],
            recv_sem=recv2_sem.at[p],
            device_id=(group(1), fe),
            device_id_type=MESH,
        )

    def layer_copy():
        return pltpu.make_async_remote_copy(
            src_ref=below_ref,
            dst_ref=land_ref,
            send_sem=layer_sem.at[0],
            recv_sem=layer_sem.at[1],
            device_id=(ca, lax.rem(fe + MEMBERS - 1, MEMBERS)),
            device_id_type=MESH,
        )

    def top_copy():
        return pltpu.make_async_remote_copy(
            src_ref=top_ref,
            dst_ref=under_ref,
            send_sem=layer_sem.at[2],
            recv_sem=layer_sem.at[3],
            device_id=(ca, member(1)),
            device_id_type=MESH,
        )

    def start1(p):
        if p == 0:
            pl.semaphore_wait(barrier, MEMBERS + GROUPS - 2)
            layer_copy().start()

        for i in range(1, MEMBERS):
            hop1(p, i).start()

        here = pl.ds(pl.multiple_of(fe * GROUPS, 8), GROUPS)
        for q in range(*CHUNKS[p]):
            in1_ref[q, :, here] = out1_ref[q, :, here]

    def pass_on(p):
        all1(p).wait_recv()

        for q in range(*CHUNKS[p]):
            for c in range(WORDS // 128):
                for g in range(GROUPS):
                    out2_ref[q, c, g * MEMBERS : g * MEMBERS + MEMBERS] = in1_ref[
                        q, c, pl.ds(g, MEMBERS, stride=GROUPS), :
                    ]

        for i in range(1, GROUPS):
            hop2(p, i).start()

        here = pl.ds(pl.multiple_of(ca * MEMBERS, 8), MEMBERS)
        for q in range(*CHUNKS[p]):
            in2_ref[q, :, here] = out2_ref[q, :, here]

    def take_in(p):
        all2(p).wait_recv()

        for q in range(*CHUNKS[p]):
            for c in range(WORDS // 128):
                flipped = in2_ref[q, c].T
                got_ref[q, c * 128 : c * 128 + 128] = flipped
                if c == 2:
                    last_ref[pl.ds(q, CAP, stride=OCTANTS), :] = flipped[
                        ENTRY_ROWS - 256 : ENTRY_ROWS - 256 + CAP
                    ]

    part_ref[...] = jnp.zeros(part_ref.shape, jnp.bfloat16)
    pend_ref[...] = jnp.zeros(pend_ref.shape, jnp.int32)
    open_ref[...] = jnp.zeros(open_ref.shape, jnp.float32)
    target = jnp.minimum(lax.broadcasted_iota(jnp.int32, (16, 160), 0), 8)
    source = lax.broadcasted_iota(jnp.int32, (16, 160), 1)
    source = jnp.right_shift(jnp.where(source >= 80, source - 80, source), 3)
    pool_ref[...] = jnp.where(target == source, 1.0, 0.0).astype(jnp.bfloat16)
    wide_ref[...] = jnp.zeros(wide_ref.shape, jnp.bfloat16)
    acc_ref[...] = jnp.zeros(acc_ref.shape, jnp.float32)
    for copy in small[:5]:
        copy.wait()
    build_table(euler_ref, angle_ref, table_ref)
    find_slots(owner_ref, element_ref, active_ref, owned_ref, rank_ref, single_ref, label_ref)

    def keep_parts(u, entries):
        stacked = jnp.concatenate(entries + [jnp.zeros((8, 128), jnp.float32)], axis=0)
        high = stacked.astype(jnp.bfloat16)
        lanes = slice(u * 128, u * 128 + 128)
        part_ref[:80, lanes] = high
        part_ref[80:, lanes] = (stacked - high.astype(jnp.float32)).astype(jnp.bfloat16)

    cuts = [min((q + 1) * per_octant - 8 * (-(-(q + 1) * per_octant // 8) - 1), 8) for q in range(OCTANTS)]

    def settle(cut, step):
        terms = rotation_terms(pend_ref[0], pend_ref[1])
        inside = row < cut
        for n in range(9):
            carry_ref[step * UNROLL + UNROLL - 1, n] = jnp.where(inside, 0.0, terms[n])
        sums = [open_ref[n] + jnp.where(inside, terms[n], 0.0) for n in range(9)]
        keep_parts(UNROLL - 1, octant_entries(sums, per_octant))

    def totals(out):
        out["sum"] = jnp.dot(pool_ref[...], part_ref[...], preferred_element_type=jnp.float32)

    def spread(block, u, q, total):
        parts = {}

        def split():
            columns = slice(u * 128, u * 128 + 128)
            parts["main"] = halves(total["sum"][:8, columns])
            parts["single"] = halves(total["sum"][8:, columns])

        def main(n, first):
            lanes = slice(u * 256 + n * 128, u * 256 + n * 128 + 128)
            for pair in range(first, first + 5):
                rows = slice(16 * pair, 16 * pair + 16)
                wide_ref[rows, lanes] = rank_ref[block, rows] * parts["main"][n]

        def single(n):
            lanes = slice(u * 256 + n * 128, u * 256 + n * 128 + 128)
            for part in range(3):
                rows = slice(16 * part, 16 * part + 16)
                target = slice(ENTRY_ROWS + 16 * part, ENTRY_ROWS + 16 * part + 16)
                wide_ref[target, lanes] = single_ref[block, rows] * parts["single"][n]
            if n == 0 and not (isinstance(q, int) and q >= 3):
                rows = pl.ds(pl.multiple_of(16 * q, 16), 16)
                wide_ref[LABEL_ROWS:, u * 256 : u * 256 + 128] = label_ref[block, rows]

        yield split
        for n in range(2):
            for first in range(0, CAP // 2, 5):
                yield functools.partial(main, n, first)
            yield functools.partial(single, n)

    def place(step):
        acc_ref[...] += lax.dot_general(
            owned_ref[step], wide_ref[...], NT_DIMS, preferred_element_type=jnp.float32
        )

    def finish(q):
        for c in range(WORDS // 128):
            out1_ref[q, c] = acc_ref[:, c * 128 : c * 128 + 128]
        acc_ref[...] = jnp.zeros(acc_ref.shape, jnp.float32)

    todo = {}
    for action, times in (
        (start1, ((2, 0), (4, 0), (5, 0), (6, 0), (7, 0), (8, 0))),
        (pass_on, ((3, 1), (5, 1), (6, 0), (7, 0), (7, 3), (8, 0))),
        (take_in, ((4, 3), (6, 3), (7, 3), (8, 0), (8, 0), (8, 0))),
    ):
        for p, time in enumerate(times):
            todo.setdefault(time, []).append((action, p))
    arrived = 0

    for q in range(OCTANTS):
        first = (q * per_octant) // 8
        stop = -(-((q + 1) * per_octant) // 8)
        fresh = first if first * 8 == q * per_octant else first + 1
        while id_cuts[arrived] < stop * 8:
            ids_copy(arrived).wait()
            arrived += 1

        @pl.loop(0, steps)
        def _(step, q=q, fresh=fresh, stop=stop):
            before = lax.rem(step + steps - 1, steps)
            label_octant = jnp.where(step == 0, max(q - 1, 0), min(q, 2)) if q < 4 else q
            if q > 0:
                for u in range(UNROLL):
                    stage_ref[0, u] = carry_ref[step * UNROLL + u]
            total = {}
            work = collections.deque()
            work.append(functools.partial(settle, jnp.where(step == 0, cuts[q - 1], cuts[q]), before))
            work.append(functools.partial(totals, total))
            for u in range(UNROLL):
                work.extend(spread(before * UNROLL + u, u, label_octant, total))
            work.append(functools.partial(place, before))
            state = {}

            def decode(u, t, words):
                terms = rotation_terms(*words)
                if t == stop - 1 and cuts[q] < 8:
                    inside = row < cuts[q]
                    for n in range(9):
                        stage_ref[1, u, n] = jnp.where(inside, 0.0, terms[n])
                    terms = [jnp.where(inside, v, 0.0) for v in terms]
                if t == fresh:
                    if q > 0:
                        terms = [stage_ref[0, u, n] + v for n, v in enumerate(terms)]
                else:
                    terms = [s + v for s, v in zip(state[u], terms)]
                state[u] = terms
                if t == stop - 1:
                    keep_parts(u, octant_entries(terms, per_octant))

            for u in range(UNROLL):
                columns = pl.ds(pl.multiple_of((step * UNROLL + u) * 128, 128), 128)
                for t in range(fresh, stop):
                    words = lookup(table_ref, ids_ref[8 * t : 8 * t + 8, columns], work)
                    if u < UNROLL - 1 or t < stop - 1:
                        work.appendleft(functools.partial(decode, u, t, words))
            while work:
                work.popleft()()
            for n in range(2):
                pend_ref[n] = words[n]
            for n in range(9):
                open_ref[n] = state[UNROLL - 1][n]
            if q < OCTANTS - 1:
                for u in range(UNROLL - 1):
                    carry_ref[step * UNROLL + u] = stage_ref[1, u]

            @pl.when(step == 0)
            def _():
                if q > 0:
                    finish(q - 1)
                else:
                    acc_ref[...] = jnp.zeros(acc_ref.shape, jnp.float32)

            for late in range(4):
                if (q, late) in todo:

                    @pl.when(step == late * steps // 4)
                    def _(late=late):
                        for action, p in todo[q, late]:
                            action(p)

    settle(cuts[OCTANTS - 1], steps - 1)
    total = {}
    totals(total)
    for u in range(UNROLL):
        for part in spread((steps - 1) * UNROLL + u, u, OCTANTS - 1, total):
            part()
    place(steps - 1)
    finish(OCTANTS - 1)
    rest = sorted(todo[OCTANTS, 0], key=lambda item: ORDER[item[0].__name__] + item[1])
    for action, p in rest[:1]:
        action(p)
    for copy in small[5:]:
        copy.wait()
    layer_copy().wait()
    above_ref[...] = jnp.where(fe == MEMBERS - 1, 0.0, land_ref[...])
    for n, trial in enumerate(trial_stress(below_ref, above_ref, stress_ref, grads_ref)):
        trial_ref[n] = trial
    for action, p in rest[1:-1]:
        action(p)

    ones = jnp.ones((16, 128), jnp.bfloat16)

    def owner_sums(octants, last, rows):
        sums = jnp.zeros((rows, NODES), jnp.float32)
        for r in range(0, CAP, 2):
            left = []
            for n in (r, r + 1):
                values = [got_ref[q, 8 * n : 8 * n + 8] for q in octants]
                if last:
                    values.append(last_ref[8 * n : 8 * n + 8])
                values = jnp.concatenate(values, axis=0)
                high = values.astype(jnp.bfloat16).astype(jnp.float32)
                both = jnp.concatenate([high, values - high], axis=0).astype(jnp.bfloat16)
                left.append(both if last else jnp.concatenate([both, ones], axis=0))
            sums = sums + lax.dot_general(
                jnp.concatenate(left, axis=1),
                hit_ref[r // 2],
                NT_DIMS,
                preferred_element_type=jnp.float32,
            )
        return sums

    label_value = lax.broadcasted_iota(jnp.int32, (NODES, 128), 0).astype(jnp.float32) + 1.0
    for n in range(CAP):
        line = LABEL_ROWS + n % 16
        hit = label_value == got_ref[n // 16, line : line + 1, :]
        lanes = slice((n & 1) * 128, (n & 1) * 128 + 128)
        hit_ref[n // 2, :, lanes] = hit.astype(jnp.bfloat16)
    early = owner_sums(range(OCTANTS - 1), False, 128)
    action, p = rest[-1]
    action(p)
    late = owner_sums([OCTANTS - 1], True, 32)
    for half in range(2):
        lanes = slice(half * 128, half * 128 + 128)
        sums_ref[half, :56] = early[:56, lanes] + early[56:112, lanes]
        sums_ref[half, 56:72] = late[:16, lanes] + late[16:32, lanes]
        sums_ref[half, 72:80] = early[112:120, lanes]
    trial = [trial_ref[n] for n in range(6)]
    updated = stress_update(sums_ref, trial, resistance_ref)
    placed = nodal_parts(updated, weights_ref, gather_ref)
    for comp in range(3):
        top_ref[comp] = layer_forces(placed, comp, 1)
    top_copy().start()
    for component in range(6):
        stress_out[component] = updated[component]
    owned = [layer_forces(placed, comp, 0) for comp in range(3)]
    for p in range(len(CHUNKS)):
        all1(p).wait_send()
        all2(p).wait_send()

    top_copy().wait()
    for comp in range(3):
        forces_out[comp] = owned[comp] + jnp.where(fe == 0, 0.0, under_ref[comp])


ORDER = {"start1": 0, "pass_on": 10, "take_in": 20}


def fused_step(
    grain_ids, euler_angles, owner, element, active, below, stress_old, resistance, quad_weights
):
    grads, forces = gradient_matrices()
    bricks = grain_ids.shape[1]
    blocks = bricks // 128
    hop = pltpu.VMEM((OCTANTS, WORDS // 128, DEVICES, 128), jnp.float32)
    vmem = pl.BlockSpec(memory_space=pltpu.VMEM)
    line = pltpu.VMEM((1, bricks), jnp.int32)
    layer = pltpu.VMEM(below.shape, jnp.float32)
    chunks = len(CHUNKS)
    return pl.pallas_call(
        exchange_kernel,
        out_shape=(
            jax.ShapeDtypeStruct(stress_old.shape, jnp.float32),
            jax.ShapeDtypeStruct(below.shape, jnp.float32),
        ),
        in_specs=[pl.BlockSpec(memory_space=pltpu.HBM)] * 11,
        out_specs=(vmem, vmem),
        scratch_shapes=[
            pltpu.VMEM(grain_ids.shape, jnp.int32),
            pltpu.VMEM(euler_angles.shape, jnp.float32),
            line,
            line,
            line,
            pltpu.VMEM(below.shape, jnp.float32),
            pltpu.VMEM((3, 32, 128), jnp.float32),
            pltpu.VMEM((64, 8, 128), jnp.int32),
            pltpu.VMEM((blocks, 9, 8, 128), jnp.float32),
            pltpu.VMEM((blocks // UNROLL, DEVICES, 256 * UNROLL), jnp.bfloat16),
            pltpu.VMEM((blocks, ENTRY_ROWS, 128), jnp.bfloat16),
            pltpu.VMEM((blocks, 48, 128), jnp.bfloat16),
            pltpu.VMEM((blocks, 48, 128), jnp.bfloat16),
            pltpu.VMEM((160, 128 * UNROLL), jnp.bfloat16),
            pltpu.VMEM((16, 160), jnp.bfloat16),
            pltpu.VMEM((2, 8, 128), jnp.int32),
            pltpu.VMEM((9, 8, 128), jnp.float32),
            pltpu.VMEM((2, UNROLL, 9, 8, 128), jnp.float32),
            pltpu.VMEM((WORDS, 256 * UNROLL), jnp.bfloat16),
            pltpu.VMEM((DEVICES, WORDS), jnp.float32),
            hop,
            hop,
            hop,
            hop,
            pltpu.VMEM((OCTANTS, WORDS, 128), jnp.float32),
            pltpu.VMEM((OCTANTS * CAP, 128), jnp.float32),
            pltpu.VMEM((CAP // 2, NODES, 256), jnp.bfloat16),
            pltpu.VMEM((2, 80, 128), jnp.float32),
            pltpu.VMEM(stress_old.shape, jnp.float32),
            pltpu.VMEM(resistance.shape, jnp.float32),
            pltpu.VMEM(quad_weights.shape, jnp.int32),
            pltpu.VMEM(grads.shape, jnp.float32),
            pltpu.VMEM(forces.shape, jnp.float32),
            layer,
            layer,
            layer,
            layer,
            pltpu.VMEM(stress_old.shape, jnp.float32),
            pltpu.SemaphoreType.DMA((5,)),
            pltpu.SemaphoreType.DMA((10,)),
            pltpu.SemaphoreType.DMA((chunks,)),
            pltpu.SemaphoreType.DMA((chunks,)),
            pltpu.SemaphoreType.DMA((chunks,)),
            pltpu.SemaphoreType.DMA((chunks,)),
            pltpu.SemaphoreType.DMA((4,)),
        ],
        compiler_params=pltpu.CompilerParams(
            vmem_limit_bytes=EXCHANGE_VMEM, collective_id=0, has_side_effects=True
        ),
        name="fused_step",
    )(
        grain_ids,
        euler_angles,
        owner.reshape(1, bricks),
        element.reshape(1, bricks),
        active.reshape(1, bricks),
        below,
        stress_old,
        resistance,
        quad_weights,
        jnp.asarray(grads),
        jnp.asarray(forces),
    )


def handing_kernel(stress_in, forces_in, stress_out, forces_out, stress_ref, forces_ref, sem):
    for hop, pairs in enumerate(
        (
            ((stress_in, stress_ref), (forces_in, forces_ref)),
            ((stress_ref, stress_out), (forces_ref, forces_out)),
        )
    ):
        copies = [
            pltpu.make_async_copy(source, target, sem.at[hop, n])
            for n, (source, target) in enumerate(pairs)
        ]
        for copy in copies:
            copy.start()
        for copy in copies:
            copy.wait()


def handed_out(stress, forces):
    hbm = pl.BlockSpec(memory_space=pltpu.HBM)
    return pl.pallas_call(
        handing_kernel,
        out_shape=tuple(jax.ShapeDtypeStruct(x.shape, x.dtype) for x in (stress, forces)),
        in_specs=[hbm, hbm],
        out_specs=(hbm, hbm),
        scratch_shapes=[
            pltpu.VMEM(stress.shape, stress.dtype),
            pltpu.VMEM(forces.shape, forces.dtype),
            pltpu.SemaphoreType.DMA((2, 2)),
        ],
        name="handed_out",
    )(stress, forces)


def body(
    grain_ids,
    euler_angles,
    brick_active,
    brick_owner,
    brick_element,
    displacement,
    stress_old,
    resistance,
    quad_weights,
):
    return handed_out(
        *fused_step(
            grain_ids,
            euler_angles,
            brick_owner,
            brick_element,
            brick_active,
            displacement,
            stress_old,
            resistance,
            quad_weights,
        )
    )


def solution(mesh):
    placed = (
        P(None, ("ca", "fe")),
        P(),
        P(("ca", "fe")),
        P(("ca", "fe"), None),
        P(("ca", "fe")),
        P(None, ("ca", "fe"), None),
        P(None, None, ("ca", "fe")),
        P(None, None, ("ca", "fe")),
        P(None, ("ca", "fe")),
    )
    return jax.shard_map(
        body,
        mesh=mesh,
        in_specs=placed,
        out_specs=(P(None, None, ("ca", "fe")), P(None, ("ca", "fe"), None)),
        check_vma=False,
    )
```

```python
import collections
import functools
import math

import jax
import jax.numpy as jnp
import numpy as np
from jax import lax
from jax.experimental import pallas as pl
from jax.experimental.pallas import tpu as pltpu
from jax.sharding import PartitionSpec as P

GX = 15
NODES = 256
CAP = 40
GROUPS = 8
MEMBERS = 16
DEVICES = GROUPS * MEMBERS
FIXED_STEPS = float(2**20 - 1)

SLIP_PLANES = [
    [value / math.sqrt(3.0) for value in row]
    for row in [[1, 1, 1]] * 3 + [[-1, 1, 1]] * 3 + [[1, -1, 1]] * 3 + [[1, 1, -1]] * 3
]
SLIP_DIRECTIONS = [
    [value / math.sqrt(2.0) for value in row]
    for row in [
        [0, 1, -1],
        [1, 0, -1],
        [1, -1, 0],
        [0, 1, -1],
        [1, 0, 1],
        [1, 1, 0],
        [0, 1, 1],
        [1, 0, -1],
        [1, 1, 0],
        [0, 1, 1],
        [1, 0, 1],
        [1, -1, 0],
    ]
]
LAMBDA_ELASTIC = 1.5
SHEAR_MODULUS = 1.0
RATE_STEP = 0.1
FIXED_POINT = 65536.0
EXCHANGE_VMEM = 63 << 20


def shape_gradients():
    grad_table = np.zeros((8, 8, 3))
    point_offset = 1.0 / math.sqrt(3.0)
    for quadrature in range(8):
        natural = [
            (2 * (quadrature >> shift_bits & 1) - 1) * point_offset for shift_bits in (2, 1, 0)
        ]
        for corner in range(8):
            sign_list = [2 * (corner >> shift_bits & 1) - 1 for shift_bits in (2, 1, 0)]
            factors = [1.0 + sign_list[axis_id] * natural[axis_id] for axis_id in range(3)]
            for direction in range(3):
                others = 1.0
                for axis_id in range(3):
                    if axis_id != direction:
                        others = others * factors[axis_id]
                grad_table[quadrature, corner, direction] = (
                    2.0 * sign_list[direction] * others / 8.0
                )
    return grad_table


def gradient_matrices():
    table = shape_gradients()
    grads = np.zeros((72, 24), np.float32)
    forces = np.zeros((24, 72), np.float32)
    for comp in range(3):
        for direction in range(3):
            for q in range(8):
                for corner in range(8):
                    value = table[q, corner, direction]
                    grads[(comp * 3 + direction) * 8 + q, comp * 8 + corner] = value
                    forces[comp * 8 + corner, (comp * 3 + direction) * 8 + q] = value
    return grads, forces


def lane_pick(row, lanes):
    return jnp.take_along_axis(row, lanes, axis=1, mode="promise_in_bounds")


def merge_tree(stack, value, index, bits):
    level = 0
    while index & 1:
        value = jnp.where(bits[level], value, stack.pop())
        level += 1
        index >>= 1
    stack.append(value)


def build_table(euler_ref, angle_ref, table_ref):
    for angle in range(3):
        for row in range(32):
            angle_ref[angle, row : row + 1] = euler_ref[
                angle : angle + 1, row * 128 : row * 128 + 128
            ]
    half_sum = 0.5 * (angle_ref[0] + angle_ref[2])
    half_diff = 0.5 * (angle_ref[0] - angle_ref[2])
    half_mid = 0.5 * angle_ref[1]
    cos_mid, sin_mid = jnp.cos(half_mid), jnp.sin(half_mid)
    real = cos_mid * jnp.cos(half_sum)
    flip = jnp.where(real < 0.0, -1.0, 1.0)
    scale = flip * FIXED_STEPS / (1.0 + jnp.abs(real))
    first = jnp.round(sin_mid * jnp.cos(half_diff) * scale).astype(jnp.int32)
    second = jnp.round(sin_mid * jnp.sin(half_diff) * scale).astype(jnp.int32)
    third = jnp.round(cos_mid * jnp.sin(half_sum) * scale).astype(jnp.int32)
    word_a = jnp.left_shift(first, 11) | (jnp.right_shift(third, 10) & 0x7FF)
    word_b = jnp.left_shift(second, 11) | (third & 0x3FF)
    for row in range(32):
        table_ref[row] = jnp.broadcast_to(word_a[row : row + 1], (8, 128))
        table_ref[32 + row] = jnp.broadcast_to(word_b[row : row + 1], (8, 128))


def lookup(table_ref, ids, work):
    lanes = ids & 127
    bits = [(ids & (128 << level)) != 0 for level in range(5)]
    words = ([], [])
    for n, stack in enumerate(words):
        for row in range(32):
            merge_tree(stack, lane_pick(table_ref[n * 32 + row], lanes), row, bits)
            if work and row % 5 == 4:
                work.popleft()()
    return words[0][0], words[1][0]


def rotation_terms(word_a, word_b):
    a = jnp.right_shift(word_a, 11).astype(jnp.float32)
    b = jnp.right_shift(word_b, 11).astype(jnp.float32)
    c_bits = jnp.right_shift(jnp.left_shift(word_a, 21), 11) | (word_b & 0x3FF)
    c = c_bits.astype(jnp.float32)
    unit = 1.0 / FIXED_STEPS
    square = (a * a + b * b + c * c) * (unit * unit)
    inverse = 1.0 / (1.0 + square)
    inverse_square = inverse * inverse
    quad = inverse_square * (8.0 * unit * unit)
    lin = inverse_square * ((1.0 - square) * (4.0 * unit))
    qa, qb, qc = quad * a, quad * b, quad * c
    return [qa * a, qb * b, qc * c, qa * b, qa * c, qb * c, lin * a, lin * b, lin * c]


def octant_entries(terms, per_octant):
    xx, yy, zz, xy, xz, yz, wx, wy, wz = terms
    share = per_octant / 8.0
    return [
        share - (yy + zz),
        xy - wz,
        xz + wy,
        xy + wz,
        share - (xx + zz),
        yz - wx,
        xz - wy,
        yz + wx,
        share - (xx + yy),
    ]


NT_DIMS = (((1,), (1,)), ((), ()))
MESH = pl.DeviceIdType.MESH
OCTANTS = 8
CHUNKS = ((0, 3), (3, 6), (6, 7), (7, 8))
UNROLL = 4
WORDS = 384
ENTRY_ROWS = 8 * CAP
LABEL_ROWS = 368


def find_slots(owner_ref, element_ref, active_ref, owned_ref, rank_ref, single_ref, label_ref):
    span = 256
    device = lax.broadcasted_iota(jnp.int32, (DEVICES, span), 0)
    before = (
        lax.broadcasted_iota(jnp.int32, (span, span), 0)
        < lax.broadcasted_iota(jnp.int32, (span, span), 1)
    ).astype(jnp.bfloat16)
    ones = jnp.ones((span, span), jnp.bfloat16)
    slot = lax.broadcasted_iota(jnp.int32, (48, span), 0).astype(jnp.float32)
    carry = jnp.zeros((DEVICES, span), jnp.float32)
    for start in range(0, owner_ref.shape[1], span):
        owner = owner_ref[:, start : start + span]
        owned = device == ((owner & (MEMBERS - 1)) * GROUPS + jnp.right_shift(owner, 4))
        owned_half = owned.astype(jnp.bfloat16)
        earlier = carry + jnp.dot(owned_half, before, preferred_element_type=jnp.float32)
        carry = carry + jnp.dot(owned_half, ones, preferred_element_type=jnp.float32)
        rank = jnp.sum(jnp.where(owned, earlier, 0.0), axis=0, keepdims=True)
        label = jnp.where(
            active_ref[:, start : start + span] > 0, element_ref[:, start : start + span] + 1, 0
        ).astype(jnp.float32)
        single = jnp.where(slot == rank, 1.0, 0.0)
        labels = (single * label).astype(jnp.bfloat16)
        single = single.astype(jnp.bfloat16)
        eight = jnp.broadcast_to(rank, (8, span))
        for half in range(span // 128):
            lanes = slice(half * 128, half * 128 + 128)
            block = start // 128 + half
            place = (block % UNROLL) * 256
            owned_ref[block // UNROLL, :, place : place + 128] = owned_half[:, lanes]
            owned_ref[block // UNROLL, :, place + 128 : place + 256] = owned_half[:, lanes]
            single_ref[block] = single[:, lanes]
            label_ref[block] = labels[:, lanes]
            for pair in range(CAP // 2):
                both = [
                    jnp.where(eight[:, lanes] == float(2 * pair + n), 1.0, 0.0) for n in range(2)
                ]
                rank_ref[block, 16 * pair : 16 * pair + 16] = jnp.concatenate(
                    both, axis=0
                ).astype(jnp.bfloat16)


def halves(values):
    high = values.astype(jnp.bfloat16).astype(jnp.float32)
    out = []
    for part in (high, values - high):
        out.append(jnp.concatenate([part, part], axis=0).astype(jnp.bfloat16))
    return out


def split_three(values):
    high = values.astype(jnp.bfloat16)
    rest = values - high.astype(jnp.float32)
    mid = rest.astype(jnp.bfloat16)
    low = (rest - mid.astype(jnp.float32)).astype(jnp.bfloat16)
    return jnp.concatenate([high, mid, low], axis=0)


def joined_three(product):
    rows = product.shape[0] // 3
    return product[:rows] + product[rows : 2 * rows] + product[2 * rows :]


def element_places(elements):
    node = lax.broadcasted_iota(jnp.int32, (NODES, NODES), 0)
    lane = lax.broadcasted_iota(jnp.int32, (NODES, NODES), 1)
    base = lane
    for bound in range(GX, GX * GX, GX):
        base = base + jnp.where(lane >= bound, 1, 0)
    return ((node == base) & (lane < elements)).astype(jnp.bfloat16)


def trial_stress(below_ref, above_ref, stress_ref, grads_ref):
    elements = stress_ref.shape[2]
    to_element = element_places(elements)
    rows = []
    for comp in range(3):
        for corner in range(8):
            step_x, step_y, step_z = (corner >> 2 & 1, corner >> 1 & 1, corner & 1)
            source = above_ref if step_z else below_ref
            offset = step_y * (GX + 1) + step_x
            line = source[comp]
            rows.append(line if offset == 0 else pltpu.roll(line, NODES - offset, 1))
    corners = joined_three(
        jnp.dot(
            split_three(jnp.concatenate(rows, axis=0)),
            to_element,
            preferred_element_type=jnp.float32,
        )
    )
    gradients = jnp.dot(
        grads_ref[...],
        corners,
        precision=lax.Precision.HIGHEST,
        preferred_element_type=jnp.float32,
    )

    def grad(comp, direction):
        n = (comp * 3 + direction) * 8
        return gradients[n : n + 8, :elements]

    strain = [
        grad(0, 0),
        grad(1, 1),
        grad(2, 2),
        0.5 * (grad(1, 2) + grad(2, 1)),
        0.5 * (grad(0, 2) + grad(2, 0)),
        0.5 * (grad(0, 1) + grad(1, 0)),
    ]
    volume = strain[0] + strain[1] + strain[2]
    trial = []
    for component in range(6):
        change = 2.0 * SHEAR_MODULUS * strain[component]
        if component < 3:
            change = change + LAMBDA_ELASTIC * volume
        trial.append(stress_ref[component] + change)
    return trial


def stress_update(sums_ref, trial, resistance_ref):
    elements = resistance_ref.shape[2]
    weights = [1.0 / (8.0 * jnp.maximum(sums_ref[half, 72:73], 1.0)) for half in range(2)]
    frames = []
    for n in range(9):
        rows = pl.ds(n, OCTANTS, stride=8) if n < 8 else pl.ds(64, OCTANTS)
        parts = [sums_ref[half, rows, :] * weights[half] for half in range(2)]
        frames.append(jnp.concatenate(parts, axis=1)[:, :elements])

    def frame(i, j):
        return frames[i * 3 + j]

    def rotated(vector):
        out = []
        for i in range(3):
            terms = [float(vector[j]) * frame(i, j) for j in range(3) if vector[j] != 0.0]
            out.append(functools.reduce(lambda x, y: x + y, terms))
        return out

    normals = {tuple(vector): rotated(vector) for vector in SLIP_PLANES}
    correction = [jnp.zeros_like(trial[0]) for component in range(6)]
    for system in range(12):
        d = rotated(SLIP_DIRECTIONS[system])
        m = normals[tuple(SLIP_PLANES[system])]
        schmid = [
            d[0] * m[0],
            d[1] * m[1],
            d[2] * m[2],
            0.5 * (d[1] * m[2] + d[2] * m[1]),
            0.5 * (d[0] * m[2] + d[2] * m[0]),
            0.5 * (d[0] * m[1] + d[1] * m[0]),
        ]
        resolved = (
            trial[0] * schmid[0]
            + trial[1] * schmid[1]
            + trial[2] * schmid[2]
            + 2.0 * (trial[3] * schmid[3] + trial[4] * schmid[4] + trial[5] * schmid[5])
        )
        ratio = resolved / resistance_ref[system]
        slip_step = RATE_STEP * ratio * jnp.abs(ratio)
        correction = [
            correction[component] + slip_step * schmid[component] for component in range(6)
        ]
    updated = [
        trial[component] - 2.0 * SHEAR_MODULUS * correction[component] for component in range(6)
    ]
    return updated


def nodal_parts(updated, weights_ref, gather_ref):
    elements = weights_ref.shape[1]
    to_element = element_places(elements)
    scale = weights_ref[...].astype(jnp.float32) * (1.0 / (FIXED_POINT * 8.0))
    order = [0, 5, 4, 5, 1, 3, 4, 3, 2]
    pad = jnp.zeros((8, NODES - elements), jnp.float32)
    tensor = jnp.concatenate(
        [jnp.concatenate([updated[component] * scale, pad], axis=1) for component in order], axis=0
    )
    element_forces = jnp.dot(
        gather_ref[...],
        tensor,
        precision=lax.Precision.HIGHEST,
        preferred_element_type=jnp.float32,
    )
    placed = joined_three(
        lax.dot_general(
            split_three(element_forces), to_element, NT_DIMS, preferred_element_type=jnp.float32
        )
    )
    return placed


def layer_forces(placed, comp, step_z):
    line = jnp.zeros((1, NODES), jnp.float32)
    for corner in range(8):
        if (corner & 1) != step_z:
            continue
        offset = (corner >> 1 & 1) * (GX + 1) + (corner >> 2 & 1)
        part = placed[comp * 8 + corner : comp * 8 + corner + 1]
        line = line + (part if offset == 0 else pltpu.roll(part, offset, 1))
    return line


def exchange_kernel(
    ids_hbm,
    euler_hbm,
    owner_hbm,
    element_hbm,
    active_hbm,
    below_hbm,
    stress_hbm,
    resistance_hbm,
    weights_hbm,
    grads_hbm,
    gather_hbm,
    stress_out,
    forces_out,
    ids_ref,
    euler_ref,
    owner_ref,
    element_ref,
    active_ref,
    below_ref,
    angle_ref,
    table_ref,
    carry_ref,
    owned_ref,
    rank_ref,
    single_ref,
    label_ref,
    part_ref,
    pool_ref,
    pend_ref,
    open_ref,
    stage_ref,
    wide_ref,
    acc_ref,
    out1_ref,
    in1_ref,
    out2_ref,
    in2_ref,
    got_ref,
    last_ref,
    hit_ref,
    sums_ref,
    stress_ref,
    resistance_ref,
    weights_ref,
    grads_ref,
    gather_ref,
    land_ref,
    above_ref,
    top_ref,
    under_ref,
    trial_ref,
    ids_sem,
    small_sem,
    send1_sem,
    recv1_sem,
    send2_sem,
    recv2_sem,
    layer_sem,
):
    ca, fe = lax.axis_index("ca"), lax.axis_index("fe")
    barrier = pltpu.get_barrier_semaphore()

    def member(i):
        return lax.rem(fe + i, MEMBERS)

    def group(i):
        return lax.rem(ca + i, GROUPS)

    row = lax.broadcasted_iota(jnp.int32, (8, 128), 0)
    cells = ids_hbm.shape[0]
    per_octant = cells // OCTANTS
    tiles = cells // 8
    blocks = ids_hbm.shape[1] // 128
    steps = blocks // UNROLL
    id_cuts = (0, 32, 56, 112, 168, 216)

    def ids_copy(n):
        rows = pl.ds(id_cuts[n], id_cuts[n + 1] - id_cuts[n])
        return pltpu.make_async_copy(ids_hbm.at[rows], ids_ref.at[rows], ids_sem.at[n])

    small = [
        pltpu.make_async_copy(source, target, small_sem.at[n])
        for n, (source, target) in enumerate(
            [
                (owner_hbm, owner_ref),
                (element_hbm, element_ref),
                (active_hbm, active_ref),
                (euler_hbm, euler_ref),
                (below_hbm, below_ref),
                (stress_hbm, stress_ref),
                (resistance_hbm, resistance_ref),
                (weights_hbm, weights_ref),
                (grads_hbm, grads_ref),
                (gather_hbm, gather_ref),
            ]
        )
    ]
    for copy in small[:5]:
        copy.start()
    for n in range(len(id_cuts) - 1):
        ids_copy(n).start()
    for copy in small[5:]:
        copy.start()

    @pl.loop(1, MEMBERS)
    def _(i):
        pl.semaphore_signal(barrier, inc=1, device_id=(ca, member(i)), device_id_type=MESH)

    @pl.loop(1, GROUPS)
    def _(i):
        pl.semaphore_signal(barrier, inc=1, device_id=(group(i), fe), device_id_type=MESH)

    def hop1(p, i):
        there = pl.ds(pl.multiple_of(member(i) * GROUPS, 8), GROUPS)
        here = pl.ds(pl.multiple_of(fe * GROUPS, 8), GROUPS)
        octants = pl.ds(CHUNKS[p][0], CHUNKS[p][1] - CHUNKS[p][0])
        return pltpu.make_async_remote_copy(
            src_ref=out1_ref.at[octants, :, there],
            dst_ref=in1_ref.at[octants, :, here],
            send_sem=send1_sem.at[p],
            recv_sem=recv1_sem.at[p],
            device_id=(ca, member(i)),
            device_id_type=MESH,
        )

    def hop2(p, i):
        there = pl.ds(pl.multiple_of(group(i) * MEMBERS, 8), MEMBERS)
        here = pl.ds(pl.multiple_of(ca * MEMBERS, 8), MEMBERS)
        octants = pl.ds(CHUNKS[p][0], CHUNKS[p][1] - CHUNKS[p][0])
        return pltpu.make_async_remote_copy(
            src_ref=out2_ref.at[octants, :, there],
            dst_ref=in2_ref.at[octants, :, here],
            send_sem=send2_sem.at[p],
            recv_sem=recv2_sem.at[p],
            device_id=(group(i), fe),
            device_id_type=MESH,
        )

    def all1(p):
        octants = pl.ds(CHUNKS[p][0], CHUNKS[p][1] - CHUNKS[p][0])
        rows = pl.ds(0, DEVICES - GROUPS)
        return pltpu.make_async_remote_copy(
            src_ref=out1_ref.at[octants, :, rows],
            dst_ref=in1_ref.at[octants, :, rows],
            send_sem=send1_sem.at[p],
            recv_sem=recv1_sem.at[p],
            device_id=(ca, member(1)),
            device_id_type=MESH,
        )

    def all2(p):
        octants = pl.ds(CHUNKS[p][0], CHUNKS[p][1] - CHUNKS[p][0])
        rows = pl.ds(0, DEVICES - MEMBERS)
        return pltpu.make_async_remote_copy(
            src_ref=out2_ref.at[octants, :, rows],
            dst_ref=in2_ref.at[octants, :, rows],
            send_sem=send2_sem.at[p],
            recv_sem=recv2_sem.at[p],
            device_id=(group(1), fe),
            device_id_type=MESH,
        )

    def layer_copy():
        return pltpu.make_async_remote_copy(
            src_ref=below_ref,
            dst_ref=land_ref,
            send_sem=layer_sem.at[0],
            recv_sem=layer_sem.at[1],
            device_id=(ca, lax.rem(fe + MEMBERS - 1, MEMBERS)),
            device_id_type=MESH,
        )

    def top_copy():
        return pltpu.make_async_remote_copy(
            src_ref=top_ref,
            dst_ref=under_ref,
            send_sem=layer_sem.at[2],
            recv_sem=layer_sem.at[3],
            device_id=(ca, member(1)),
            device_id_type=MESH,
        )

    def start1(p):
        if p == 0:
            pl.semaphore_wait(barrier, MEMBERS + GROUPS - 2)
            layer_copy().start()

        for i in range(1, MEMBERS):
            hop1(p, i).start()

        here = pl.ds(pl.multiple_of(fe * GROUPS, 8), GROUPS)
        for q in range(*CHUNKS[p]):
            in1_ref[q, :, here] = out1_ref[q, :, here]

    def pass_on(p):
        all1(p).wait_recv()

        for q in range(*CHUNKS[p]):
            for c in range(WORDS // 128):
                for g in range(GROUPS):
                    out2_ref[q, c, g * MEMBERS : g * MEMBERS + MEMBERS] = in1_ref[
                        q, c, pl.ds(g, MEMBERS, stride=GROUPS), :
                    ]

        for i in range(1, GROUPS):
            hop2(p, i).start()

        here = pl.ds(pl.multiple_of(ca * MEMBERS, 8), MEMBERS)
        for q in range(*CHUNKS[p]):
            in2_ref[q, :, here] = out2_ref[q, :, here]

    def take_in(p):
        all2(p).wait_recv()

        for q in range(*CHUNKS[p]):
            for c in range(WORDS // 128):
                flipped = in2_ref[q, c].T
                got_ref[q, c * 128 : c * 128 + 128] = flipped
                if c == 2:
                    last_ref[pl.ds(q, CAP, stride=OCTANTS), :] = flipped[
                        ENTRY_ROWS - 256 : ENTRY_ROWS - 256 + CAP
                    ]

    part_ref[...] = jnp.zeros(part_ref.shape, jnp.bfloat16)
    pend_ref[...] = jnp.zeros(pend_ref.shape, jnp.int32)
    open_ref[...] = jnp.zeros(open_ref.shape, jnp.float32)
    target = jnp.minimum(lax.broadcasted_iota(jnp.int32, (16, 160), 0), 8)
    source = lax.broadcasted_iota(jnp.int32, (16, 160), 1)
    source = jnp.right_shift(jnp.where(source >= 80, source - 80, source), 3)
    pool_ref[...] = jnp.where(target == source, 1.0, 0.0).astype(jnp.bfloat16)
    wide_ref[...] = jnp.zeros(wide_ref.shape, jnp.bfloat16)
    acc_ref[...] = jnp.zeros(acc_ref.shape, jnp.float32)
    for copy in small[:5]:
        copy.wait()
    build_table(euler_ref, angle_ref, table_ref)
    find_slots(owner_ref, element_ref, active_ref, owned_ref, rank_ref, single_ref, label_ref)

    def keep_parts(u, entries):
        stacked = jnp.concatenate(entries + [jnp.zeros((8, 128), jnp.float32)], axis=0)
        high = stacked.astype(jnp.bfloat16)
        lanes = slice(u * 128, u * 128 + 128)
        part_ref[:80, lanes] = high
        part_ref[80:, lanes] = (stacked - high.astype(jnp.float32)).astype(jnp.bfloat16)

    cuts = [min((q + 1) * per_octant - 8 * (-(-(q + 1) * per_octant // 8) - 1), 8) for q in range(OCTANTS)]

    def settle(cut, step):
        terms = rotation_terms(pend_ref[0], pend_ref[1])
        inside = row < cut
        for n in range(9):
            carry_ref[step * UNROLL + UNROLL - 1, n] = jnp.where(inside, 0.0, terms[n])
        sums = [open_ref[n] + jnp.where(inside, terms[n], 0.0) for n in range(9)]
        keep_parts(UNROLL - 1, octant_entries(sums, per_octant))

    def totals(out):
        out["sum"] = jnp.dot(pool_ref[...], part_ref[...], preferred_element_type=jnp.float32)

    def spread(block, u, q, total):
        parts = {}

        def split():
            columns = slice(u * 128, u * 128 + 128)
            parts["main"] = halves(total["sum"][:8, columns])
            parts["single"] = halves(total["sum"][8:, columns])

        def main(n, first):
            lanes = slice(u * 256 + n * 128, u * 256 + n * 128 + 128)
            for pair in range(first, first + 5):
                rows = slice(16 * pair, 16 * pair + 16)
                wide_ref[rows, lanes] = rank_ref[block, rows] * parts["main"][n]

        def single(n):
            lanes = slice(u * 256 + n * 128, u * 256 + n * 128 + 128)
            for part in range(3):
                rows = slice(16 * part, 16 * part + 16)
                target = slice(ENTRY_ROWS + 16 * part, ENTRY_ROWS + 16 * part + 16)
                wide_ref[target, lanes] = single_ref[block, rows] * parts["single"][n]
            if n == 0 and not (isinstance(q, int) and q >= 3):
                rows = pl.ds(pl.multiple_of(16 * q, 16), 16)
                wide_ref[LABEL_ROWS:, u * 256 : u * 256 + 128] = label_ref[block, rows]

        yield split
        for n in range(2):
            for first in range(0, CAP // 2, 5):
                yield functools.partial(main, n, first)
            yield functools.partial(single, n)

    def place(step):
        acc_ref[...] += lax.dot_general(
            owned_ref[step], wide_ref[...], NT_DIMS, preferred_element_type=jnp.float32
        )

    def finish(q):
        for c in range(WORDS // 128):
            out1_ref[q, c] = acc_ref[:, c * 128 : c * 128 + 128]
        acc_ref[...] = jnp.zeros(acc_ref.shape, jnp.float32)

    todo = {}
    for action, times in (
        (start1, ((3, 0), (6, 0), (7, 0), (8, 0))),
        (pass_on, ((5, 0), (7, 2), (8, 0), (8, 0))),
        (take_in, ((6, 3), (8, 0), (8, 0), (8, 0))),
    ):
        for p, time in enumerate(times):
            todo.setdefault(time, []).append((action, p))
    arrived = 0

    for q in range(OCTANTS):
        first = (q * per_octant) // 8
        stop = -(-((q + 1) * per_octant) // 8)
        fresh = first if first * 8 == q * per_octant else first + 1
        while id_cuts[arrived] < stop * 8:
            ids_copy(arrived).wait()
            arrived += 1

        @pl.loop(0, steps)
        def _(step, q=q, fresh=fresh, stop=stop):
            before = lax.rem(step + steps - 1, steps)
            label_octant = jnp.where(step == 0, max(q - 1, 0), min(q, 2)) if q < 4 else q
            if q > 0:
                for u in range(UNROLL):
                    stage_ref[0, u] = carry_ref[step * UNROLL + u]
            total = {}
            work = collections.deque()
            work.append(functools.partial(settle, jnp.where(step == 0, cuts[q - 1], cuts[q]), before))
            work.append(functools.partial(totals, total))
            for u in range(UNROLL):
                work.extend(spread(before * UNROLL + u, u, label_octant, total))
            work.append(functools.partial(place, before))
            state = {}

            def decode(u, t, words):
                terms = rotation_terms(*words)
                if t == stop - 1 and cuts[q] < 8:
                    inside = row < cuts[q]
                    for n in range(9):
                        stage_ref[1, u, n] = jnp.where(inside, 0.0, terms[n])
                    terms = [jnp.where(inside, v, 0.0) for v in terms]
                if t == fresh:
                    if q > 0:
                        terms = [stage_ref[0, u, n] + v for n, v in enumerate(terms)]
                else:
                    terms = [s + v for s, v in zip(state[u], terms)]
                state[u] = terms
                if t == stop - 1:
                    keep_parts(u, octant_entries(terms, per_octant))

            for u in range(UNROLL):
                columns = pl.ds(pl.multiple_of((step * UNROLL + u) * 128, 128), 128)
                for t in range(fresh, stop):
                    words = lookup(table_ref, ids_ref[8 * t : 8 * t + 8, columns], work)
                    if u < UNROLL - 1 or t < stop - 1:
                        work.appendleft(functools.partial(decode, u, t, words))
            while work:
                work.popleft()()
            for n in range(2):
                pend_ref[n] = words[n]
            for n in range(9):
                open_ref[n] = state[UNROLL - 1][n]
            if q < OCTANTS - 1:
                for u in range(UNROLL - 1):
                    carry_ref[step * UNROLL + u] = stage_ref[1, u]

            @pl.when(step == 0)
            def _():
                if q > 0:
                    finish(q - 1)
                else:
                    acc_ref[...] = jnp.zeros(acc_ref.shape, jnp.float32)

            for late in range(4):
                if (q, late) in todo:

                    @pl.when(step == late * steps // 4)
                    def _(late=late):
                        for action, p in todo[q, late]:
                            action(p)

    settle(cuts[OCTANTS - 1], steps - 1)
    total = {}
    totals(total)
    for u in range(UNROLL):
        for part in spread((steps - 1) * UNROLL + u, u, OCTANTS - 1, total):
            part()
    place(steps - 1)
    finish(OCTANTS - 1)
    rest = sorted(todo[OCTANTS, 0], key=lambda item: ORDER[item[0].__name__] + item[1])
    for action, p in rest[:1]:
        action(p)
    for copy in small[5:]:
        copy.wait()
    layer_copy().wait()
    above_ref[...] = jnp.where(fe == MEMBERS - 1, 0.0, land_ref[...])
    for n, trial in enumerate(trial_stress(below_ref, above_ref, stress_ref, grads_ref)):
        trial_ref[n] = trial
    for action, p in rest[1:-1]:
        action(p)

    ones = jnp.ones((16, 128), jnp.bfloat16)

    def owner_sums(octants, last, rows):
        sums = jnp.zeros((rows, NODES), jnp.float32)
        for r in range(0, CAP, 2):
            left = []
            for n in (r, r + 1):
                values = [got_ref[q, 8 * n : 8 * n + 8] for q in octants]
                if last:
                    values.append(last_ref[8 * n : 8 * n + 8])
                values = jnp.concatenate(values, axis=0)
                high = values.astype(jnp.bfloat16).astype(jnp.float32)
                both = jnp.concatenate([high, values - high], axis=0).astype(jnp.bfloat16)
                left.append(both if last else jnp.concatenate([both, ones], axis=0))
            sums = sums + lax.dot_general(
                jnp.concatenate(left, axis=1),
                hit_ref[r // 2],
                NT_DIMS,
                preferred_element_type=jnp.float32,
            )
        return sums

    label_value = lax.broadcasted_iota(jnp.int32, (NODES, 128), 0).astype(jnp.float32) + 1.0
    for n in range(CAP):
        line = LABEL_ROWS + n % 16
        hit = label_value == got_ref[n // 16, line : line + 1, :]
        lanes = slice((n & 1) * 128, (n & 1) * 128 + 128)
        hit_ref[n // 2, :, lanes] = hit.astype(jnp.bfloat16)
    early = owner_sums(range(OCTANTS - 1), False, 128)
    action, p = rest[-1]
    action(p)
    late = owner_sums([OCTANTS - 1], True, 32)
    for half in range(2):
        lanes = slice(half * 128, half * 128 + 128)
        sums_ref[half, :56] = early[:56, lanes] + early[56:112, lanes]
        sums_ref[half, 56:72] = late[:16, lanes] + late[16:32, lanes]
        sums_ref[half, 72:80] = early[112:120, lanes]
    trial = [trial_ref[n] for n in range(6)]
    updated = stress_update(sums_ref, trial, resistance_ref)
    placed = nodal_parts(updated, weights_ref, gather_ref)
    for comp in range(3):
        top_ref[comp] = layer_forces(placed, comp, 1)
    top_copy().start()
    for component in range(6):
        stress_out[component] = updated[component]
    owned = [layer_forces(placed, comp, 0) for comp in range(3)]
    for p in range(len(CHUNKS)):
        all1(p).wait_send()
        all2(p).wait_send()

    top_copy().wait()
    for comp in range(3):
        forces_out[comp] = owned[comp] + jnp.where(fe == 0, 0.0, under_ref[comp])


ORDER = {"start1": 0, "pass_on": 10, "take_in": 20}


def fused_step(
    grain_ids, euler_angles, owner, element, active, below, stress_old, resistance, quad_weights
):
    grads, forces = gradient_matrices()
    bricks = grain_ids.shape[1]
    blocks = bricks // 128
    hop = pltpu.VMEM((OCTANTS, WORDS // 128, DEVICES, 128), jnp.float32)
    vmem = pl.BlockSpec(memory_space=pltpu.VMEM)
    line = pltpu.VMEM((1, bricks), jnp.int32)
    layer = pltpu.VMEM(below.shape, jnp.float32)
    chunks = len(CHUNKS)
    return pl.pallas_call(
        exchange_kernel,
        out_shape=(
            jax.ShapeDtypeStruct(stress_old.shape, jnp.float32),
            jax.ShapeDtypeStruct(below.shape, jnp.float32),
        ),
        in_specs=[pl.BlockSpec(memory_space=pltpu.HBM)] * 11,
        out_specs=(vmem, vmem),
        scratch_shapes=[
            pltpu.VMEM(grain_ids.shape, jnp.int32),
            pltpu.VMEM(euler_angles.shape, jnp.float32),
            line,
            line,
            line,
            pltpu.VMEM(below.shape, jnp.float32),
            pltpu.VMEM((3, 32, 128), jnp.float32),
            pltpu.VMEM((64, 8, 128), jnp.int32),
            pltpu.VMEM((blocks, 9, 8, 128), jnp.float32),
            pltpu.VMEM((blocks // UNROLL, DEVICES, 256 * UNROLL), jnp.bfloat16),
            pltpu.VMEM((blocks, ENTRY_ROWS, 128), jnp.bfloat16),
            pltpu.VMEM((blocks, 48, 128), jnp.bfloat16),
            pltpu.VMEM((blocks, 48, 128), jnp.bfloat16),
            pltpu.VMEM((160, 128 * UNROLL), jnp.bfloat16),
            pltpu.VMEM((16, 160), jnp.bfloat16),
            pltpu.VMEM((2, 8, 128), jnp.int32),
            pltpu.VMEM((9, 8, 128), jnp.float32),
            pltpu.VMEM((2, UNROLL, 9, 8, 128), jnp.float32),
            pltpu.VMEM((WORDS, 256 * UNROLL), jnp.bfloat16),
            pltpu.VMEM((DEVICES, WORDS), jnp.float32),
            hop,
            hop,
            hop,
            hop,
            pltpu.VMEM((OCTANTS, WORDS, 128), jnp.float32),
            pltpu.VMEM((OCTANTS * CAP, 128), jnp.float32),
            pltpu.VMEM((CAP // 2, NODES, 256), jnp.bfloat16),
            pltpu.VMEM((2, 80, 128), jnp.float32),
            pltpu.VMEM(stress_old.shape, jnp.float32),
            pltpu.VMEM(resistance.shape, jnp.float32),
            pltpu.VMEM(quad_weights.shape, jnp.int32),
            pltpu.VMEM(grads.shape, jnp.float32),
            pltpu.VMEM(forces.shape, jnp.float32),
            layer,
            layer,
            layer,
            layer,
            pltpu.VMEM(stress_old.shape, jnp.float32),
            pltpu.SemaphoreType.DMA((5,)),
            pltpu.SemaphoreType.DMA((10,)),
            pltpu.SemaphoreType.DMA((chunks,)),
            pltpu.SemaphoreType.DMA((chunks,)),
            pltpu.SemaphoreType.DMA((chunks,)),
            pltpu.SemaphoreType.DMA((chunks,)),
            pltpu.SemaphoreType.DMA((4,)),
        ],
        compiler_params=pltpu.CompilerParams(
            vmem_limit_bytes=EXCHANGE_VMEM, collective_id=0, has_side_effects=True
        ),
        name="fused_step",
    )(
        grain_ids,
        euler_angles,
        owner.reshape(1, bricks),
        element.reshape(1, bricks),
        active.reshape(1, bricks),
        below,
        stress_old,
        resistance,
        quad_weights,
        jnp.asarray(grads),
        jnp.asarray(forces),
    )


def handing_kernel(stress_in, forces_in, stress_out, forces_out, stress_ref, forces_ref, sem):
    for hop, pairs in enumerate(
        (
            ((stress_in, stress_ref), (forces_in, forces_ref)),
            ((stress_ref, stress_out), (forces_ref, forces_out)),
        )
    ):
        copies = [
            pltpu.make_async_copy(source, target, sem.at[hop, n])
            for n, (source, target) in enumerate(pairs)
        ]
        for copy in copies:
            copy.start()
        for copy in copies:
            copy.wait()


def handed_out(stress, forces):
    hbm = pl.BlockSpec(memory_space=pltpu.HBM)
    return pl.pallas_call(
        handing_kernel,
        out_shape=tuple(jax.ShapeDtypeStruct(x.shape, x.dtype) for x in (stress, forces)),
        in_specs=[hbm, hbm],
        out_specs=(hbm, hbm),
        scratch_shapes=[
            pltpu.VMEM(stress.shape, stress.dtype),
            pltpu.VMEM(forces.shape, forces.dtype),
            pltpu.SemaphoreType.DMA((2, 2)),
        ],
        name="handed_out",
    )(stress, forces)


def body(
    grain_ids,
    euler_angles,
    brick_active,
    brick_owner,
    brick_element,
    displacement,
    stress_old,
    resistance,
    quad_weights,
):
    return handed_out(
        *fused_step(
            grain_ids,
            euler_angles,
            brick_owner,
            brick_element,
            brick_active,
            displacement,
            stress_old,
            resistance,
            quad_weights,
        )
    )


def solution(mesh):
    placed = (
        P(None, ("ca", "fe")),
        P(),
        P(("ca", "fe")),
        P(("ca", "fe"), None),
        P(("ca", "fe")),
        P(None, ("ca", "fe"), None),
        P(None, None, ("ca", "fe")),
        P(None, None, ("ca", "fe")),
        P(None, ("ca", "fe")),
    )
    return jax.shard_map(
        body,
        mesh=mesh,
        in_specs=placed,
        out_specs=(P(None, None, ("ca", "fe")), P(None, ("ca", "fe"), None)),
        check_vma=False,
    )
```
